128 devices in a mesh: leaf: 8 (over x, core), front: 16 (over z, y).
Axes of the slice: x: 4, y: 4, z: 4, core: 2. Of those that a mesh axis runs over, the one named last changes fastest.
Arguments:
- front_matrix: float32 [8, 2048, 2048], P('leaf', 'front'), as said below
- child_blocks: float32 [128, 8, 3, 128, 128], P(('leaf', 'front')), may hold values from -0.046875 to 0.046875
- child_target: int32 [128, 8, 3], P(('leaf', 'front')), may hold values from 0 to 15, as said below
- child_count: int32 [128, 8], P(('leaf', 'front')), may hold values from 1 to 3, as said below
- shot_rhs: float32 [8, 64, 2048], P('leaf'), may hold values from -6 to 6
Outputs:
- factored: float32 [8, 2048, 2048], P('leaf', 'front')
- eliminated: float32 [8, 64, 2048], P('leaf')
The draws below stay inside these ranges and needn't reach their ends.
Inputs may be any that keep to these rules, and one draw needn't show every extreme that they name: `child_target`: A bucket's code places its block on a row block that the receiving device (leaf index of the bucket, front index of the sender) holds, at a column block no later than that row block. Slots from child_count on are empty and hold no data. In every draw some leaf index receives 3 live blocks from every sender. `front_matrix`: after the child blocks are added, the symmetric matrix that each front's lower triangle defines is positive definite.
All inputs are finite; a program needn't handle non-finite values.
Results may differ from the reference program's by a relative error of at most 0.00013.
Values sent between devices are 32-bit elements; how exact they have to be, the bound alone decides.
No kernel may reach another device: no remote copies, remote signals or barrier semaphores. Data moves between devices by JAX's collectives and lax.ppermute only.
A program may use at most 64 MiB of HBM per device.

```python
import jax
import jax.numpy as jnp
from jax import lax

BLOCK = 128
ORDER = 2048
PIVOTS = 1024
NRHS = 64
FR_DEV = 1
CAP = 3
FRONTS = 8
SENDERS = 128
NCB = 16
RB_LOC = 1
N_LEAF = 8
N_FRONT = 16


def draw_front_matrix(key, part):
    key_off, key_diag = jax.random.split(key)
    array_shape = (FRONTS, ORDER, ORDER)
    offdiag = jax.random.normal(key_off, array_shape, jnp.float32)
    offdiag = offdiag * (0.2 * ORDER ** (-0.5))
    row_ids = lax.broadcasted_iota(jnp.int32, (ORDER, ORDER), 0)
    col_ids = lax.broadcasted_iota(jnp.int32, (ORDER, ORDER), 1)
    distance = jnp.abs(row_ids - col_ids)
    coupling = jnp.where((distance == 1) | (distance == 32), jnp.float32(-1.0), jnp.float32(0.0))
    identity_mat = jnp.where(distance == 0, jnp.float32(1.0), jnp.float32(0.0))
    diagonal = jax.random.uniform(key_diag, (FRONTS, ORDER), jnp.float32, 5.5, 6.5)
    return offdiag * (1.0 - identity_mat) + coupling[None, :, :] + diagonal[:, :, None] * identity_mat


def draw_child_target(key, part):
    key_front, key_row, key_col = jax.random.split(key, 3)
    target_dims = (SENDERS, N_LEAF, CAP)
    front_pick = jax.random.randint(key_front, target_dims, 0, FR_DEV)
    row_pick = jax.random.randint(key_row, target_dims, 0, RB_LOC)
    sender_front = lax.broadcasted_iota(jnp.int32, target_dims, 0) % N_FRONT
    global_row = sender_front * RB_LOC + row_pick
    col_pick = jax.random.randint(key_col, target_dims, 0, global_row + 1)
    return ((front_pick * RB_LOC + row_pick) * NCB + col_pick).astype(jnp.int32)


def draw_child_count(key, part):
    key_count, key_full = jax.random.split(key)
    counts = jax.random.randint(key_count, (SENDERS, N_LEAF), 1, CAP + 1)
    full_leaf = jax.random.randint(key_full, (), 0, N_LEAF)
    column_ids = lax.broadcasted_iota(jnp.int32, (SENDERS, N_LEAF), 1)
    return jnp.where(column_ids == full_leaf, CAP, counts).astype(jnp.int32)


def block_scale(stream_key, shape, cuts, low, largest):
    def one(dim, shards_of):
        steps = jax.random.uniform(jax.random.fold_in(jax.random.fold_in(stream_key, 6), dim), (shards_of,), jnp.float32, low / len(cuts), largest / len(cuts))
        return jnp.repeat(jnp.exp(steps), shape[dim] // shards_of).reshape((-1,) + (1,) * (len(shape) - dim - 1))

    level = one(*cuts[0])
    for cut in cuts[1:]:
        level = level * one(*cut)
    return level


def scatter_about(stream_key, extent, scale, limit, shards=(), kind=jnp.bfloat16):
    factor_of = block_scale(stream_key, extent, shards, -0.22, 0.18) if shards else 1.0
    result = jax.random.normal(stream_key, extent, jnp.float32) * scale * factor_of
    return jnp.minimum(jnp.maximum(result, -limit), limit).astype(kind)


def setup_inputs(seed: int = 0) -> dict:
    keys = jax.random.split(jax.random.key(seed), 6)
    front_matrix = draw_front_matrix(jax.random.fold_in(keys[5], 71), 0)
    child_blocks = scatter_about(keys[1], (SENDERS, N_LEAF, CAP, BLOCK, BLOCK), (0.15 * ORDER ** -0.5), 0.046875, ((0, 128),), jnp.float32)
    child_target = draw_child_target(jax.random.fold_in(keys[5], 71), 0)
    child_count = draw_child_count(jax.random.fold_in(keys[5], 71), 0)
    shot_rhs = scatter_about(keys[4], (FRONTS, NRHS, ORDER), 1.0, 6.0, ((0, 8),), jnp.float32)
    return {"front_matrix": front_matrix, "child_blocks": child_blocks, "child_target": child_target, "child_count": child_count, "shot_rhs": shot_rhs}


def lower_sym(square):
    return jnp.tril(square) + jnp.swapaxes(jnp.tril(square, -1), -1, -2)

def extend_add(child_blocks, child_target, child_count):
    slot_ids = lax.broadcasted_iota(jnp.int32, child_target.shape, 2)
    sender_ids = lax.broadcasted_iota(jnp.int32, child_target.shape, 0)
    dest_leaf = lax.broadcasted_iota(jnp.int32, child_target.shape, 1)
    live_mask = slot_ids < child_count[:, :, None]
    front_ids = dest_leaf * FR_DEV + child_target // (RB_LOC * NCB)
    row_ids = sender_ids % N_FRONT * RB_LOC + child_target // NCB % RB_LOC
    col_ids = child_target % NCB
    values = jnp.where(live_mask[:, :, :, None, None], child_blocks, jnp.float32(0.0))
    block_grid = jnp.zeros((FRONTS, NCB, NCB, BLOCK, BLOCK), jnp.float32)
    block_grid = block_grid.at[front_ids, row_ids, col_ids].add(values)
    return block_grid.transpose(0, 1, 3, 2, 4).reshape(FRONTS, ORDER, ORDER)

def factor_one(operands):
    matrix, current_rhs = operands
    row_index = jnp.arange(ORDER, dtype=jnp.int32)[:, None]
    col_index = jnp.arange(ORDER, dtype=jnp.int32)[None, :]
    left_parts = []
    diag_parts = []
    solved_parts = []
    for pivot_step in range(PIVOTS // BLOCK):
        start_col = pivot_step * BLOCK
        end_col = start_col + BLOCK
        column_panel = matrix[:, start_col:end_col]
        pivot_factor = jnp.linalg.cholesky(lower_sym(column_panel[start_col:end_col]))
        panel_solved = jax.scipy.linalg.solve_triangular(pivot_factor, column_panel.T, lower=True).T
        panel_solved = jnp.where(row_index < start_col, jnp.float32(0.0), panel_solved)
        panel_solved = panel_solved.at[start_col:end_col].set(pivot_factor)
        tail_panel = panel_solved[end_col:]
        update = jnp.dot(panel_solved.astype(jnp.float32), tail_panel.T.astype(jnp.float32), precision=lax.Precision.HIGHEST, preferred_element_type=jnp.float32)
        matrix = matrix.at[:, end_col:].add(-update)
        zeta = jax.scipy.linalg.solve_triangular(pivot_factor, current_rhs[:, start_col:end_col].T, lower=True).T
        rhs_update = jnp.dot(zeta.astype(jnp.float32), tail_panel.T.astype(jnp.float32), precision=lax.Precision.HIGHEST, preferred_element_type=jnp.float32)
        current_rhs = current_rhs.at[:, end_col:].add(-rhs_update)
        pivots_now = jnp.diagonal(pivot_factor)
        left_parts.append(panel_solved / pivots_now[None, :])
        diag_parts.append(pivots_now * pivots_now)
        solved_parts.append(zeta * pivots_now[None, :])
    combined = jnp.concatenate(left_parts + [matrix[:, PIVOTS:]], axis=1)
    combined = jnp.where(row_index < col_index, jnp.float32(0.0), combined)
    diag_full = jnp.concatenate(diag_parts + [jnp.zeros((ORDER - PIVOTS,), jnp.float32)], axis=0)
    on_diagonal = (row_index == col_index) & (col_index < PIVOTS)
    factored = jnp.where(on_diagonal, diag_full[None, :], combined)
    eliminated = jnp.concatenate(solved_parts + [current_rhs[:, PIVOTS:]], axis=1)
    return (factored, eliminated)

def reference(front_matrix, child_blocks, child_target, child_count, shot_rhs):
    assembled = front_matrix + extend_add(child_blocks, child_target, child_count)
    factored, eliminated = lax.map(factor_one, (assembled, shot_rhs))
    return (factored, eliminated)
```

```python
import jax
import jax.numpy as jnp
from jax import lax
from jax.experimental import pallas as pl
from jax.experimental.pallas import tpu as pltpu
from jax.sharding import PartitionSpec as P

B = 128
PIV = 1024
NP = PIV // B
F32 = jnp.float32
BF16 = jnp.bfloat16
VMEM_LIMIT = 56 * 1024 * 1024


def split(x):
    hi = x.astype(BF16)
    lo = (x - hi.astype(F32)).astype(BF16)
    return hi, lo


def dot_t(a, b):
    return lax.dot_general(a, b, (((1,), (1,)), ((), ())), preferred_element_type=F32)


def dot_n(a, b):
    return lax.dot_general(a, b, (((1,), (0,)), ((), ())), preferred_element_type=F32)


def dot3_t(ah, al, bh, bl):
    return dot_t(ah, bh) + dot_t(al, bh) + dot_t(ah, bl)


def dot3_n(ah, al, bh, bl):
    return dot_n(ah, bh) + dot_n(al, bh) + dot_n(ah, bl)


def assemble_kernel(code_ref, idx_ref, recv_ref, front_ref, out_ref):
    out_ref[...] = front_ref[...]
    for s in range(recv_ref.shape[0]):
        for j in range(code_ref.shape[1]):
            code = code_ref[s, j]

            @pl.when(code >= 0)
            def _(s=s, j=j, code=code):
                cols = pl.ds(pl.multiple_of(code * B, B), B)
                out_ref[:, cols] += recv_ref[s, j * B : (j + 1) * B, :]

    cols = pl.ds(pl.multiple_of(idx_ref[0] * B, B), B)
    square = out_ref[:, cols]
    row = lax.broadcasted_iota(jnp.int32, (B, B), 0)
    col = lax.broadcasted_iota(jnp.int32, (B, B), 1)
    out_ref[:, cols] = jnp.where(row >= col, square, square.T)


def assemble(codes, index, recv, front):
    return pl.pallas_call(
        assemble_kernel,
        out_shape=jax.ShapeDtypeStruct(front.shape, F32),
        in_specs=[
            pl.BlockSpec(memory_space=pltpu.SMEM),
            pl.BlockSpec(memory_space=pltpu.SMEM),
            pl.BlockSpec(memory_space=pltpu.VMEM),
            pl.BlockSpec(memory_space=pltpu.VMEM),
        ],
        out_specs=pl.BlockSpec(memory_space=pltpu.VMEM),
        compiler_params=pltpu.CompilerParams(vmem_limit_bytes=VMEM_LIMIT),
        name="assemble",
    )(codes, index, recv, front)


def chain(a_rows, e_rows, store):
    sub = lax.broadcasted_iota(jnp.int32, (8, B), 0)
    for g in range(16):
        ra, re = a_rows[g], e_rows[g]
        base = 8 * g
        b = [jnp.broadcast_to(ra[:, base + t : base + t + 1], (8, B)) for t in range(8)]
        ga, ge = ra, re
        fa, fe = ra, re
        rcps = []
        for t in range(8):
            piv = jnp.broadcast_to(b[t][t : t + 1, :], (8, B))
            r = 1.0 / piv
            rcps.append(r)
            m = b[t] * r
            mg = jnp.where(sub == t, 0.0, m)
            mf = jnp.where(sub > t, m, 0.0)
            for u in range(t + 1, 8):
                b[u] = b[u] - mg * jnp.broadcast_to(b[u][t : t + 1, :], (8, B))
            pa = jnp.broadcast_to(fa[t : t + 1, :], (8, B))
            pe = jnp.broadcast_to(fe[t : t + 1, :], (8, B))
            fa = fa - mf * pa
            fe = fe - mf * pe
            ga = ga - mg * pa
            ge = ge - mg * pe
        rc = rcps[0]
        for t in range(1, 8):
            rc = jnp.where(sub == t, rcps[t], rc)
        store(g, fa, fe, rc)
        ga = ga * rc
        ge = ge * rc
        if g < 15:
            gab = [jnp.broadcast_to(ga[t : t + 1, :], (8, B)) for t in range(8)]
            geb = [jnp.broadcast_to(ge[t : t + 1, :], (8, B)) for t in range(8)]
            for i in range(g + 1, 16):
                acc_a, acc_e = a_rows[i], e_rows[i]
                for t in range(8):
                    c = jnp.broadcast_to(a_rows[i][:, base + t : base + t + 1], (8, B))
                    acc_a = acc_a - c * gab[t]
                    acc_e = acc_e - c * geb[t]
                a_rows[i], e_rows[i] = acc_a, acc_e


def factor_kernel(idx_ref, a_ref, b_ref, lh_ref, ll_ref, t_ref, dinv_ref, y_ref, own_ref,
                  vh, vl, u_ref, lt_ref):
    me = idx_ref[0]
    vh[...] = jnp.zeros_like(vh)
    vl[...] = jnp.zeros_like(vl)
    lh_ref[...] = jnp.zeros_like(lh_ref)
    ll_ref[...] = jnp.zeros_like(ll_ref)
    own_ref[...] = jnp.zeros_like(own_ref)
    row = lax.broadcasted_iota(jnp.int32, (B, B), 0)
    col = lax.broadcasted_iota(jnp.int32, (B, B), 1)
    ri = lax.broadcasted_iota(jnp.int32, (8, B), 0)
    ci = lax.broadcasted_iota(jnp.int32, (8, B), 1)

    def panel(k, _):
        kcols = pl.ds(pl.multiple_of(k * B, B), B)
        krows = pl.ds(pl.multiple_of(k * B, B), B)
        chunks = (k + 1) // 2

        def updated(value, rows):
            def body(c, acc):
                cols = pl.ds(pl.multiple_of(c * 256, 256), 256)
                return acc - dot3_t(vh[rows, cols], vl[rows, cols], lh_ref[krows, cols], ll_ref[krows, cols])

            return lax.fori_loop(0, chunks, body, value)

        u_ref[...] = updated(a_ref[krows, kcols], krows)
        a_rows = [u_ref[8 * i : 8 * i + 8, :] for i in range(16)]
        e_rows = [jnp.where(ri + 8 * i == ci, 1.0, 0.0) for i in range(16)]
        diag = []

        def store(g, fa, fe, rc):
            own = ri + 8 * g == ci
            diag.append(jnp.where(own, fa, 0.0))
            lt_ref[8 * g : 8 * g + 8, :] = jnp.where(own, fa, jnp.where(ri + 8 * g < ci, fa * rc, 0.0))
            t_ref[k, 8 * g : 8 * g + 8, :] = fe

        chain(a_rows, e_rows, store)
        total = diag[0]
        for g in range(1, 16):
            total = total + diag[g]
        dinv = 1.0 / jnp.sum(total, axis=0, keepdims=True)
        dinv_ref[0:1, kcols] = dinv
        th, tl = split(t_ref[k])

        @pl.when(me == k)
        def _():
            own_ref[:, kcols] = lt_ref[...].T

        def rest(r, _):
            rows = pl.ds(pl.multiple_of(r * B, B), B)
            uh, ul = split(updated(a_ref[rows, kcols], rows))
            v = dot3_t(uh, ul, th, tl)
            vh[rows, kcols], vl[rows, kcols] = split(v)
            lower = v * dinv
            lh_ref[rows, kcols], ll_ref[rows, kcols] = split(lower)

            @pl.when(me == r)
            def _():
                own_ref[:, kcols] = lower

            return 0

        lax.fori_loop(k + 1, NP, rest, 0)
        rows = pl.ds(PIV, b_ref.shape[0])
        uh, ul = split(updated(b_ref[:, kcols], rows))
        v = dot3_t(uh, ul, th, tl)
        vh[rows, kcols], vl[rows, kcols] = split(v)
        y_ref[:, kcols] = v
        return 0

    lax.fori_loop(0, NP, panel, 0)


def factor(index, gathered, rhs):
    nrhs = rhs.shape[0]
    vmem = pl.BlockSpec(memory_space=pltpu.VMEM)
    return pl.pallas_call(
        factor_kernel,
        grid=(1,),
        out_shape=(
            jax.ShapeDtypeStruct((PIV, PIV), BF16),
            jax.ShapeDtypeStruct((PIV, PIV), BF16),
            jax.ShapeDtypeStruct((NP, B, B), F32),
            jax.ShapeDtypeStruct((8, PIV), F32),
            jax.ShapeDtypeStruct((nrhs, PIV), F32),
            jax.ShapeDtypeStruct((B, PIV), F32),
        ),
        in_specs=[
            pl.BlockSpec(memory_space=pltpu.SMEM),
            pl.BlockSpec((PIV, PIV), lambda i: (0, 0)),
            pl.BlockSpec((nrhs, PIV), lambda i: (0, 0)),
        ],
        out_specs=(
            pl.BlockSpec((PIV, PIV), lambda i: (0, 0)),
            pl.BlockSpec((PIV, PIV), lambda i: (0, 0)),
            pl.BlockSpec((NP, B, B), lambda i: (0, 0, 0)),
            pl.BlockSpec((8, PIV), lambda i: (0, 0)),
            pl.BlockSpec((nrhs, PIV), lambda i: (0, 0)),
            pl.BlockSpec((B, PIV), lambda i: (0, 0)),
        ),
        scratch_shapes=[
            pltpu.VMEM((PIV + nrhs, PIV), BF16),
            pltpu.VMEM((PIV + nrhs, PIV), BF16),
            pltpu.VMEM((B, B), F32),
            pltpu.VMEM((B, B), F32),
        ],
        compiler_params=pltpu.CompilerParams(vmem_limit_bytes=VMEM_LIMIT),
        name="factor",
    )(index, gathered, rhs)


def finish_kernel(idx_ref, a_ref, lh_ref, ll_ref, t_ref, dinv_ref, y_ref, own_ref, mine_ref, b_ref,
                  fac_ref, eli_ref, vh, vl, wh, wl, v32):
    me = idx_ref[0]
    order = fac_ref.shape[1]
    W2 = 2 * B
    for p in range(NP // 2):
        t0h, t0l = split(t_ref[2 * p])
        t1h, t1l = split(t_ref[2 * p + 1])
        r1 = slice((2 * p + 1) * B, (2 * p + 2) * B)
        c0 = slice(2 * p * B, (2 * p + 1) * B)
        xh, xl = split(dot3_n(lh_ref[r1, c0], ll_ref[r1, c0], t0h, t0l))
        xh, xl = split(-dot3_n(t1h, t1l, xh, xl))
        zero = jnp.zeros((B, B), BF16)
        tph = jnp.concatenate([jnp.concatenate([t0h, zero], 1), jnp.concatenate([xh, t1h], 1)], 0)
        tpl = jnp.concatenate([jnp.concatenate([t0l, zero], 1), jnp.concatenate([xl, t1l], 1)], 0)
        pc = slice(p * W2, (p + 1) * W2)
        dinv = dinv_ref[0:1, pc]

        def rows_body(r, _, p=p, pc=pc, tph=tph, tpl=tpl, dinv=dinv):
            rows = pl.ds(pl.multiple_of(r * W2, W2), W2)
            u = a_ref[rows, pc]
            if p:
                prev = slice(0, p * W2)
                u = u - dot3_t(vh[rows, prev], vl[rows, prev], lh_ref[pc, prev], ll_ref[pc, prev])
            uh, ul = split(u)
            v = dot3_t(uh, ul, tph, tpl)
            v32[rows, pc] = v
            vh[rows, pc], vl[rows, pc] = split(v)
            wh[rows, pc], wl[rows, pc] = split(v * dinv)
            return 0

        lax.fori_loop(0, (order - PIV) // W2, rows_body, 0)

    yh, yl = split(y_ref[...])
    eli_ref[:, :PIV] = y_ref[...]
    nblk = (order - PIV) // W2

    def b_body(c, _):
        rows = pl.ds(pl.multiple_of(c * W2, W2), W2)
        dst = pl.ds(pl.multiple_of(PIV + c * W2, W2), W2)
        eli_ref[:, dst] = b_ref[:, dst] - dot3_t(yh, yl, wh[rows, :], wl[rows, :])
        return 0

    lax.fori_loop(0, nblk, b_body, 0)

    @pl.when(me < NP)
    def _():
        fac_ref[:, :PIV] = own_ref[...]
        fac_ref[:, PIV:] = jnp.zeros((B, order - PIV), F32)

    @pl.when(me >= NP)
    def _():
        mine = pl.ds(pl.multiple_of((me - NP) * B, B), B)
        fac_ref[:, :PIV] = v32[mine, :] * dinv_ref[0:1, :]
        mh, ml = vh[mine, :], vl[mine, :]

        def s_body(c, _):
            rows = pl.ds(pl.multiple_of(c * W2, W2), W2)
            dst = pl.ds(pl.multiple_of(PIV + c * W2, W2), W2)
            s = mine_ref[:, dst] - dot3_t(mh, ml, wh[rows, :], wl[rows, :])
            row = me * B + lax.broadcasted_iota(jnp.int32, (B, W2), 0)
            col = PIV + c * W2 + lax.broadcasted_iota(jnp.int32, (B, W2), 1)
            fac_ref[:, dst] = jnp.where(row >= col, s, 0.0)
            return 0

        lax.fori_loop(0, nblk, s_body, 0)


def finish(index, gathered, lh, ll, t, dinv, y, own, mine, rhs):
    nrhs, order = rhs.shape
    low = order - PIV
    return pl.pallas_call(
        finish_kernel,
        grid=(1,),
        out_shape=(
            jax.ShapeDtypeStruct((B, order), F32),
            jax.ShapeDtypeStruct((nrhs, order), F32),
        ),
        in_specs=[
            pl.BlockSpec(memory_space=pltpu.SMEM),
            pl.BlockSpec((low, PIV), lambda i: (1, 0)),
            pl.BlockSpec((PIV, PIV), lambda i: (0, 0)),
            pl.BlockSpec((PIV, PIV), lambda i: (0, 0)),
            pl.BlockSpec((NP, B, B), lambda i: (0, 0, 0)),
            pl.BlockSpec((8, PIV), lambda i: (0, 0)),
            pl.BlockSpec((nrhs, PIV), lambda i: (0, 0)),
            pl.BlockSpec((B, PIV), lambda i: (0, 0)),
            pl.BlockSpec((B, order), lambda i: (0, 0)),
            pl.BlockSpec((nrhs, order), lambda i: (0, 0)),
        ],
        out_specs=(
            pl.BlockSpec((B, order), lambda i: (0, 0)),
            pl.BlockSpec((nrhs, order), lambda i: (0, 0)),
        ),
        scratch_shapes=[
            pltpu.VMEM((low, PIV), BF16),
            pltpu.VMEM((low, PIV), BF16),
            pltpu.VMEM((low, PIV), BF16),
            pltpu.VMEM((low, PIV), BF16),
            pltpu.VMEM((low, PIV), F32),
        ],
        compiler_params=pltpu.CompilerParams(vmem_limit_bytes=VMEM_LIMIT),
        name="finish",
    )(index, gathered, lh, ll, t, dinv, y, own, mine, rhs)


def local(front_matrix, child_blocks, child_target, child_count, shot_rhs):
    leaves, slots = child_blocks.shape[1:3]
    slot_ids = lax.broadcasted_iota(jnp.int32, (leaves, slots), 1)
    live_code = jnp.where(slot_ids < child_count[0][:, None], child_target[0], -1)
    code_rows = jnp.zeros((leaves, 8, B), F32).at[:, 0, :slots].set(live_code.astype(F32))
    payload = jnp.concatenate([child_blocks[0].reshape(leaves, slots * B, B), code_rows], axis=1)
    arrived = lax.all_to_all(payload, "leaf", split_axis=0, concat_axis=0, tiled=True)
    codes = arrived[:, slots * B, :slots].astype(jnp.int32)
    index = lax.axis_index("front").astype(jnp.int32).reshape(1)
    mine = assemble(codes, index, arrived, front_matrix[0])
    gathered = lax.all_gather(mine[:, :PIV], "front", axis=0, tiled=True)
    rhs = shot_rhs[0]
    lh, ll, t, dinv, y, own = factor(index, gathered, rhs)
    factored, eliminated = finish(index, gathered, lh, ll, t, dinv, y, own, mine, rhs)
    return factored[None], eliminated[None]


def solution(mesh):
    return jax.shard_map(
        local,
        mesh=mesh,
        in_specs=(
            P("leaf", "front", None),
            P(("leaf", "front"), None, None, None, None),
            P(("leaf", "front"), None, None),
            P(("leaf", "front"), None),
            P("leaf", None, None),
        ),
        out_specs=(P("leaf", "front", None), P("leaf", None, None)),
        check_vma=False,
    )
```

```python
import jax
import jax.numpy as jnp
from jax import lax
from jax.experimental import pallas as pl
from jax.experimental.pallas import tpu as pltpu
from jax.sharding import PartitionSpec as P

B = 128
PIV = 1024
NP = PIV // B
F32 = jnp.float32
BF16 = jnp.bfloat16
VMEM_LIMIT = 56 * 1024 * 1024


def split(x):
    hi = x.astype(BF16)
    lo = (x - hi.astype(F32)).astype(BF16)
    return hi, lo


def dot_t(a, b):
    return lax.dot_general(a, b, (((1,), (1,)), ((), ())), preferred_element_type=F32)


def dot_n(a, b):
    return lax.dot_general(a, b, (((1,), (0,)), ((), ())), preferred_element_type=F32)


def dot3_t(ah, al, bh, bl):
    return dot_t(ah, bh) + dot_t(al, bh) + dot_t(ah, bl)


def dot3_n(ah, al, bh, bl):
    return dot_n(ah, bh) + dot_n(al, bh) + dot_n(ah, bl)


def assemble_kernel(code_ref, idx_ref, recv_ref, front_ref, out_ref):
    out_ref[...] = front_ref[...]
    for s in range(recv_ref.shape[0]):
        for j in range(code_ref.shape[1]):
            code = code_ref[s, j]

            @pl.when(code >= 0)
            def _(s=s, j=j, code=code):
                cols = pl.ds(pl.multiple_of(code * B, B), B)
                out_ref[:, cols] += recv_ref[s, j * B : (j + 1) * B, :]

    cols = pl.ds(pl.multiple_of(idx_ref[0] * B, B), B)
    square = out_ref[:, cols]
    row = lax.broadcasted_iota(jnp.int32, (B, B), 0)
    col = lax.broadcasted_iota(jnp.int32, (B, B), 1)
    out_ref[:, cols] = jnp.where(row >= col, square, square.T)


def assemble(codes, index, recv, front):
    return pl.pallas_call(
        assemble_kernel,
        out_shape=jax.ShapeDtypeStruct(front.shape, F32),
        in_specs=[
            pl.BlockSpec(memory_space=pltpu.SMEM),
            pl.BlockSpec(memory_space=pltpu.SMEM),
            pl.BlockSpec(memory_space=pltpu.VMEM),
            pl.BlockSpec(memory_space=pltpu.VMEM),
        ],
        out_specs=pl.BlockSpec(memory_space=pltpu.VMEM),
        compiler_params=pltpu.CompilerParams(vmem_limit_bytes=VMEM_LIMIT),
        name="assemble",
    )(codes, index, recv, front)


def chain(a_rows, e_rows, store, side):
    sub = lax.broadcasted_iota(jnp.int32, (8, B), 0)
    for g in range(16):
        if g < len(side):
            side[g]()
        ra, re = a_rows[g], e_rows[g]
        base = 8 * g
        b = [jnp.broadcast_to(ra[:, base + t : base + t + 1], (8, B)) for t in range(8)]
        ga, ge = ra, re
        fa, fe = ra, re
        rcps = []
        for t in range(8):
            piv = jnp.broadcast_to(b[t][t : t + 1, :], (8, B))
            r = 1.0 / piv
            rcps.append(r)
            m = b[t] * r
            mg = jnp.where(sub == t, 0.0, m)
            mf = jnp.where(sub > t, m, 0.0)
            for u in range(t + 1, 8):
                b[u] = b[u] - mg * jnp.broadcast_to(b[u][t : t + 1, :], (8, B))
            pa = jnp.broadcast_to(fa[t : t + 1, :], (8, B))
            pe = jnp.broadcast_to(fe[t : t + 1, :], (8, B))
            fa = fa - mf * pa
            fe = fe - mf * pe
            ga = ga - mg * pa
            ge = ge - mg * pe
        rc = rcps[0]
        for t in range(1, 8):
            rc = jnp.where(sub == t, rcps[t], rc)
        store(g, fa, fe, rc)
        ga = ga * rc
        ge = ge * rc
        if g < 15:
            gab = [jnp.broadcast_to(ga[t : t + 1, :], (8, B)) for t in range(8)]
            geb = [jnp.broadcast_to(ge[t : t + 1, :], (8, B)) for t in range(8)]
            for i in range(g + 1, 16):
                acc_a, acc_e = a_rows[i], e_rows[i]
                for t in range(8):
                    c = jnp.broadcast_to(a_rows[i][:, base + t : base + t + 1], (8, B))
                    acc_a = acc_a - c * gab[t]
                    acc_e = acc_e - c * geb[t]
                a_rows[i], e_rows[i] = acc_a, acc_e


HALF = PIV // 2
W2 = 2 * B


def cat_blocks(a, b, c, d):
    return jnp.concatenate([jnp.concatenate([a, b], 1), jnp.concatenate([c, d], 1)], 0)


def factor_panels(k0, k1, a_ref, b_ref, vh, vl, v32, lh, ll, t_ref, lt_ref, dinv_ref,
                  rest_ref, u_ref, part_ref, e_ref, extra):
    row0 = k0 * B
    na, nrhs = a_ref.shape[0], b_ref.shape[0]
    ri = lax.broadcasted_iota(jnp.int32, (8, B), 0)
    ci = lax.broadcasted_iota(jnp.int32, (8, B), 1)
    chunks = [(c * W2, W2) for c in range(na // W2)] + [(na, nrhs)]

    def settle(k, r0, n):
        rows, cols = slice(r0, r0 + n), pl.ds(pl.multiple_of(k * B, B), B)
        th, tl = split(t_ref[k])
        uh, ul = split(rest_ref[rows, :])
        v = dot3_t(uh, ul, th, tl)
        v32[rows, cols] = v
        vh[rows, cols], vl[rows, cols] = split(v)
        if r0 < na:
            lrows = slice(row0 + r0, row0 + r0 + n)
            lh[lrows, cols], ll[lrows, cols] = split(v * dinv_ref[0:1, cols])

    def panel(k, _):
        kcols = pl.ds(pl.multiple_of(k * B, B), B)
        acols = pl.ds(pl.multiple_of((k - k0) * B, B), B)
        prev = jnp.maximum(k - 1, k0)
        after = jnp.minimum(k + 1, k1 - 1)
        nabs = pl.ds(pl.multiple_of(after * B, B), B)
        nloc = pl.ds(pl.multiple_of((after - k0) * B, B), B)
        a_rows = [u_ref[8 * i : 8 * i + 8, :] for i in range(16)]
        e_rows = [jnp.where(ri + 8 * i == ci, 1.0, 0.0) for i in range(16)]
        diag = []

        def store(g, fa, fe, rc):
            own = ri + 8 * g == ci
            diag.append(jnp.where(own, fa, 0.0))
            lt_ref[k, 8 * g : 8 * g + 8, :] = jnp.where(own, fa, jnp.where(ri + 8 * g < ci, fa * rc, 0.0))
            e_ref[8 * g : 8 * g + 8, :] = fe

        def update(r0, n):
            rows = slice(r0, r0 + n)
            src = a_ref[rows, acols] if r0 < na else b_ref[:, acols]
            rest_ref[rows, :] = src - dot3_t(vh[rows, :], vl[rows, :], lh[kcols, :], ll[kcols, :])

        def partial():
            part_ref[...] = a_ref[nloc, nloc] - dot3_t(vh[nloc, :], vl[nloc, :], lh[nabs, :], ll[nabs, :])

        side = [lambda c=c: settle(prev, *c) for c in chunks]
        side += [lambda c=c: update(*c) for c in chunks]
        side += [partial] + extra(k)
        chain(a_rows, e_rows, store, side)
        total = diag[0]
        for g in range(1, 16):
            total = total + diag[g]
        dinv = 1.0 / jnp.sum(total, axis=0, keepdims=True)
        dinv_ref[0:1, kcols] = dinv
        t = e_ref[...]
        t_ref[k] = t
        th, tl = split(t)
        uh, ul = split(rest_ref[nloc, :])
        v = dot3_t(uh, ul, th, tl)
        v_h, v_l = split(v)
        l_h, l_l = split(v * dinv)
        u_ref[...] = part_ref[...] - dot3_t(v_h, v_l, l_h, l_l)
        return 0

    lax.fori_loop(k0, k1, panel, 0)
    for c in chunks:
        settle(k1 - 1, *c)


def first_kernel(idx_ref, y0_ref, y1_ref, y2_ref, y3_ref, b_ref,
                 vh, vl, lh, ll, t_ref, dinv_ref, y_ref, own_ref,
                 a_ref, v32, lt_ref, rest_ref, u_ref, part_ref, e_ref):
    me = idx_ref[0]
    ypos = lax.rem(me, 4)
    for d, ref in enumerate((y0_ref, y1_ref, y2_ref, y3_ref)):
        src = lax.rem(ypos + 4 - d, 4)
        for z in range(2):
            rows = pl.ds(pl.multiple_of((4 * z + src) * B, B), B)
            a_ref[rows, :] = ref[z * B : (z + 1) * B, :]
    for ref in (vh, vl, lh, ll, rest_ref, dinv_ref):
        ref[...] = jnp.zeros_like(ref)
    t_ref[0] = jnp.zeros((B, B), F32)
    u_ref[...] = a_ref[0:B, 0:B]
    factor_panels(0, NP // 2, a_ref, b_ref, vh, vl, v32, lh, ll, t_ref, lt_ref, dinv_ref,
                  rest_ref, u_ref, part_ref, e_ref, lambda k: [])
    nrhs = b_ref.shape[0]
    y_ref[...] = v32[PIV : PIV + nrhs, :]
    near = jnp.minimum(me, NP - 1)
    rows = pl.ds(pl.multiple_of(near * B, B), B)
    col = lax.broadcasted_iota(jnp.int32, (B, HALF), 1)
    own_ref[...] = jnp.where(col < near * B, v32[rows, :] * dinv_ref[0:1, :], 0.0)

    @pl.when(me < NP // 2)
    def _():
        own_ref[:, rows] = lt_ref[me].T


def whole(shape):
    zeros = (0,) * len(shape)
    return pl.BlockSpec(shape, lambda i: zeros)


def first(index, parts, rhs):
    nrhs = rhs.shape[0]
    outs = (
        ((PIV + nrhs, HALF), BF16),
        ((PIV + nrhs, HALF), BF16),
        ((PIV, HALF), BF16),
        ((PIV, HALF), BF16),
        ((NP // 2, B, B), F32),
        ((8, HALF), F32),
        ((nrhs, HALF), F32),
        ((B, HALF), F32),
    )
    return pl.pallas_call(
        first_kernel,
        grid=(1,),
        out_shape=tuple(jax.ShapeDtypeStruct(*o) for o in outs),
        in_specs=[pl.BlockSpec(memory_space=pltpu.SMEM)] + [whole((W2, HALF))] * 4 + [whole((nrhs, HALF))],
        out_specs=tuple(whole(o[0]) for o in outs),
        scratch_shapes=[
            pltpu.VMEM((PIV, HALF), F32),
            pltpu.VMEM((PIV + nrhs, HALF), F32),
            pltpu.VMEM((NP // 2, B, B), F32),
            pltpu.VMEM((PIV + nrhs, B), F32),
            pltpu.VMEM((B, B), F32),
            pltpu.VMEM((B, B), F32),
            pltpu.VMEM((B, B), F32),
        ],
        compiler_params=pltpu.CompilerParams(vmem_limit_bytes=VMEM_LIMIT),
        cost_estimate=pl.CostEstimate(flops=2 * 10**10, bytes_accessed=2 * 10**7, transcendentals=0),
        name="first",
    )(index, *parts, rhs)


def second_kernel(idx_ref, all_ref, vh0, vl0, lh0, ll0, t0, dinv0, y0, own0, mine_ref, b_ref,
                  fac_ref, eli_ref,
                  a_ref, a21, vh, vl, v32, lh, ll, t_ref, lt_ref, dinv_ref, rest_ref, u_ref, part_ref,
                  e_ref, xh, xl, x32, wh, wl, u21, tph_ref, tpl_ref, sem):
    me = idx_ref[0]
    nrhs, order = b_ref.shape
    low = order - PIV
    near_copy = pltpu.make_async_copy(all_ref.at[pl.ds(HALF, HALF), pl.ds(HALF, HALF)], a_ref, sem.at[0])
    far_copy = pltpu.make_async_copy(all_ref.at[pl.ds(PIV, low), :], a21, sem.at[1])
    near_copy.start()
    far_copy.start()
    for ref, src in ((vh, vh0), (vl, vl0)):
        ref[:, :HALF] = src[HALF:, :]
        ref[:, HALF:] = jnp.zeros((ref.shape[0], HALF), BF16)
    for ref, src in ((lh, lh0), (ll, ll0)):
        ref[:, :HALF] = src[...]
        ref[:, HALF:] = jnp.zeros((ref.shape[0], HALF), BF16)
    dinv_ref[...] = jnp.zeros_like(dinv_ref)
    dinv_ref[:, :HALF] = dinv0[...]
    t_ref[: NP // 2] = t0[...]
    t_ref[NP // 2 :] = jnp.zeros((NP // 2, B, B), F32)
    rest_ref[...] = jnp.zeros_like(rest_ref)
    xh[...] = jnp.zeros_like(xh)
    xl[...] = jnp.zeros_like(xl)
    near_copy.wait()
    u_ref[...] = a_ref[0:B, 0:B] - dot3_t(
        vh[0:B, :HALF], vl[0:B, :HALF], lh[HALF : HALF + B, :HALF], ll[HALF : HALF + B, :HALF]
    )
    far_copy.wait()

    def pair_inverse(i):
        t0h, t0l = split(t_ref[2 * i])
        t1h, t1l = split(t_ref[2 * i + 1])
        r1 = pl.ds(pl.multiple_of((2 * i + 1) * B, B), B)
        c0 = pl.ds(pl.multiple_of(2 * i * B, B), B)
        zh, zl = split(dot3_n(lh[r1, c0], ll[r1, c0], t0h, t0l))
        zh, zl = split(-dot3_n(t1h, t1l, zh, zl))
        zero = jnp.zeros((B, B), BF16)
        tph_ref[...] = cat_blocks(t0h, zero, zh, t1h)
        tpl_ref[...] = cat_blocks(t0l, zero, zl, t1l)

    def below_update(i, r0):
        rows, pc = slice(r0, r0 + W2), pl.ds(pl.multiple_of(i * W2, W2), W2)
        u21[rows, :] = a21[rows, pc] - dot3_t(xh[rows, :], xl[rows, :], lh[pc, :], ll[pc, :])

    def below_settle(i, r0):
        rows, pc = slice(r0, r0 + W2), pl.ds(pl.multiple_of(i * W2, W2), W2)
        uh, ul = split(u21[rows, :])
        v = dot3_t(uh, ul, tph_ref[...], tpl_ref[...])
        x32[rows, pc] = v
        xh[rows, pc], xl[rows, pc] = split(v)
        wh[rows, pc], wl[rows, pc] = split(v * dinv_ref[0:1, pc])

    starts = range(0, low, W2)

    def extra(k):
        i = k - NP // 2
        tasks = [lambda: pair_inverse(i)]
        for r0 in starts:
            tasks += [lambda r0=r0: (below_update(i, r0), below_settle(i, r0))]
        return tasks

    factor_panels(NP // 2, NP, a_ref, b_half(b_ref), vh, vl, v32, lh, ll, t_ref, lt_ref, dinv_ref,
                  rest_ref, u_ref, part_ref, e_ref, extra)
    last = NP // 2 - 1
    pair_inverse(last)
    for r0 in starts:
        below_settle(last, r0)

    y_late = v32[HALF : HALF + nrhs, HALF:]
    eli_ref[:, :HALF] = y0[...]
    eli_ref[:, HALF:PIV] = y_late
    mine = pl.ds(pl.multiple_of(jnp.maximum(me - NP, 0) * B, B), B)
    qh = jnp.concatenate([xh[mine, :], vh[HALF : HALF + nrhs, :]], 0)
    ql = jnp.concatenate([xl[mine, :], vl[HALF : HALF + nrhs, :]], 0)
    lower = me >= NP
    for c in range(low // W2):
        rows = slice(c * W2, (c + 1) * W2)
        dst = slice(PIV + c * W2, PIV + (c + 1) * W2)
        prod = dot3_t(qh, ql, wh[rows, :], wl[rows, :])
        row = me * B + lax.broadcasted_iota(jnp.int32, (B, W2), 0)
        col = PIV + c * W2 + lax.broadcasted_iota(jnp.int32, (B, W2), 1)
        fac_ref[:, dst] = jnp.where(row >= col, mine_ref[:, dst] - prod[:B], 0.0)
        eli_ref[:, dst] = b_ref[:, dst] - prod[B:]

    @pl.when(lower)
    def _():
        fac_ref[:, :PIV] = x32[mine, :] * dinv_ref[0:1, :]

    @pl.when(jnp.logical_not(lower))
    def _():
        fac_ref[:, :HALF] = own0[...]
        near = jnp.maximum(me - NP // 2, 0)
        rows = pl.ds(pl.multiple_of(near * B, B), B)
        col = HALF + lax.broadcasted_iota(jnp.int32, (B, HALF), 1)
        fac_ref[:, HALF:PIV] = jnp.where(col < me * B, v32[rows, HALF:] * dinv_ref[0:1, HALF:], 0.0)

    @pl.when((me >= NP // 2) & (me < NP))
    def _():
        fac_ref[:, pl.ds(pl.multiple_of(me * B, B), B)] = lt_ref[me].T


def b_half(b_ref):
    return b_ref.at[:, pl.ds(HALF, HALF)]


def second(index, gathered, state, mine, rhs):
    nrhs, order = rhs.shape
    low = order - PIV
    na = PIV - HALF
    return pl.pallas_call(
        second_kernel,
        grid=(1,),
        out_shape=(
            jax.ShapeDtypeStruct((B, order), F32),
            jax.ShapeDtypeStruct((nrhs, order), F32),
        ),
        in_specs=[pl.BlockSpec(memory_space=pltpu.SMEM), pl.BlockSpec(memory_space=pl.ANY)]
        + [whole(x.shape) for x in state]
        + [whole((B, order)), whole((nrhs, order))],
        out_specs=(whole((B, order)), whole((nrhs, order))),
        scratch_shapes=[
            pltpu.VMEM((na, na), F32),
            pltpu.VMEM((low, PIV), F32),
            pltpu.VMEM((na + nrhs, PIV), BF16),
            pltpu.VMEM((na + nrhs, PIV), BF16),
            pltpu.VMEM((na + nrhs, PIV), F32),
            pltpu.VMEM((PIV, PIV), BF16),
            pltpu.VMEM((PIV, PIV), BF16),
            pltpu.VMEM((NP, B, B), F32),
            pltpu.VMEM((NP, B, B), F32),
            pltpu.VMEM((8, PIV), F32),
            pltpu.VMEM((na + nrhs, B), F32),
            pltpu.VMEM((B, B), F32),
            pltpu.VMEM((B, B), F32),
            pltpu.VMEM((B, B), F32),
            pltpu.VMEM((low, PIV), BF16),
            pltpu.VMEM((low, PIV), BF16),
            pltpu.VMEM((low, PIV), F32),
            pltpu.VMEM((low, PIV), BF16),
            pltpu.VMEM((low, PIV), BF16),
            pltpu.VMEM((low, W2), F32),
            pltpu.VMEM((W2, W2), BF16),
            pltpu.VMEM((W2, W2), BF16),
            pltpu.SemaphoreType.DMA((2,)),
        ],
        compiler_params=pltpu.CompilerParams(vmem_limit_bytes=VMEM_LIMIT),
        name="second",
    )(index, gathered, *state, mine, rhs)


def shift_y(x, d):
    return lax.ppermute(x, "front", [(4 * z + y, 4 * z + (y + d) % 4) for z in range(4) for y in range(4)])


def planes(x, pairs):
    return lax.ppermute(x, "front", [(4 * a + y, 4 * b + y) for a, b in pairs for y in range(4)])


def gather_pivot_rows(x):
    z = lax.axis_index("front") // 4
    swap = planes(x, ((0, 1), (1, 0)))
    side = planes(x, ((1, 2), (0, 3)))
    far = planes(x, ((0, 2), (1, 3)))
    x0 = jnp.where(z == 0, x, jnp.where(z == 1, swap, jnp.where(z == 2, far, side)))
    x1 = jnp.where(z == 0, swap, jnp.where(z == 1, x, jnp.where(z == 2, side, far)))
    both = jnp.concatenate([x0, x1], 0)
    return [both] + [shift_y(both, d) for d in (1, 2, 3)]


def local(front_matrix, child_blocks, child_target, child_count, shot_rhs):
    leaves, slots = child_blocks.shape[1:3]
    slot_ids = lax.broadcasted_iota(jnp.int32, (leaves, slots), 1)
    live_code = jnp.where(slot_ids < child_count[0][:, None], child_target[0], -1)
    code_rows = jnp.zeros((leaves, 8, B), F32).at[:, 0, :slots].set(live_code.astype(F32))
    payload = jnp.concatenate([child_blocks[0].reshape(leaves, slots * B, B), code_rows], axis=1)
    arrived = lax.all_to_all(payload, "leaf", split_axis=0, concat_axis=0, tiled=True)
    codes = arrived[:, slots * B, :slots].astype(jnp.int32)
    index = lax.axis_index("front").astype(jnp.int32).reshape(1)
    mine = assemble(codes, index, arrived, front_matrix[0])
    gathered = lax.all_gather(mine[:, :PIV], "front", axis=0, tiled=True)
    rhs = shot_rhs[0]
    state = first(index, gather_pivot_rows(mine[:, :HALF]), rhs)
    factored, eliminated = second(index, gathered, state, mine, rhs)
    return factored[None], eliminated[None]


def solution(mesh):
    return jax.shard_map(
        local,
        mesh=mesh,
        in_specs=(
            P("leaf", "front", None),
            P(("leaf", "front"), None, None, None, None),
            P(("leaf", "front"), None, None),
            P(("leaf", "front"), None),
            P("leaf", None, None),
        ),
        out_specs=(P("leaf", "front", None), P("leaf", None, None)),
        check_vma=False,
    )
```

```python
import jax
import jax.numpy as jnp
from jax import lax
from jax.experimental import pallas as pl
from jax.experimental.pallas import tpu as pltpu
from jax.sharding import PartitionSpec as P

B = 128
PIV = 1024
NP = PIV // B
HALF = PIV // 2
W2 = 2 * B
F32 = jnp.float32
BF16 = jnp.bfloat16


def split(x):
    hi = x.astype(BF16)
    lo = (x - hi.astype(F32)).astype(BF16)
    return hi, lo


def dot_t(a, b):
    return lax.dot_general(a, b, (((1,), (1,)), ((), ())), preferred_element_type=F32)


def dot_n(a, b):
    return lax.dot_general(a, b, (((1,), (0,)), ((), ())), preferred_element_type=F32)


def dot3_t(ah, al, bh, bl):
    return dot_t(ah, bh) + dot_t(al, bh) + dot_t(ah, bl)


def dot3_n(ah, al, bh, bl):
    return dot_n(ah, bh) + dot_n(al, bh) + dot_n(ah, bl)


def assemble_kernel(code_ref, idx_ref, recv_ref, front_ref, late_ref, early_ref, pivot_ref, out_ref):
    out_ref[...] = front_ref[...]
    for s in range(recv_ref.shape[0]):
        for j in range(code_ref.shape[1]):
            code = code_ref[s, j]

            @pl.when(code >= 0)
            def _(s=s, j=j, code=code):
                cols = pl.ds(pl.multiple_of(code * B, B), B)
                out_ref[:, cols] += recv_ref[s, j * B : (j + 1) * B, :]

    cols = pl.ds(pl.multiple_of(idx_ref[0] * B, B), B)
    square = out_ref[:, cols]
    row = lax.broadcasted_iota(jnp.int32, (B, B), 0)
    col = lax.broadcasted_iota(jnp.int32, (B, B), 1)
    out_ref[:, cols] = jnp.where(row >= col, square, square.T)
    early_ref[...] = out_ref[:, :HALF]
    pivot_ref[...] = out_ref[:, :PIV]
    late_ref[...] = out_ref[:, PIV:]


def assemble(codes, index, recv, front):
    rows, order = front.shape
    vmem = pl.BlockSpec(memory_space=pltpu.VMEM)
    return pl.pallas_call(
        assemble_kernel,
        out_shape=(
            jax.ShapeDtypeStruct((rows, order - PIV), F32),
            jax.ShapeDtypeStruct((rows, HALF), F32),
            jax.ShapeDtypeStruct((rows, PIV), F32),
        ),
        in_specs=[pl.BlockSpec(memory_space=pltpu.SMEM)] * 2 + [vmem, vmem],
        out_specs=(vmem, vmem, vmem),
        scratch_shapes=[pltpu.VMEM((rows, order), F32)],
        compiler_params=pltpu.CompilerParams(vmem_limit_bytes=8 * 1024 * 1024),
        name="assemble",
    )(codes, index, recv, front)


def lane(x, c):
    return jnp.broadcast_to(x[:, c : c + 1], (8, B))


def sublane(x, t):
    return jnp.broadcast_to(x[t : t + 1, :], (8, B))


def chain(a_rows, e_rows, store, side):
    sub = lax.broadcasted_iota(jnp.int32, (8, B), 0)
    ahead = None
    for g in range(16):
        if g < len(side):
            side[g]()
        ra, re = a_rows[g], e_rows[g]
        base = 8 * g
        b = ahead or [lane(ra, base + t) for t in range(8)]
        more, far = g < 15, g < 14
        if more:
            na, ne = a_rows[g + 1], e_rows[g + 1]
            c = [lane(na, base + t) for t in range(8)]
            q = [lane(ra, base + 8 + t) for t in range(8)]
            ahead = [lane(na, base + 8 + t) for t in range(8)]
        ga, ge = ra, re
        fa, fe = ra, re
        rcps = []
        for t in range(8):
            r = 1.0 / sublane(b[t], t)
            rcps.append(r)
            m = b[t] * r
            mg = jnp.where(sub == t, 0.0, m)
            mf = jnp.where(sub > t, m, 0.0)
            pa, pe = sublane(fa, t), sublane(fe, t)
            if more:
                mn = c[t] * r
            for u in range(t + 1, 8):
                w = sublane(b[u], t)
                b[u] = b[u] - mg * w
                if more:
                    c[u] = c[u] - mn * w
            if more:
                for u in range(8):
                    w = sublane(q[u], t)
                    q[u] = q[u] - mf * w
                    ahead[u] = ahead[u] - mn * w
                na = na - mn * pa
                ne = ne - mn * pe
            fa = fa - mf * pa
            fe = fe - mf * pe
            if far:
                ga = ga - mg * pa
                ge = ge - mg * pe
        rc = rcps[0]
        for t in range(1, 8):
            rc = jnp.where(sub == t, rcps[t], rc)
        store(g, fa, fe, rc)
        if more:
            a_rows[g + 1], e_rows[g + 1] = na, ne
        if far:
            ga = ga * rc
            ge = ge * rc
            gab = [sublane(ga, t) for t in range(8)]
            geb = [sublane(ge, t) for t in range(8)]
            for i in range(g + 2, 16):
                acc_a, acc_e = a_rows[i], e_rows[i]
                for t in range(8):
                    cc = lane(a_rows[i], base + t)
                    acc_a = acc_a - cc * gab[t]
                    acc_e = acc_e - cc * geb[t]
                a_rows[i], e_rows[i] = acc_a, acc_e


def cat_blocks(a, b, c, d):
    return jnp.concatenate([jnp.concatenate([a, b], 1), jnp.concatenate([c, d], 1)], 0)


def factor_panels(k0, k1, a_ref, b_ref, vh, vl, v32, lh, ll, t_ref, lt_ref, dinv_ref,
                  rest_ref, u_ref, part_ref, e_ref, extra):
    row0 = k0 * B
    na, nrhs = a_ref.shape[0], b_ref.shape[0]
    ri = lax.broadcasted_iota(jnp.int32, (8, B), 0)
    ci = lax.broadcasted_iota(jnp.int32, (8, B), 1)

    def settle(k):
        cols = pl.ds(pl.multiple_of(k * B, B), B)
        th, tl = split(t_ref[k])
        uh, ul = split(rest_ref[...])
        v = dot3_t(uh, ul, th, tl)
        v32[:, cols] = v
        vh[:, cols], vl[:, cols] = split(v)
        lrows = slice(row0, row0 + na)
        lh[lrows, cols], ll[lrows, cols] = split(v[:na] * dinv_ref[0:1, cols])

    def panel(k, _):
        kcols = pl.ds(pl.multiple_of(k * B, B), B)
        acols = pl.ds(pl.multiple_of((k - k0) * B, B), B)
        prev = jnp.maximum(k - 1, k0)
        after = jnp.minimum(k + 1, k1 - 1)
        nabs = pl.ds(pl.multiple_of(after * B, B), B)
        nloc = pl.ds(pl.multiple_of((after - k0) * B, B), B)
        a_rows = [u_ref[8 * i : 8 * i + 8, :] for i in range(16)]
        e_rows = [jnp.where(ri + 8 * i == ci, 1.0, 0.0) for i in range(16)]
        diag = []

        def store(g, fa, fe, rc):
            own = ri + 8 * g == ci
            diag.append(jnp.where(own, fa, 0.0))
            lt_ref[k, 8 * g : 8 * g + 8, :] = jnp.where(own, fa, jnp.where(ri + 8 * g < ci, fa * rc, 0.0))
            e_ref[8 * g : 8 * g + 8, :] = fe

        def update():
            prod = dot3_t(vh[...], vl[...], lh[kcols, :], ll[kcols, :])
            rest_ref[:na, :] = a_ref[:, acols] - prod[:na]
            rest_ref[na:, :] = b_ref[:, acols] - prod[na:]

        def partial():
            part_ref[...] = a_ref[nloc, nloc] - dot3_t(vh[nloc, :], vl[nloc, :], lh[nabs, :], ll[nabs, :])

        side = [lambda: settle(prev), update, partial] + extra(k)
        chain(a_rows, e_rows, store, side)
        total = diag[0]
        for g in range(1, 16):
            total = total + diag[g]
        dinv = 1.0 / jnp.sum(total, axis=0, keepdims=True)
        dinv_ref[0:1, kcols] = dinv
        t = e_ref[...]
        t_ref[k] = t
        th, tl = split(t)
        uh, ul = split(rest_ref[nloc, :])
        v = dot3_t(uh, ul, th, tl)
        v_h, v_l = split(v)
        l_h, l_l = split(v * dinv)
        u_ref[...] = part_ref[...] - dot3_t(v_h, v_l, l_h, l_l)
        return 0

    lax.fori_loop(k0, k1, panel, 0)
    settle(k1 - 1)


def first_kernel(idx_ref, y0_ref, y1_ref, y2_ref, y3_ref, b_ref,
                 vh, vl, lh, ll, t_ref, dinv_ref, y_ref, own_ref,
                 a_ref, v32, lt_ref, rest_ref, u_ref, part_ref, e_ref):
    me = idx_ref[0]
    ypos = lax.rem(me, 4)
    for d, ref in enumerate((y0_ref, y1_ref, y2_ref, y3_ref)):
        src = lax.rem(ypos + 4 - d, 4)
        for z in range(2):
            rows = pl.ds(pl.multiple_of((4 * z + src) * B, B), B)
            a_ref[rows, :] = ref[z * B : (z + 1) * B, :]
    for ref in (vh, vl, lh, ll, rest_ref, dinv_ref):
        ref[...] = jnp.zeros_like(ref)
    t_ref[0] = jnp.zeros((B, B), F32)
    u_ref[...] = a_ref[0:B, 0:B]
    factor_panels(0, NP // 2, a_ref, b_ref.at[:, pl.ds(0, HALF)], vh, vl, v32, lh, ll, t_ref, lt_ref, dinv_ref,
                  rest_ref, u_ref, part_ref, e_ref, lambda k: [])
    nrhs = b_ref.shape[0]
    y_ref[...] = v32[PIV : PIV + nrhs, :]
    near = jnp.minimum(me, NP - 1)
    rows = pl.ds(pl.multiple_of(near * B, B), B)
    col = lax.broadcasted_iota(jnp.int32, (B, HALF), 1)
    own_ref[...] = jnp.where(col < near * B, v32[rows, :] * dinv_ref[0:1, :], 0.0)

    @pl.when(me < NP // 2)
    def _():
        own_ref[:, rows] = lt_ref[me].T


VMEM_SPEC = pl.BlockSpec(memory_space=pltpu.VMEM)


def first(index, parts, rhs):
    nrhs = rhs.shape[0]
    outs = (
        ((PIV + nrhs, HALF), BF16),
        ((PIV + nrhs, HALF), BF16),
        ((PIV, HALF), BF16),
        ((PIV, HALF), BF16),
        ((NP // 2, B, B), F32),
        ((8, HALF), F32),
        ((nrhs, HALF), F32),
        ((B, HALF), F32),
    )
    return pl.pallas_call(
        first_kernel,
        out_shape=tuple(jax.ShapeDtypeStruct(*o) for o in outs),
        in_specs=[pl.BlockSpec(memory_space=pltpu.SMEM)] + [VMEM_SPEC] * 5,
        out_specs=(VMEM_SPEC,) * len(outs),
        scratch_shapes=[
            pltpu.VMEM((PIV, HALF), F32),
            pltpu.VMEM((PIV + nrhs, HALF), F32),
            pltpu.VMEM((NP // 2, B, B), F32),
            pltpu.VMEM((PIV + nrhs, B), F32),
            pltpu.VMEM((B, B), F32),
            pltpu.VMEM((B, B), F32),
            pltpu.VMEM((B, B), F32),
        ],
        compiler_params=pltpu.CompilerParams(vmem_limit_bytes=20 * 1024 * 1024),
        cost_estimate=pl.CostEstimate(flops=2 * 10**10, bytes_accessed=2 * 10**7, transcendentals=0),
        name="first",
    )(index, *parts, rhs)


def second_kernel(idx_ref, all_ref, vh0, vl0, lh0, ll0, t0, dinv0, y0, own0, mine_ref, b_ref,
                  fac_ref, eli_ref,
                  a_ref, a21, vh, vl, v32, lh, ll, t_ref, lt_ref, dinv_ref, rest_ref, u_ref, part_ref,
                  e_ref, xh, xl, x32, wh, wl, u21, tph_ref, tpl_ref, sem):
    me = idx_ref[0]
    nrhs, order = b_ref.shape
    low = order - PIV
    near_copy = pltpu.make_async_copy(all_ref.at[pl.ds(HALF, HALF), pl.ds(HALF, HALF)], a_ref, sem.at[0])
    far_copy = pltpu.make_async_copy(all_ref.at[pl.ds(PIV, low), :], a21, sem.at[1])
    near_copy.start()
    far_copy.start()
    for ref, src in ((vh, vh0), (vl, vl0)):
        ref[:, :HALF] = src[HALF:, :]
        ref[:, HALF:] = jnp.zeros((ref.shape[0], HALF), BF16)
    for ref, src in ((lh, lh0), (ll, ll0)):
        ref[:, :HALF] = src[...]
        ref[:, HALF:] = jnp.zeros((ref.shape[0], HALF), BF16)
    dinv_ref[...] = jnp.zeros_like(dinv_ref)
    dinv_ref[:, :HALF] = dinv0[...]
    t_ref[: NP // 2] = t0[...]
    t_ref[NP // 2 :] = jnp.zeros((NP // 2, B, B), F32)
    rest_ref[...] = jnp.zeros_like(rest_ref)
    xh[...] = jnp.zeros_like(xh)
    xl[...] = jnp.zeros_like(xl)
    near_copy.wait()
    u_ref[...] = a_ref[0:B, 0:B] - dot3_t(
        vh[0:B, :HALF], vl[0:B, :HALF], lh[HALF : HALF + B, :HALF], ll[HALF : HALF + B, :HALF]
    )
    far_copy.wait()

    def pair_inverse(i):
        t0h, t0l = split(t_ref[2 * i])
        t1h, t1l = split(t_ref[2 * i + 1])
        r1 = pl.ds(pl.multiple_of((2 * i + 1) * B, B), B)
        c0 = pl.ds(pl.multiple_of(2 * i * B, B), B)
        zh, zl = split(dot3_n(lh[r1, c0], ll[r1, c0], t0h, t0l))
        zh, zl = split(-dot3_n(t1h, t1l, zh, zl))
        zero = jnp.zeros((B, B), BF16)
        tph_ref[...] = cat_blocks(t0h, zero, zh, t1h)
        tpl_ref[...] = cat_blocks(t0l, zero, zl, t1l)

    def below_update(i):
        pc = pl.ds(pl.multiple_of(i * W2, W2), W2)
        u21[...] = a21[:, pc] - dot3_t(xh[...], xl[...], lh[pc, :], ll[pc, :])

    def below_settle(i):
        pc = pl.ds(pl.multiple_of(i * W2, W2), W2)
        uh, ul = split(u21[...])
        v = dot3_t(uh, ul, tph_ref[...], tpl_ref[...])
        x32[:, pc] = v
        xh[:, pc], xl[:, pc] = split(v)
        wh[:, pc], wl[:, pc] = split(v * dinv_ref[0:1, pc])

    def extra(k):
        i = k - NP // 2
        return [lambda: pair_inverse(i), lambda: below_update(i), lambda: below_settle(i)]

    factor_panels(NP // 2, NP, a_ref, b_half(b_ref), vh, vl, v32, lh, ll, t_ref, lt_ref, dinv_ref,
                  rest_ref, u_ref, part_ref, e_ref, extra)
    last = NP // 2 - 1
    pair_inverse(last)
    below_settle(last)

    y_late = v32[HALF : HALF + nrhs, HALF:]
    eli_ref[:, :HALF] = y0[...]
    eli_ref[:, HALF:PIV] = y_late
    mine = pl.ds(pl.multiple_of(jnp.maximum(me - NP, 0) * B, B), B)
    qh = jnp.concatenate([xh[mine, :], vh[HALF : HALF + nrhs, :]], 0)
    ql = jnp.concatenate([xl[mine, :], vl[HALF : HALF + nrhs, :]], 0)
    lower = me >= NP
    for c in range(low // W2):
        rows = slice(c * W2, (c + 1) * W2)
        dst = slice(PIV + c * W2, PIV + (c + 1) * W2)
        prod = dot3_t(qh, ql, wh[rows, :], wl[rows, :])
        row = me * B + lax.broadcasted_iota(jnp.int32, (B, W2), 0)
        col = PIV + c * W2 + lax.broadcasted_iota(jnp.int32, (B, W2), 1)
        fac_ref[:, dst] = jnp.where(row >= col, mine_ref[:, rows] - prod[:B], 0.0)
        eli_ref[:, dst] = b_ref[:, dst] - prod[B:]

    @pl.when(lower)
    def _():
        fac_ref[:, :PIV] = x32[mine, :] * dinv_ref[0:1, :]

    @pl.when(jnp.logical_not(lower))
    def _():
        fac_ref[:, :HALF] = own0[...]
        near = jnp.maximum(me - NP // 2, 0)
        rows = pl.ds(pl.multiple_of(near * B, B), B)
        col = HALF + lax.broadcasted_iota(jnp.int32, (B, HALF), 1)
        fac_ref[:, HALF:PIV] = jnp.where(col < me * B, v32[rows, HALF:] * dinv_ref[0:1, HALF:], 0.0)

    @pl.when((me >= NP // 2) & (me < NP))
    def _():
        fac_ref[:, pl.ds(pl.multiple_of(me * B, B), B)] = lt_ref[me].T


def b_half(b_ref):
    return b_ref.at[:, pl.ds(HALF, HALF)]


def second(index, gathered, state, mine, rhs):
    nrhs, order = rhs.shape
    low = order - PIV
    na = PIV - HALF
    return pl.pallas_call(
        second_kernel,
        out_shape=(
            jax.ShapeDtypeStruct((B, order), F32),
            jax.ShapeDtypeStruct((nrhs, order), F32),
        ),
        in_specs=[pl.BlockSpec(memory_space=pltpu.SMEM), pl.BlockSpec(memory_space=pl.ANY)]
        + [VMEM_SPEC] * (len(state) + 2),
        out_specs=(VMEM_SPEC, VMEM_SPEC),
        scratch_shapes=[
            pltpu.VMEM((na, na), F32),
            pltpu.VMEM((low, PIV), F32),
            pltpu.VMEM((na + nrhs, PIV), BF16),
            pltpu.VMEM((na + nrhs, PIV), BF16),
            pltpu.VMEM((na + nrhs, PIV), F32),
            pltpu.VMEM((PIV, PIV), BF16),
            pltpu.VMEM((PIV, PIV), BF16),
            pltpu.VMEM((NP, B, B), F32),
            pltpu.VMEM((NP, B, B), F32),
            pltpu.VMEM((8, PIV), F32),
            pltpu.VMEM((na + nrhs, B), F32),
            pltpu.VMEM((B, B), F32),
            pltpu.VMEM((B, B), F32),
            pltpu.VMEM((B, B), F32),
            pltpu.VMEM((low, PIV), BF16),
            pltpu.VMEM((low, PIV), BF16),
            pltpu.VMEM((low, PIV), F32),
            pltpu.VMEM((low, PIV), BF16),
            pltpu.VMEM((low, PIV), BF16),
            pltpu.VMEM((low, W2), F32),
            pltpu.VMEM((W2, W2), BF16),
            pltpu.VMEM((W2, W2), BF16),
            pltpu.SemaphoreType.DMA((2,)),
        ],
        compiler_params=pltpu.CompilerParams(vmem_limit_bytes=44 * 1024 * 1024),
        name="second",
    )(index, gathered, *state, mine, rhs)


def shift_y(x, d):
    return lax.ppermute(x, "front", [(4 * z + y, 4 * z + (y + d) % 4) for z in range(4) for y in range(4)])


def planes(x, pairs):
    return lax.ppermute(x, "front", [(4 * a + y, 4 * b + y) for a, b in pairs for y in range(4)])


def gather_pivot_rows(x):
    z = lax.axis_index("front") // 4
    swap = planes(x, ((0, 1), (1, 0)))
    side = planes(x, ((1, 2), (0, 3)))
    far = planes(x, ((0, 2), (1, 3)))
    x0 = jnp.where(z == 0, x, jnp.where(z == 1, swap, jnp.where(z == 2, far, side)))
    x1 = jnp.where(z == 0, swap, jnp.where(z == 1, x, jnp.where(z == 2, side, far)))
    both = jnp.concatenate([x0, x1], 0)
    return [both] + [shift_y(both, d) for d in (1, 2, 3)]


def local(front_matrix, child_blocks, child_target, child_count, shot_rhs):
    leaves, slots = child_blocks.shape[1:3]
    slot_ids = lax.broadcasted_iota(jnp.int32, (leaves, slots), 1)
    live_code = jnp.where(slot_ids < child_count[0][:, None], child_target[0], -1)
    code_rows = jnp.zeros((leaves, 8, B), F32).at[:, 0, :slots].set(live_code.astype(F32))
    payload = jnp.concatenate([child_blocks[0].reshape(leaves, slots * B, B), code_rows], axis=1)
    arrived = lax.all_to_all(payload, "leaf", split_axis=0, concat_axis=0, tiled=True)
    codes = arrived[:, slots * B, :slots].astype(jnp.int32)
    index = lax.axis_index("front").astype(jnp.int32).reshape(1)
    late, early, pivots = assemble(codes, index, arrived, front_matrix[0])
    gathered = lax.all_gather(pivots, "front", axis=0, tiled=True)
    rhs = shot_rhs[0]
    state = first(index, gather_pivot_rows(early), rhs)
    factored, eliminated = second(index, gathered, state, late, rhs)
    return factored[None], eliminated[None]


def solution(mesh):
    return jax.shard_map(
        local,
        mesh=mesh,
        in_specs=(
            P("leaf", "front", None),
            P(("leaf", "front"), None, None, None, None),
            P(("leaf", "front"), None, None),
            P(("leaf", "front"), None),
            P("leaf", None, None),
        ),
        out_specs=(P("leaf", "front", None), P("leaf", None, None)),
        check_vma=False,
    )
```

```python
import jax
import jax.numpy as jnp
from jax import lax
from jax.experimental import pallas as pl
from jax.experimental.pallas import tpu as pltpu
from jax.sharding import PartitionSpec as P

B = 128
PIV = 1024
NP = PIV // B
HALF = PIV // 2
W2 = 2 * B
F32 = jnp.float32
BF16 = jnp.bfloat16


def split(x):
    hi = x.astype(BF16)
    lo = (x - hi.astype(F32)).astype(BF16)
    return hi, lo


def dot_t(a, b):
    return lax.dot_general(a, b, (((1,), (1,)), ((), ())), preferred_element_type=F32)


def dot_n(a, b):
    return lax.dot_general(a, b, (((1,), (0,)), ((), ())), preferred_element_type=F32)


def dot3_t(ah, al, bh, bl):
    return dot_t(ah, bh) + dot_t(al, bh) + dot_t(ah, bl)


def dot3_n(ah, al, bh, bl):
    return dot_n(ah, bh) + dot_n(al, bh) + dot_n(ah, bl)


def assemble_kernel(code_ref, idx_ref, recv_ref, front_ref, late_ref, pivot_ref, out_ref):
    out_ref[...] = front_ref[...]
    for s in range(recv_ref.shape[0]):
        for j in range(code_ref.shape[1]):
            code = code_ref[s, j]

            @pl.when(code >= 0)
            def _(s=s, j=j, code=code):
                cols = pl.ds(pl.multiple_of(code * B, B), B)
                out_ref[:, cols] += recv_ref[s, j * B : (j + 1) * B, :]

    cols = pl.ds(pl.multiple_of(idx_ref[0] * B, B), B)
    square = out_ref[:, cols]
    row = lax.broadcasted_iota(jnp.int32, (B, B), 0)
    col = lax.broadcasted_iota(jnp.int32, (B, B), 1)
    out_ref[:, cols] = jnp.where(row >= col, square, square.T)
    pivot_ref[...] = out_ref[:, :PIV]
    late_ref[...] = out_ref[:, PIV:]


def assemble(codes, index, recv, front):
    rows, order = front.shape
    vmem = pl.BlockSpec(memory_space=pltpu.VMEM)
    return pl.pallas_call(
        assemble_kernel,
        out_shape=(
            jax.ShapeDtypeStruct((rows, order - PIV), F32),
            jax.ShapeDtypeStruct((rows, PIV), F32),
        ),
        in_specs=[pl.BlockSpec(memory_space=pltpu.SMEM)] * 2 + [vmem, vmem],
        out_specs=(vmem, vmem),
        scratch_shapes=[pltpu.VMEM((rows, order), F32)],
        compiler_params=pltpu.CompilerParams(vmem_limit_bytes=8 * 1024 * 1024),
        name="assemble",
    )(codes, index, recv, front)


def lane(x, c):
    return jnp.broadcast_to(x[:, c : c + 1], (8, B))


def sublane(x, t):
    return jnp.broadcast_to(x[t : t + 1, :], (8, B))


def chain(a_rows, e_rows, store, side):
    sub = lax.broadcasted_iota(jnp.int32, (8, B), 0)
    ahead = None
    for g in range(16):
        if g < len(side):
            side[g]()
        ra, re = a_rows[g], e_rows[g]
        base = 8 * g
        b = ahead or [lane(ra, base + t) for t in range(8)]
        more, far = g < 15, g < 14
        if more:
            na, ne = a_rows[g + 1], e_rows[g + 1]
            c = [lane(na, base + t) for t in range(8)]
            q = [lane(ra, base + 8 + t) for t in range(8)]
            ahead = [lane(na, base + 8 + t) for t in range(8)]
        ga, ge = ra, re
        fa, fe = ra, re
        rcps = []
        for t in range(8):
            r = 1.0 / sublane(b[t], t)
            rcps.append(r)
            m = b[t] * r
            mg = jnp.where(sub == t, 0.0, m)
            mf = jnp.where(sub > t, m, 0.0)
            pa, pe = sublane(fa, t), sublane(fe, t)
            if more:
                mn = c[t] * r
            for u in range(t + 1, 8):
                w = sublane(b[u], t)
                b[u] = b[u] - mg * w
                if more:
                    c[u] = c[u] - mn * w
            if more:
                for u in range(8):
                    w = sublane(q[u], t)
                    q[u] = q[u] - mf * w
                    ahead[u] = ahead[u] - mn * w
                na = na - mn * pa
                ne = ne - mn * pe
            fa = fa - mf * pa
            fe = fe - mf * pe
            if far:
                ga = ga - mg * pa
                ge = ge - mg * pe
        rc = rcps[0]
        for t in range(1, 8):
            rc = jnp.where(sub == t, rcps[t], rc)
        store(g, fa, fe, rc)
        if more:
            a_rows[g + 1], e_rows[g + 1] = na, ne
        if far:
            ga = ga * rc
            ge = ge * rc
            gab = [sublane(ga, t) for t in range(8)]
            geb = [sublane(ge, t) for t in range(8)]
            for i in range(g + 2, 16):
                acc_a, acc_e = a_rows[i], e_rows[i]
                for t in range(8):
                    cc = lane(a_rows[i], base + t)
                    acc_a = acc_a - cc * gab[t]
                    acc_e = acc_e - cc * geb[t]
                a_rows[i], e_rows[i] = acc_a, acc_e


def cat_blocks(a, b, c, d):
    return jnp.concatenate([jnp.concatenate([a, b], 1), jnp.concatenate([c, d], 1)], 0)


def factor_panels(k0, k1, a_ref, b_ref, vh, vl, v32, lh, ll, t_ref, lt_ref, dinv_ref,
                  rest_ref, u_ref, part_ref, e_ref, extra):
    row0 = k0 * B
    na, nrhs = a_ref.shape[0], b_ref.shape[0]
    ri = lax.broadcasted_iota(jnp.int32, (8, B), 0)
    ci = lax.broadcasted_iota(jnp.int32, (8, B), 1)

    def settle(k):
        cols = pl.ds(pl.multiple_of(k * B, B), B)
        th, tl = split(t_ref[k])
        uh, ul = split(rest_ref[...])
        v = dot3_t(uh, ul, th, tl)
        v32[:, cols] = v
        vh[:, cols], vl[:, cols] = split(v)
        lrows = slice(row0, row0 + na)
        lh[lrows, cols], ll[lrows, cols] = split(v[:na] * dinv_ref[0:1, cols])

    def panel(k, _):
        kcols = pl.ds(pl.multiple_of(k * B, B), B)
        acols = pl.ds(pl.multiple_of((k - k0) * B, B), B)
        prev = jnp.maximum(k - 1, k0)
        after = jnp.minimum(k + 1, k1 - 1)
        nabs = pl.ds(pl.multiple_of(after * B, B), B)
        nloc = pl.ds(pl.multiple_of((after - k0) * B, B), B)
        a_rows = [u_ref[8 * i : 8 * i + 8, :] for i in range(16)]
        e_rows = [jnp.where(ri + 8 * i == ci, 1.0, 0.0) for i in range(16)]
        diag = []

        def store(g, fa, fe, rc):
            own = ri + 8 * g == ci
            diag.append(jnp.where(own, fa, 0.0))
            lt_ref[k, 8 * g : 8 * g + 8, :] = jnp.where(own, fa, jnp.where(ri + 8 * g < ci, fa * rc, 0.0))
            e_ref[8 * g : 8 * g + 8, :] = fe

        def update():
            prod = dot3_t(vh[...], vl[...], lh[kcols, :], ll[kcols, :])
            rest_ref[:na, :] = a_ref[:, acols] - prod[:na]
            rest_ref[na:, :] = b_ref[:, acols] - prod[na:]

        def partial():
            part_ref[...] = a_ref[nloc, nloc] - dot3_t(vh[nloc, :], vl[nloc, :], lh[nabs, :], ll[nabs, :])

        side = [lambda: settle(prev), update, partial] + extra(k)
        chain(a_rows, e_rows, store, side)
        total = diag[0]
        for g in range(1, 16):
            total = total + diag[g]
        dinv = 1.0 / jnp.sum(total, axis=0, keepdims=True)
        dinv_ref[0:1, kcols] = dinv
        t = e_ref[...]
        t_ref[k] = t
        th, tl = split(t)
        uh, ul = split(rest_ref[nloc, :])
        v = dot3_t(uh, ul, th, tl)
        v_h, v_l = split(v)
        l_h, l_l = split(v * dinv)
        u_ref[...] = part_ref[...] - dot3_t(v_h, v_l, l_h, l_l)
        return 0

    lax.fori_loop(k0, k1, panel, 0)
    settle(k1 - 1)


def first_kernel(idx_ref, y0_ref, y1_ref, y2_ref, y3_ref, b_ref,
                 vh, vl, lh, ll, t_ref, dinv_ref, y_ref, own_ref,
                 a_ref, v32, lt_ref, rest_ref, u_ref, part_ref, e_ref):
    me = idx_ref[0]
    ypos = lax.rem(me, 4)
    for d, ref in enumerate((y0_ref, y1_ref, y2_ref, y3_ref)):
        src = lax.rem(ypos + 4 - d, 4)
        for z in range(2):
            rows = pl.ds(pl.multiple_of((4 * z + src) * B, B), B)
            a_ref[rows, :] = ref[z * B : (z + 1) * B, :]
    for ref in (vh, vl, lh, ll, rest_ref, dinv_ref):
        ref[...] = jnp.zeros_like(ref)
    t_ref[0] = jnp.zeros((B, B), F32)
    u_ref[...] = a_ref[0:B, 0:B]
    factor_panels(0, NP // 2, a_ref, b_ref.at[:, pl.ds(0, HALF)], vh, vl, v32, lh, ll, t_ref, lt_ref, dinv_ref,
                  rest_ref, u_ref, part_ref, e_ref, lambda k: [])
    nrhs = b_ref.shape[0]
    y_ref[...] = v32[PIV : PIV + nrhs, :]
    near = jnp.minimum(me, NP - 1)
    rows = pl.ds(pl.multiple_of(near * B, B), B)
    col = lax.broadcasted_iota(jnp.int32, (B, HALF), 1)
    own_ref[...] = jnp.where(col < near * B, v32[rows, :] * dinv_ref[0:1, :], 0.0)

    @pl.when(me < NP // 2)
    def _():
        own_ref[:, rows] = lt_ref[me].T


VMEM_SPEC = pl.BlockSpec(memory_space=pltpu.VMEM)


def first(index, parts, rhs):
    nrhs = rhs.shape[0]
    outs = (
        ((PIV + nrhs, HALF), BF16),
        ((PIV + nrhs, HALF), BF16),
        ((PIV, HALF), BF16),
        ((PIV, HALF), BF16),
        ((NP // 2, B, B), F32),
        ((8, HALF), F32),
        ((nrhs, HALF), F32),
        ((B, HALF), F32),
    )
    return pl.pallas_call(
        first_kernel,
        out_shape=tuple(jax.ShapeDtypeStruct(*o) for o in outs),
        in_specs=[pl.BlockSpec(memory_space=pltpu.SMEM)] + [VMEM_SPEC] * 5,
        out_specs=(VMEM_SPEC,) * len(outs),
        scratch_shapes=[
            pltpu.VMEM((PIV, HALF), F32),
            pltpu.VMEM((PIV + nrhs, HALF), F32),
            pltpu.VMEM((NP // 2, B, B), F32),
            pltpu.VMEM((PIV + nrhs, B), F32),
            pltpu.VMEM((B, B), F32),
            pltpu.VMEM((B, B), F32),
            pltpu.VMEM((B, B), F32),
        ],
        compiler_params=pltpu.CompilerParams(vmem_limit_bytes=20 * 1024 * 1024),
        cost_estimate=pl.CostEstimate(flops=2 * 10**10, bytes_accessed=2 * 10**7, transcendentals=0),
        name="first",
    )(index, *parts, rhs)


def second_kernel(idx_ref, near_ref, far_ref, p0_ref, p1_ref, p2_ref, p3_ref, vh0, vl0, lh0, ll0, t0, dinv0, y0, own0, mine_ref, b_ref,
                  fac_ref, eli_ref,
                  a_ref, a21, vh, vl, v32, lh, ll, t_ref, lt_ref, dinv_ref, rest_ref, u_ref, part_ref,
                  e_ref, xh, xl, x32, wh, wl, u21, tph_ref, tpl_ref, sem):
    me = idx_ref[0]
    nrhs, order = b_ref.shape
    low = order - PIV
    ypos, zpos = lax.rem(me, 4), jnp.maximum(me // 4 - 2, 0)
    copies = []
    for n, (ref, z) in enumerate(((near_ref, zpos), (far_ref, 1 - jnp.minimum(zpos, 1)))):
        for d in range(4):
            row = pl.multiple_of((4 * z + lax.rem(ypos + 4 - d, 4)) * B, B)
            copies.append(pltpu.make_async_copy(
                ref.at[pl.ds(d * B, B), :], a21.at[pl.ds(row, B), :], sem.at[4 * n + d]))
    for copy in copies:
        copy.start()
    for d, ref in enumerate((p0_ref, p1_ref, p2_ref, p3_ref)):
        rows = pl.ds(pl.multiple_of(lax.rem(ypos + 4 - d, 4) * B, B), B)
        a_ref[rows, :] = ref[W2 : W2 + B, :]
    for ref, src in ((vh, vh0), (vl, vl0)):
        ref[:, :HALF] = src[HALF:, :]
        ref[:, HALF:] = jnp.zeros((ref.shape[0], HALF), BF16)
    for ref, src in ((lh, lh0), (ll, ll0)):
        ref[:, :HALF] = src[...]
        ref[:, HALF:] = jnp.zeros((ref.shape[0], HALF), BF16)
    dinv_ref[...] = jnp.zeros_like(dinv_ref)
    dinv_ref[:, :HALF] = dinv0[...]
    t_ref[: NP // 2] = t0[...]
    t_ref[NP // 2 :] = jnp.zeros((NP // 2, B, B), F32)
    rest_ref[...] = jnp.zeros_like(rest_ref)
    xh[...] = jnp.zeros_like(xh)
    xl[...] = jnp.zeros_like(xl)
    u_ref[...] = a_ref[0:B, 0:B] - dot3_t(
        vh[0:B, :HALF], vl[0:B, :HALF], lh[HALF : HALF + B, :HALF], ll[HALF : HALF + B, :HALF]
    )
    for copy in copies:
        copy.wait()

    def pair_inverse(i):
        t0h, t0l = split(t_ref[2 * i])
        t1h, t1l = split(t_ref[2 * i + 1])
        r1 = pl.ds(pl.multiple_of((2 * i + 1) * B, B), B)
        c0 = pl.ds(pl.multiple_of(2 * i * B, B), B)
        zh, zl = split(dot3_n(lh[r1, c0], ll[r1, c0], t0h, t0l))
        zh, zl = split(-dot3_n(t1h, t1l, zh, zl))
        zero = jnp.zeros((B, B), BF16)
        tph_ref[...] = cat_blocks(t0h, zero, zh, t1h)
        tpl_ref[...] = cat_blocks(t0l, zero, zl, t1l)

    def below_update(i):
        pc = pl.ds(pl.multiple_of(i * W2, W2), W2)
        u21[...] = a21[:, pc] - dot3_t(xh[...], xl[...], lh[pc, :], ll[pc, :])

    def below_settle(i):
        pc = pl.ds(pl.multiple_of(i * W2, W2), W2)
        uh, ul = split(u21[...])
        v = dot3_t(uh, ul, tph_ref[...], tpl_ref[...])
        x32[:, pc] = v
        xh[:, pc], xl[:, pc] = split(v)
        wh[:, pc], wl[:, pc] = split(v * dinv_ref[0:1, pc])

    def extra(k):
        i = k - NP // 2
        return [lambda: pair_inverse(i), lambda: below_update(i), lambda: below_settle(i)]

    factor_panels(NP // 2, NP, a_ref, b_half(b_ref), vh, vl, v32, lh, ll, t_ref, lt_ref, dinv_ref,
                  rest_ref, u_ref, part_ref, e_ref, extra)
    last = NP // 2 - 1
    pair_inverse(last)
    below_settle(last)

    y_late = v32[HALF : HALF + nrhs, HALF:]
    eli_ref[:, :HALF] = y0[...]
    eli_ref[:, HALF:PIV] = y_late
    mine = pl.ds(pl.multiple_of(jnp.maximum(me - NP, 0) * B, B), B)
    qh = jnp.concatenate([xh[mine, :], vh[HALF : HALF + nrhs, :]], 0)
    ql = jnp.concatenate([xl[mine, :], vl[HALF : HALF + nrhs, :]], 0)
    lower = me >= NP
    for c in range(low // W2):
        rows = slice(c * W2, (c + 1) * W2)
        dst = slice(PIV + c * W2, PIV + (c + 1) * W2)
        prod = dot3_t(qh, ql, wh[rows, :], wl[rows, :])
        row = me * B + lax.broadcasted_iota(jnp.int32, (B, W2), 0)
        col = PIV + c * W2 + lax.broadcasted_iota(jnp.int32, (B, W2), 1)
        fac_ref[:, dst] = jnp.where(row >= col, mine_ref[:, rows] - prod[:B], 0.0)
        eli_ref[:, dst] = b_ref[:, dst] - prod[B:]

    @pl.when(lower)
    def _():
        fac_ref[:, :PIV] = x32[mine, :] * dinv_ref[0:1, :]

    @pl.when(jnp.logical_not(lower))
    def _():
        fac_ref[:, :HALF] = own0[...]
        near = jnp.maximum(me - NP // 2, 0)
        rows = pl.ds(pl.multiple_of(near * B, B), B)
        col = HALF + lax.broadcasted_iota(jnp.int32, (B, HALF), 1)
        fac_ref[:, HALF:PIV] = jnp.where(col < me * B, v32[rows, HALF:] * dinv_ref[0:1, HALF:], 0.0)

    @pl.when((me >= NP // 2) & (me < NP))
    def _():
        fac_ref[:, pl.ds(pl.multiple_of(me * B, B), B)] = lt_ref[me].T


def b_half(b_ref):
    return b_ref.at[:, pl.ds(HALF, HALF)]


def second(index, near, far, parts, state, mine, rhs):
    nrhs, order = rhs.shape
    low = order - PIV
    na = PIV - HALF
    return pl.pallas_call(
        second_kernel,
        out_shape=(
            jax.ShapeDtypeStruct((B, order), F32),
            jax.ShapeDtypeStruct((nrhs, order), F32),
        ),
        in_specs=[pl.BlockSpec(memory_space=pltpu.SMEM)]
        + [VMEM_SPEC] * (len(parts) + len(state) + 4),
        out_specs=(VMEM_SPEC, VMEM_SPEC),
        scratch_shapes=[
            pltpu.VMEM((na, na), F32),
            pltpu.VMEM((low, PIV), F32),
            pltpu.VMEM((na + nrhs, PIV), BF16),
            pltpu.VMEM((na + nrhs, PIV), BF16),
            pltpu.VMEM((na + nrhs, PIV), F32),
            pltpu.VMEM((PIV, PIV), BF16),
            pltpu.VMEM((PIV, PIV), BF16),
            pltpu.VMEM((NP, B, B), F32),
            pltpu.VMEM((NP, B, B), F32),
            pltpu.VMEM((8, PIV), F32),
            pltpu.VMEM((na + nrhs, B), F32),
            pltpu.VMEM((B, B), F32),
            pltpu.VMEM((B, B), F32),
            pltpu.VMEM((B, B), F32),
            pltpu.VMEM((low, PIV), BF16),
            pltpu.VMEM((low, PIV), BF16),
            pltpu.VMEM((low, PIV), F32),
            pltpu.VMEM((low, PIV), BF16),
            pltpu.VMEM((low, PIV), BF16),
            pltpu.VMEM((low, W2), F32),
            pltpu.VMEM((W2, W2), BF16),
            pltpu.VMEM((W2, W2), BF16),
            pltpu.SemaphoreType.DMA((8,)),
        ],
        compiler_params=pltpu.CompilerParams(vmem_limit_bytes=36 * 1024 * 1024),
        name="second",
    )(index, near, far, *parts, *state, mine, rhs)


def shift_y(x, d, zs=(0, 1, 2, 3)):
    return lax.ppermute(x, "front", [(4 * z + y, 4 * z + (y + d) % 4) for z in zs for y in range(4)])


def planes(x, pairs):
    return lax.ppermute(x, "front", [(4 * a + y, 4 * b + y) for a, b in pairs for y in range(4)])


def gather_pivot_rows(x, z):
    swap = planes(x, ((0, 1), (1, 0)))
    side = planes(x, ((1, 2), (0, 3)))
    far = planes(x, ((0, 2), (1, 3)))
    x0 = jnp.where(z == 0, x, jnp.where(z == 1, swap, jnp.where(z == 2, far, side)))[:, :HALF]
    x1 = jnp.where(z == 0, swap, jnp.where(z == 1, x, jnp.where(z == 2, side, far)))
    rows = jnp.concatenate([x0, x1[:, :HALF], x1[:, HALF:]], 0)
    return [rows] + [shift_y(rows, d) for d in (1, 2, 3)]


def gather_lower_rows(x):
    near = jnp.concatenate([x] + [shift_y(x, d, (2, 3)) for d in (1, 2, 3)], 0)
    return near, planes(near, ((2, 3), (3, 2)))


def local(front_matrix, child_blocks, child_target, child_count, shot_rhs):
    leaves, slots = child_blocks.shape[1:3]
    slot_ids = lax.broadcasted_iota(jnp.int32, (leaves, slots), 1)
    live_code = jnp.where(slot_ids < child_count[0][:, None], child_target[0], -1)
    code_rows = jnp.zeros((leaves, 8, B), F32).at[:, 0, :slots].set(live_code.astype(F32))
    payload = jnp.concatenate([child_blocks[0].reshape(leaves, slots * B, B), code_rows], axis=1)
    arrived = lax.all_to_all(payload, "leaf", split_axis=0, concat_axis=0, tiled=True)
    codes = arrived[:, slots * B, :slots].astype(jnp.int32)
    index = lax.axis_index("front").astype(jnp.int32).reshape(1)
    late, pivots = assemble(codes, index, arrived, front_matrix[0])
    z = lax.axis_index("front") // 4
    near, far = gather_lower_rows(pivots)
    parts = gather_pivot_rows(pivots, z)
    rhs = shot_rhs[0]
    state = first(index, parts, rhs)
    factored, eliminated = second(index, near, far, parts, state, late, rhs)
    tail = eliminated[:, PIV:]
    tail = jnp.where(z < 2, planes(tail, ((2, 0), (3, 1))), tail)
    eliminated = jnp.concatenate([eliminated[:, :PIV], tail], 1)
    return factored[None], eliminated[None]


def solution(mesh):
    return jax.shard_map(
        local,
        mesh=mesh,
        in_specs=(
            P("leaf", "front", None),
            P(("leaf", "front"), None, None, None, None),
            P(("leaf", "front"), None, None),
            P(("leaf", "front"), None),
            P("leaf", None, None),
        ),
        out_specs=(P("leaf", "front", None), P("leaf", None, None)),
        check_vma=False,
    )
```

```python
import jax
import jax.numpy as jnp
from jax import lax
from jax.experimental import pallas as pl
from jax.experimental.pallas import tpu as pltpu
from jax.sharding import PartitionSpec as P

B = 128
PIV = 1024
NP = PIV // B
HALF = PIV // 2
W2 = 2 * B
F32 = jnp.float32
BF16 = jnp.bfloat16


def split(x):
    hi = x.astype(BF16)
    lo = (x - hi.astype(F32)).astype(BF16)
    return hi, lo


def dot_t(a, b):
    return lax.dot_general(a, b, (((1,), (1,)), ((), ())), preferred_element_type=F32)


def dot_n(a, b):
    return lax.dot_general(a, b, (((1,), (0,)), ((), ())), preferred_element_type=F32)


def dot3_t(ah, al, bh, bl):
    return dot_t(ah, bh) + dot_t(al, bh) + dot_t(ah, bl)


def dot3_n(ah, al, bh, bl):
    return dot_n(ah, bh) + dot_n(al, bh) + dot_n(ah, bl)


def assemble_kernel(code_ref, idx_ref, recv_ref, front_ref, tail_ref, early_ref, late_ref, out_ref):
    out_ref[...] = front_ref[...]
    for s in range(recv_ref.shape[0]):
        for j in range(code_ref.shape[1]):
            code = code_ref[s, j]

            @pl.when(code >= 0)
            def _(s=s, j=j, code=code):
                cols = pl.ds(pl.multiple_of(code * B, B), B)
                out_ref[:, cols] += recv_ref[s, j * B : (j + 1) * B, :]

    cols = pl.ds(pl.multiple_of(idx_ref[0] * B, B), B)
    square = out_ref[:, cols]
    row = lax.broadcasted_iota(jnp.int32, (B, B), 0)
    col = lax.broadcasted_iota(jnp.int32, (B, B), 1)
    out_ref[:, cols] = jnp.where(row >= col, square, square.T)
    early_ref[...] = out_ref[:, :HALF]
    late_ref[...] = out_ref[:, HALF:PIV]
    tail_ref[...] = out_ref[:, PIV:]


def assemble(codes, index, recv, front):
    rows, order = front.shape
    vmem = pl.BlockSpec(memory_space=pltpu.VMEM)
    return pl.pallas_call(
        assemble_kernel,
        out_shape=(
            jax.ShapeDtypeStruct((rows, order - PIV), F32),
            jax.ShapeDtypeStruct((rows, HALF), F32),
            jax.ShapeDtypeStruct((rows, HALF), F32),
        ),
        in_specs=[pl.BlockSpec(memory_space=pltpu.SMEM)] * 2 + [vmem, vmem],
        out_specs=(vmem, vmem, vmem),
        scratch_shapes=[pltpu.VMEM((rows, order), F32)],
        compiler_params=pltpu.CompilerParams(vmem_limit_bytes=8 * 1024 * 1024),
        name="assemble",
    )(codes, index, recv, front)


def lane(x, c):
    return jnp.broadcast_to(x[:, c : c + 1], (8, B))


def sublane(x, t):
    return jnp.broadcast_to(x[t : t + 1, :], (8, B))


def chain(a_rows, e_rows, store, side):
    sub = lax.broadcasted_iota(jnp.int32, (8, B), 0)
    ahead = None
    for g in range(16):
        if g < len(side):
            side[g]()
        ra, re = a_rows[g], e_rows[g]
        base = 8 * g
        b = ahead or [lane(ra, base + t) for t in range(8)]
        more, far = g < 15, g < 14
        if more:
            na, ne = a_rows[g + 1], e_rows[g + 1]
            c = [lane(na, base + t) for t in range(8)]
            q = [lane(ra, base + 8 + t) for t in range(8)]
            ahead = [lane(na, base + 8 + t) for t in range(8)]
        ga, ge = ra, re
        fa, fe = ra, re
        rcps = []
        for t in range(8):
            r = 1.0 / sublane(b[t], t)
            rcps.append(r)
            m = b[t] * r
            mg = jnp.where(sub == t, 0.0, m)
            mf = jnp.where(sub > t, m, 0.0)
            pa, pe = sublane(fa, t), sublane(fe, t)
            if more:
                mn = c[t] * r
            for u in range(t + 1, 8):
                w = sublane(b[u], t)
                b[u] = b[u] - mg * w
                if more:
                    c[u] = c[u] - mn * w
            if more:
                for u in range(8):
                    w = sublane(q[u], t)
                    q[u] = q[u] - mf * w
                    ahead[u] = ahead[u] - mn * w
                na = na - mn * pa
                ne = ne - mn * pe
            fa = fa - mf * pa
            fe = fe - mf * pe
            if far:
                ga = ga - mg * pa
                ge = ge - mg * pe
        rc = rcps[0]
        for t in range(1, 8):
            rc = jnp.where(sub == t, rcps[t], rc)
        store(g, fa, fe, rc)
        if more:
            a_rows[g + 1], e_rows[g + 1] = na, ne
        if far:
            ga = ga * rc
            ge = ge * rc
            gab = [sublane(ga, t) for t in range(8)]
            geb = [sublane(ge, t) for t in range(8)]
            for i in range(g + 2, 16):
                acc_a, acc_e = a_rows[i], e_rows[i]
                for t in range(8):
                    cc = lane(a_rows[i], base + t)
                    acc_a = acc_a - cc * gab[t]
                    acc_e = acc_e - cc * geb[t]
                a_rows[i], e_rows[i] = acc_a, acc_e


def cat_blocks(a, b, c, d):
    return jnp.concatenate([jnp.concatenate([a, b], 1), jnp.concatenate([c, d], 1)], 0)


def factor_panels(k0, k1, a_ref, b_ref, vh, vl, v32, lh, ll, t_ref, lt_ref, dinv_ref,
                  rest_ref, u_ref, part_ref, e_ref):
    row0 = k0 * B
    na, nrhs = a_ref.shape[0], b_ref.shape[0]
    ri = lax.broadcasted_iota(jnp.int32, (8, B), 0)
    ci = lax.broadcasted_iota(jnp.int32, (8, B), 1)

    def settle(k):
        cols = pl.ds(pl.multiple_of(k * B, B), B)
        th, tl = split(t_ref[k])
        uh, ul = split(rest_ref[...])
        v = dot3_t(uh, ul, th, tl)
        v32[:, cols] = v
        vh[:, cols], vl[:, cols] = split(v)
        lrows = slice(row0, row0 + na)
        lh[lrows, cols], ll[lrows, cols] = split(v[:na] * dinv_ref[0:1, cols])

    def panel(k, _):
        kcols = pl.ds(pl.multiple_of(k * B, B), B)
        acols = pl.ds(pl.multiple_of((k - k0) * B, B), B)
        prev = jnp.maximum(k - 1, k0)
        after = jnp.minimum(k + 1, k1 - 1)
        nabs = pl.ds(pl.multiple_of(after * B, B), B)
        nloc = pl.ds(pl.multiple_of((after - k0) * B, B), B)
        a_rows = [u_ref[8 * i : 8 * i + 8, :] for i in range(16)]
        e_rows = [jnp.where(ri + 8 * i == ci, 1.0, 0.0) for i in range(16)]
        diag = []

        def store(g, fa, fe, rc):
            own = ri + 8 * g == ci
            diag.append(jnp.where(own, fa, 0.0))
            lt_ref[k, 8 * g : 8 * g + 8, :] = jnp.where(own, fa, jnp.where(ri + 8 * g < ci, fa * rc, 0.0))
            e_ref[8 * g : 8 * g + 8, :] = fe

        def update():
            prod = dot3_t(vh[...], vl[...], lh[kcols, :], ll[kcols, :])
            rest_ref[:na, :] = a_ref[:, acols] - prod[:na]
            rest_ref[na:, :] = b_ref[:, acols] - prod[na:]

        def partial():
            part_ref[...] = a_ref[nloc, nloc] - dot3_t(vh[nloc, :], vl[nloc, :], lh[nabs, :], ll[nabs, :])

        side = [lambda: settle(prev), update, partial]
        chain(a_rows, e_rows, store, side)
        total = diag[0]
        for g in range(1, 16):
            total = total + diag[g]
        dinv = 1.0 / jnp.sum(total, axis=0, keepdims=True)
        dinv_ref[0:1, kcols] = dinv
        t = e_ref[...]
        t_ref[k] = t
        th, tl = split(t)
        uh, ul = split(rest_ref[nloc, :])
        v = dot3_t(uh, ul, th, tl)
        v_h, v_l = split(v)
        l_h, l_l = split(v * dinv)
        u_ref[...] = part_ref[...] - dot3_t(v_h, v_l, l_h, l_l)
        return 0

    lax.fori_loop(k0, k1, panel, 0)
    settle(k1 - 1)


def first_kernel(idx_ref, y0_ref, y1_ref, y2_ref, y3_ref, b_ref,
                 vh, vl, lh, ll, t_ref, dinv_ref, y_ref, own_ref,
                 a_ref, v32, lt_ref, rest_ref, u_ref, part_ref, e_ref):
    me = idx_ref[0]
    ypos = lax.rem(me, 4)
    for d, ref in enumerate((y0_ref, y1_ref, y2_ref, y3_ref)):
        src = lax.rem(ypos + 4 - d, 4)
        for z in range(2):
            rows = pl.ds(pl.multiple_of((4 * z + src) * B, B), B)
            a_ref[rows, :] = ref[z * B : (z + 1) * B, :]
    for ref in (vh, vl, lh, ll, rest_ref, dinv_ref):
        ref[...] = jnp.zeros_like(ref)
    t_ref[0] = jnp.zeros((B, B), F32)
    u_ref[...] = a_ref[0:B, 0:B]
    factor_panels(0, NP // 2, a_ref, b_ref.at[:, pl.ds(0, HALF)], vh, vl, v32, lh, ll, t_ref, lt_ref, dinv_ref,
                  rest_ref, u_ref, part_ref, e_ref)
    nrhs = b_ref.shape[0]
    y_ref[...] = v32[PIV : PIV + nrhs, :]
    near = jnp.minimum(me, NP - 1)
    rows = pl.ds(pl.multiple_of(near * B, B), B)
    col = lax.broadcasted_iota(jnp.int32, (B, HALF), 1)
    own_ref[...] = jnp.where(col < near * B, v32[rows, :] * dinv_ref[0:1, :], 0.0)

    @pl.when(me < NP // 2)
    def _():
        own_ref[:, rows] = lt_ref[me].T


VMEM_SPEC = pl.BlockSpec(memory_space=pltpu.VMEM)


def first(index, parts, rhs):
    nrhs = rhs.shape[0]
    outs = (
        ((PIV + nrhs, HALF), BF16),
        ((PIV + nrhs, HALF), BF16),
        ((PIV, HALF), BF16),
        ((PIV, HALF), BF16),
        ((NP // 2, B, B), F32),
        ((8, HALF), F32),
        ((nrhs, HALF), F32),
        ((B, HALF), F32),
    )
    return pl.pallas_call(
        first_kernel,
        out_shape=tuple(jax.ShapeDtypeStruct(*o) for o in outs),
        in_specs=[pl.BlockSpec(memory_space=pltpu.SMEM)] + [VMEM_SPEC] * 5,
        out_specs=(VMEM_SPEC,) * len(outs),
        scratch_shapes=[
            pltpu.VMEM((PIV, HALF), F32),
            pltpu.VMEM((PIV + nrhs, HALF), F32),
            pltpu.VMEM((NP // 2, B, B), F32),
            pltpu.VMEM((PIV + nrhs, B), F32),
            pltpu.VMEM((B, B), F32),
            pltpu.VMEM((B, B), F32),
            pltpu.VMEM((B, B), F32),
        ],
        compiler_params=pltpu.CompilerParams(vmem_limit_bytes=20 * 1024 * 1024),
        cost_estimate=pl.CostEstimate(flops=2 * 10**10, bytes_accessed=2 * 10**7, transcendentals=0),
        name="first",
    )(index, *parts, rhs)


def second_kernel(idx_ref, p0_ref, p1_ref, p2_ref, p3_ref, vh0, vl0, lh0, ll0, t0, dinv0, y0, own0, b_ref,
                  lh, ll, t_ref, dinv_ref, y_ref, own_ref,
                  a_ref, vh, vl, v32, lt_ref, rest_ref, u_ref, part_ref, e_ref):
    me = idx_ref[0]
    nrhs = b_ref.shape[0]
    ypos = lax.rem(me, 4)
    for d, ref in enumerate((p0_ref, p1_ref, p2_ref, p3_ref)):
        rows = pl.ds(pl.multiple_of(lax.rem(ypos + 4 - d, 4) * B, B), B)
        a_ref[rows, :] = ref[...]
    for ref, src in ((vh, vh0), (vl, vl0)):
        ref[:, :HALF] = src[HALF:, :]
        ref[:, HALF:] = jnp.zeros((ref.shape[0], HALF), BF16)
    for ref, src in ((lh, lh0), (ll, ll0)):
        ref[:, :HALF] = src[...]
        ref[:, HALF:] = jnp.zeros((ref.shape[0], HALF), BF16)
    dinv_ref[:, :HALF] = dinv0[...]
    dinv_ref[:, HALF:] = jnp.zeros((dinv_ref.shape[0], HALF), F32)
    t_ref[: NP // 2] = t0[...]
    t_ref[NP // 2] = jnp.zeros((B, B), F32)
    rest_ref[...] = jnp.zeros_like(rest_ref)
    u_ref[...] = a_ref[0:B, 0:B] - dot3_t(
        vh[0:B, :HALF], vl[0:B, :HALF], lh[HALF : HALF + B, :HALF], ll[HALF : HALF + B, :HALF]
    )
    factor_panels(NP // 2, NP, a_ref, b_ref.at[:, pl.ds(HALF, HALF)], vh, vl, v32, lh, ll, t_ref, lt_ref,
                  dinv_ref, rest_ref, u_ref, part_ref, e_ref)
    y_ref[:, :HALF] = y0[...]
    y_ref[:, HALF:] = v32[HALF : HALF + nrhs, HALF:]
    own_ref[:, :HALF] = own0[...]
    near = jnp.clip(me - NP // 2, 0, NP // 2 - 1)
    rows = pl.ds(pl.multiple_of(near * B, B), B)
    col = HALF + lax.broadcasted_iota(jnp.int32, (B, HALF), 1)
    own_ref[:, HALF:] = jnp.where(col < me * B, v32[rows, HALF:] * dinv_ref[0:1, HALF:], 0.0)

    @pl.when((me >= NP // 2) & (me < NP))
    def _():
        own_ref[:, pl.ds(pl.multiple_of(me * B, B), B)] = lt_ref[me].T


def second(index, parts, state, rhs):
    nrhs = rhs.shape[0]
    na = PIV - HALF
    outs = (
        ((PIV, PIV), BF16),
        ((PIV, PIV), BF16),
        ((NP, B, B), F32),
        ((8, PIV), F32),
        ((nrhs, PIV), F32),
        ((B, PIV), F32),
    )
    return pl.pallas_call(
        second_kernel,
        out_shape=tuple(jax.ShapeDtypeStruct(*o) for o in outs),
        in_specs=[pl.BlockSpec(memory_space=pltpu.SMEM)] + [VMEM_SPEC] * (len(parts) + len(state) + 1),
        out_specs=(VMEM_SPEC,) * len(outs),
        scratch_shapes=[
            pltpu.VMEM((na, na), F32),
            pltpu.VMEM((na + nrhs, PIV), BF16),
            pltpu.VMEM((na + nrhs, PIV), BF16),
            pltpu.VMEM((na + nrhs, PIV), F32),
            pltpu.VMEM((NP, B, B), F32),
            pltpu.VMEM((na + nrhs, B), F32),
            pltpu.VMEM((B, B), F32),
            pltpu.VMEM((B, B), F32),
            pltpu.VMEM((B, B), F32),
        ],
        compiler_params=pltpu.CompilerParams(vmem_limit_bytes=20 * 1024 * 1024),
        cost_estimate=pl.CostEstimate(flops=2 * 10**10, bytes_accessed=2 * 10**7, transcendentals=0),
        name="second",
    )(index, *parts, *state, rhs)


def third_kernel(idx_ref, h0, h1, h2, h3, near_ref, far_ref, lh, ll, t_ref, dinv_ref, y_ref, own_ref, tail_ref, b_ref,
                 fac_ref, eli_ref, a21, xh, xl, x32, wh, wl, sem):
    me = idx_ref[0]
    nrhs, order = b_ref.shape
    low = order - PIV
    ypos, zpos = lax.rem(me, 4), jnp.clip(me // 4 - 2, 0, 1)
    copies = []
    for d, ref in enumerate((h0, h1, h2, h3)):
        spot = lax.rem(ypos + 4 - d, 4)
        for n, z in enumerate((zpos, 1 - zpos)):
            rows = pl.ds(pl.multiple_of((4 * z + spot) * B, B), B)
            src = (near_ref, far_ref)[n]
            copies.append(pltpu.make_async_copy(
                ref.at[pl.ds(n * B, B), :], a21.at[rows, pl.ds(0, HALF)], sem.at[2 * d + n]))
            copies.append(pltpu.make_async_copy(
                src.at[pl.ds(d * B, B), :], a21.at[rows, pl.ds(HALF, HALF)], sem.at[8 + 2 * d + n]))
    for copy in copies:
        copy.start()

    inverses = []
    for i in range(NP // 2):
        t0h, t0l = split(t_ref[2 * i])
        t1h, t1l = split(t_ref[2 * i + 1])
        r1 = slice((2 * i + 1) * B, (2 * i + 2) * B)
        c0 = slice(2 * i * B, (2 * i + 1) * B)
        zh, zl = split(dot3_n(lh[r1, c0], ll[r1, c0], t0h, t0l))
        zh, zl = split(-dot3_n(t1h, t1l, zh, zl))
        zero = jnp.zeros((B, B), BF16)
        inverses.append((cat_blocks(t0h, zero, zh, t1h), cat_blocks(t0l, zero, zl, t1l)))
    for copy in copies:
        copy.wait()
    for i in range(NP // 2):
        pc, prev = slice(i * W2, (i + 1) * W2), slice(0, i * W2)
        u = a21[:, pc]
        if i:
            u = u - dot3_t(xh[:, prev], xl[:, prev], lh[pc, prev], ll[pc, prev])
        uh, ul = split(u)
        v = dot3_t(uh, ul, *inverses[i])
        x32[:, pc] = v
        xh[:, pc], xl[:, pc] = split(v)
        wh[:, pc], wl[:, pc] = split(v * dinv_ref[0:1, pc])

    y = y_ref[...]
    yh, yl = split(y)
    eli_ref[:, :PIV] = y
    mine = pl.ds(pl.multiple_of(jnp.maximum(me - NP, 0) * B, B), B)
    qh = jnp.concatenate([xh[mine, :], yh], 0)
    ql = jnp.concatenate([xl[mine, :], yl], 0)
    for c in range(low // W2):
        rows = slice(c * W2, (c + 1) * W2)
        dst = slice(PIV + c * W2, PIV + (c + 1) * W2)
        prod = dot3_t(qh, ql, wh[rows, :], wl[rows, :])
        row = me * B + lax.broadcasted_iota(jnp.int32, (B, W2), 0)
        col = PIV + c * W2 + lax.broadcasted_iota(jnp.int32, (B, W2), 1)
        fac_ref[:, dst] = jnp.where(row >= col, tail_ref[:, rows] - prod[:B], 0.0)
        eli_ref[:, dst] = b_ref[:, dst] - prod[B:]
    lower = me >= NP

    @pl.when(lower)
    def _():
        fac_ref[:, :PIV] = x32[mine, :] * dinv_ref[0:1, :]

    @pl.when(jnp.logical_not(lower))
    def _():
        fac_ref[:, :PIV] = own_ref[...]


def third(index, lower, state, tail, rhs):
    nrhs, order = rhs.shape
    low = order - PIV
    return pl.pallas_call(
        third_kernel,
        out_shape=(
            jax.ShapeDtypeStruct((B, order), F32),
            jax.ShapeDtypeStruct((nrhs, order), F32),
        ),
        in_specs=[pl.BlockSpec(memory_space=pltpu.SMEM)] + [VMEM_SPEC] * (len(lower) + len(state) + 2),
        out_specs=(VMEM_SPEC, VMEM_SPEC),
        scratch_shapes=[
            pltpu.VMEM((low, PIV), F32),
            pltpu.VMEM((low, PIV), BF16),
            pltpu.VMEM((low, PIV), BF16),
            pltpu.VMEM((low, PIV), F32),
            pltpu.VMEM((low, PIV), BF16),
            pltpu.VMEM((low, PIV), BF16),
            pltpu.SemaphoreType.DMA((16,)),
        ],
        compiler_params=pltpu.CompilerParams(vmem_limit_bytes=34 * 1024 * 1024),
        name="third",
    )(index, *lower, *state, tail, rhs)


def shift_y(x, d, zs=(0, 1, 2, 3)):
    return lax.ppermute(x, "front", [(4 * z + y, 4 * z + (y + d) % 4) for z in zs for y in range(4)])


def planes(x, pairs):
    return lax.ppermute(x, "front", [(4 * a + y, 4 * b + y) for a, b in pairs for y in range(4)])


def pick(z, *values):
    return jnp.where(z == 0, values[0], jnp.where(z == 1, values[1], jnp.where(z == 2, values[2], values[3])))


def ring_y(x, zs=(0, 1, 2, 3)):
    return [x] + [shift_y(x, d, zs) for d in (1, 2, 3)]


def local(front_matrix, child_blocks, child_target, child_count, shot_rhs):
    leaves, slots = child_blocks.shape[1:3]
    slot_ids = lax.broadcasted_iota(jnp.int32, (leaves, slots), 1)
    live_code = jnp.where(slot_ids < child_count[0][:, None], child_target[0], -1)
    code_rows = jnp.zeros((leaves, 8, B), F32).at[:, 0, :slots].set(live_code.astype(F32))
    payload = jnp.concatenate([child_blocks[0].reshape(leaves, slots * B, B), code_rows], axis=1)
    arrived = lax.all_to_all(payload, "leaf", split_axis=0, concat_axis=0, tiled=True)
    codes = arrived[:, slots * B, :slots].astype(jnp.int32)
    index = lax.axis_index("front").astype(jnp.int32).reshape(1)
    tail, early, late = assemble(codes, index, arrived, front_matrix[0])
    z = lax.axis_index("front") // 4
    rhs = shot_rhs[0]
    swap = planes(early, ((0, 1), (1, 0), (2, 3), (3, 2)))
    side = planes(early, ((1, 2), (0, 3)))
    cross = planes(early, ((0, 2), (1, 3)))
    near = jnp.concatenate(ring_y(late, (2, 3)), 0)
    early_parts = ring_y(jnp.concatenate([pick(z, early, swap, cross, side), pick(z, swap, early, side, cross)], 0))
    late_x, _ = lax.optimization_barrier((late, (swap, side, cross)))
    to0, to2, to3 = (planes(late_x, ((1, d),)) for d in (0, 2, 3))
    late_parts = ring_y(pick(z, to0, late_x, to2, to3))
    far = planes(near, ((2, 3), (3, 2)))
    state = first(index, early_parts, rhs)
    pair, _ = lax.optimization_barrier((jnp.concatenate([early, swap], 0), state[6]))
    below = ring_y(pair, (2, 3))
    state = second(index, late_parts, state, rhs)
    factored, eliminated = third(index, below + [near, far], state, tail, rhs)
    tail = eliminated[:, PIV:]
    tail = jnp.where(z < 2, planes(tail, ((2, 0), (3, 1))), tail)
    eliminated = jnp.concatenate([eliminated[:, :PIV], tail], 1)
    return factored[None], eliminated[None]


def solution(mesh):
    return jax.shard_map(
        local,
        mesh=mesh,
        in_specs=(
            P("leaf", "front", None),
            P(("leaf", "front"), None, None, None, None),
            P(("leaf", "front"), None, None),
            P(("leaf", "front"), None),
            P("leaf", None, None),
        ),
        out_specs=(P("leaf", "front", None), P("leaf", None, None)),
        check_vma=False,
    )
```

```python
import jax
import jax.numpy as jnp
from jax import lax
from jax.experimental import pallas as pl
from jax.experimental.pallas import tpu as pltpu
from jax.sharding import PartitionSpec as P

B = 128
PIV = 1024
NP = PIV // B
HALF = PIV // 2
W2 = 2 * B
F32 = jnp.float32
BF16 = jnp.bfloat16


def split(x):
    hi = x.astype(BF16)
    lo = (x - hi.astype(F32)).astype(BF16)
    return hi, lo


def dot_t(a, b):
    return lax.dot_general(a, b, (((1,), (1,)), ((), ())), preferred_element_type=F32)


def dot_n(a, b):
    return lax.dot_general(a, b, (((1,), (0,)), ((), ())), preferred_element_type=F32)


def dot3_t(ah, al, bh, bl):
    return dot_t(ah, bh) + dot_t(al, bh) + dot_t(ah, bl)


def dot3_n(ah, al, bh, bl):
    return dot_n(ah, bh) + dot_n(al, bh) + dot_n(ah, bl)


def assemble_kernel(code_ref, idx_ref, recv_ref, front_ref, tail_ref, early_ref, late_ref, out_ref):
    out_ref[...] = front_ref[...]
    for s in range(recv_ref.shape[0]):
        for j in range(code_ref.shape[1]):
            code = code_ref[s, j]

            @pl.when(code >= 0)
            def _(s=s, j=j, code=code):
                cols = pl.ds(pl.multiple_of(code * B, B), B)
                out_ref[:, cols] += recv_ref[s, j * B : (j + 1) * B, :]

    cols = pl.ds(pl.multiple_of(idx_ref[0] * B, B), B)
    square = out_ref[:, cols]
    row = lax.broadcasted_iota(jnp.int32, (B, B), 0)
    col = lax.broadcasted_iota(jnp.int32, (B, B), 1)
    out_ref[:, cols] = jnp.where(row >= col, square, square.T)
    early_ref[...] = out_ref[:, :HALF]
    late_ref[...] = out_ref[:, HALF:PIV]
    tail_ref[...] = out_ref[:, PIV:]


def assemble(codes, index, recv, front):
    rows, order = front.shape
    vmem = pl.BlockSpec(memory_space=pltpu.VMEM)
    return pl.pallas_call(
        assemble_kernel,
        out_shape=(
            jax.ShapeDtypeStruct((rows, order - PIV), F32),
            jax.ShapeDtypeStruct((rows, HALF), F32),
            jax.ShapeDtypeStruct((rows, HALF), F32),
        ),
        in_specs=[pl.BlockSpec(memory_space=pltpu.SMEM)] * 2 + [vmem, vmem],
        out_specs=(vmem, vmem, vmem),
        scratch_shapes=[pltpu.VMEM((rows, order), F32)],
        compiler_params=pltpu.CompilerParams(vmem_limit_bytes=8 * 1024 * 1024),
        name="assemble",
    )(codes, index, recv, front)


def lane(x, c):
    return jnp.broadcast_to(x[:, c : c + 1], (8, B))


def sublane(x, t):
    return jnp.broadcast_to(x[t : t + 1, :], (8, B))


def chain(a_rows, e_rows, store, side):
    sub = lax.broadcasted_iota(jnp.int32, (8, B), 0)
    ahead = None
    for g in range(16):
        if g < len(side):
            side[g]()
        ra, re = a_rows[g], e_rows[g]
        base = 8 * g
        b = ahead or [lane(ra, base + t) for t in range(8)]
        more, far = g < 15, g < 14
        if more:
            na, ne = a_rows[g + 1], e_rows[g + 1]
            c = [lane(na, base + t) for t in range(8)]
            q = [lane(ra, base + 8 + t) for t in range(8)]
            ahead = [lane(na, base + 8 + t) for t in range(8)]
        ga, ge = ra, re
        fa, fe = ra, re
        rcps = []
        for t in range(8):
            r = 1.0 / sublane(b[t], t)
            rcps.append(r)
            m = b[t] * r
            mg = jnp.where(sub == t, 0.0, m)
            mf = jnp.where(sub > t, m, 0.0)
            pa, pe = sublane(fa, t), sublane(fe, t)
            if more:
                mn = c[t] * r
            for u in range(t + 1, 8):
                w = sublane(b[u], t)
                b[u] = b[u] - mg * w
                if more:
                    c[u] = c[u] - mn * w
            if more:
                for u in range(8):
                    w = sublane(q[u], t)
                    q[u] = q[u] - mf * w
                    ahead[u] = ahead[u] - mn * w
                na = na - mn * pa
                ne = ne - mn * pe
            fa = fa - mf * pa
            fe = fe - mf * pe
            if far:
                ga = ga - mg * pa
                ge = ge - mg * pe
        rc = rcps[0]
        for t in range(1, 8):
            rc = jnp.where(sub == t, rcps[t], rc)
        store(g, fa, fe, rc)
        if more:
            a_rows[g + 1], e_rows[g + 1] = na, ne
        if far:
            ga = ga * rc
            ge = ge * rc
            gab = [sublane(ga, t) for t in range(8)]
            geb = [sublane(ge, t) for t in range(8)]
            for i in range(g + 2, 16):
                acc_a, acc_e = a_rows[i], e_rows[i]
                for t in range(8):
                    cc = lane(a_rows[i], base + t)
                    acc_a = acc_a - cc * gab[t]
                    acc_e = acc_e - cc * geb[t]
                a_rows[i], e_rows[i] = acc_a, acc_e


def cat_blocks(a, b, c, d):
    return jnp.concatenate([jnp.concatenate([a, b], 1), jnp.concatenate([c, d], 1)], 0)


def factor_panels(k0, k1, a_ref, b_ref, vh, vl, v32, lh, ll, t_ref, lt_ref, dinv_ref,
                  rest_ref, u_ref, part_ref, e_ref):
    row0 = k0 * B
    na, nrhs = a_ref.shape[0], b_ref.shape[0]
    ri = lax.broadcasted_iota(jnp.int32, (8, B), 0)
    ci = lax.broadcasted_iota(jnp.int32, (8, B), 1)

    def settle(k):
        cols = pl.ds(pl.multiple_of(k * B, B), B)
        th, tl = split(t_ref[k])
        uh, ul = split(rest_ref[...])
        v = dot3_t(uh, ul, th, tl)
        v32[:, cols] = v
        vh[:, cols], vl[:, cols] = split(v)
        lrows = slice(row0, row0 + na)
        lh[lrows, cols], ll[lrows, cols] = split(v[:na] * dinv_ref[0:1, cols])

    def panel(k, _):
        kcols = pl.ds(pl.multiple_of(k * B, B), B)
        acols = pl.ds(pl.multiple_of((k - k0) * B, B), B)
        prev = jnp.maximum(k - 1, k0)
        after = jnp.minimum(k + 1, k1 - 1)
        nabs = pl.ds(pl.multiple_of(after * B, B), B)
        nloc = pl.ds(pl.multiple_of((after - k0) * B, B), B)
        a_rows = [u_ref[8 * i : 8 * i + 8, :] for i in range(16)]
        e_rows = [jnp.where(ri + 8 * i == ci, 1.0, 0.0) for i in range(16)]
        diag = []

        def store(g, fa, fe, rc):
            own = ri + 8 * g == ci
            diag.append(jnp.where(own, fa, 0.0))
            lt_ref[k, 8 * g : 8 * g + 8, :] = jnp.where(own, fa, jnp.where(ri + 8 * g < ci, fa * rc, 0.0))
            e_ref[8 * g : 8 * g + 8, :] = fe

        def update():
            prod = dot3_t(vh[...], vl[...], lh[kcols, :], ll[kcols, :])
            rest_ref[:na, :] = a_ref[:, acols] - prod[:na]
            rest_ref[na:, :] = b_ref[:, acols] - prod[na:]

        def partial():
            part_ref[...] = a_ref[nloc, nloc] - dot3_t(vh[nloc, :], vl[nloc, :], lh[nabs, :], ll[nabs, :])

        side = [lambda: settle(prev), update, partial]
        chain(a_rows, e_rows, store, side)
        total = diag[0]
        for g in range(1, 16):
            total = total + diag[g]
        dinv = 1.0 / jnp.sum(total, axis=0, keepdims=True)
        dinv_ref[0:1, kcols] = dinv
        t = e_ref[...]
        t_ref[k] = t
        th, tl = split(t)
        uh, ul = split(rest_ref[nloc, :])
        v = dot3_t(uh, ul, th, tl)
        v_h, v_l = split(v)
        l_h, l_l = split(v * dinv)
        u_ref[...] = part_ref[...] - dot3_t(v_h, v_l, l_h, l_l)
        return 0

    lax.fori_loop(k0, k1, panel, 0)
    settle(k1 - 1)


def first_kernel(idx_ref, y0_ref, y1_ref, y2_ref, y3_ref, b_ref,
                 vh, vl, lh, ll, t_ref, dinv_ref, y_ref, own_ref,
                 a_ref, v32, lt_ref, rest_ref, u_ref, part_ref, e_ref):
    me = idx_ref[0]
    ypos = lax.rem(me, 4)
    for d, ref in enumerate((y0_ref, y1_ref, y2_ref, y3_ref)):
        src = lax.rem(ypos + 4 - d, 4)
        for z in range(2):
            rows = pl.ds(pl.multiple_of((4 * z + src) * B, B), B)
            a_ref[rows, :] = ref[z * B : (z + 1) * B, :]
    for ref in (vh, vl, lh, ll, rest_ref, dinv_ref):
        ref[...] = jnp.zeros_like(ref)
    t_ref[0] = jnp.zeros((B, B), F32)
    u_ref[...] = a_ref[0:B, 0:B]
    factor_panels(0, NP // 2, a_ref, b_ref.at[:, pl.ds(0, HALF)], vh, vl, v32, lh, ll, t_ref, lt_ref, dinv_ref,
                  rest_ref, u_ref, part_ref, e_ref)
    nrhs = b_ref.shape[0]
    y_ref[...] = v32[PIV : PIV + nrhs, :]
    near = jnp.minimum(me, NP - 1)
    rows = pl.ds(pl.multiple_of(near * B, B), B)
    col = lax.broadcasted_iota(jnp.int32, (B, HALF), 1)
    own_ref[...] = jnp.where(col < near * B, v32[rows, :] * dinv_ref[0:1, :], 0.0)

    @pl.when(me < NP // 2)
    def _():
        own_ref[:, rows] = lt_ref[me].T


VMEM_SPEC = pl.BlockSpec(memory_space=pltpu.VMEM)


def first(index, parts, rhs):
    nrhs = rhs.shape[0]
    outs = (
        ((PIV + nrhs, HALF), BF16),
        ((PIV + nrhs, HALF), BF16),
        ((PIV, HALF), BF16),
        ((PIV, HALF), BF16),
        ((NP // 2, B, B), F32),
        ((8, HALF), F32),
        ((nrhs, HALF), F32),
        ((B, HALF), F32),
    )
    return pl.pallas_call(
        first_kernel,
        out_shape=tuple(jax.ShapeDtypeStruct(*o) for o in outs),
        in_specs=[pl.BlockSpec(memory_space=pltpu.SMEM)] + [VMEM_SPEC] * 5,
        out_specs=(VMEM_SPEC,) * len(outs),
        scratch_shapes=[
            pltpu.VMEM((PIV, HALF), F32),
            pltpu.VMEM((PIV + nrhs, HALF), F32),
            pltpu.VMEM((NP // 2, B, B), F32),
            pltpu.VMEM((PIV + nrhs, B), F32),
            pltpu.VMEM((B, B), F32),
            pltpu.VMEM((B, B), F32),
            pltpu.VMEM((B, B), F32),
        ],
        compiler_params=pltpu.CompilerParams(vmem_limit_bytes=20 * 1024 * 1024),
        cost_estimate=pl.CostEstimate(flops=2 * 10**10, bytes_accessed=2 * 10**7, transcendentals=0),
        name="first",
    )(index, *parts, rhs)


def second_kernel(idx_ref, p0_ref, p1_ref, p2_ref, p3_ref, vh0, vl0, lh0, ll0, t0, dinv0, y0, own0, b_ref,
                  lh, ll, t_ref, dinv_ref, y_ref, own_ref,
                  a_ref, vh, vl, v32, lt_ref, rest_ref, u_ref, part_ref, e_ref):
    me = idx_ref[0]
    nrhs = b_ref.shape[0]
    ypos = lax.rem(me, 4)
    for d, ref in enumerate((p0_ref, p1_ref, p2_ref, p3_ref)):
        rows = pl.ds(pl.multiple_of(lax.rem(ypos + 4 - d, 4) * B, B), B)
        a_ref[rows, :] = ref[:B, :]
    for ref, src in ((vh, vh0), (vl, vl0)):
        ref[:, :HALF] = src[HALF:, :]
        ref[:, HALF:] = jnp.zeros((ref.shape[0], HALF), BF16)
    for ref, src in ((lh, lh0), (ll, ll0)):
        ref[:, :HALF] = src[...]
        ref[:, HALF:] = jnp.zeros((ref.shape[0], HALF), BF16)
    dinv_ref[:, :HALF] = dinv0[...]
    dinv_ref[:, HALF:] = jnp.zeros((dinv_ref.shape[0], HALF), F32)
    t_ref[: NP // 2] = t0[...]
    t_ref[NP // 2] = jnp.zeros((B, B), F32)
    rest_ref[...] = jnp.zeros_like(rest_ref)
    u_ref[...] = a_ref[0:B, 0:B] - dot3_t(
        vh[0:B, :HALF], vl[0:B, :HALF], lh[HALF : HALF + B, :HALF], ll[HALF : HALF + B, :HALF]
    )
    factor_panels(NP // 2, NP, a_ref, b_ref.at[:, pl.ds(HALF, HALF)], vh, vl, v32, lh, ll, t_ref, lt_ref,
                  dinv_ref, rest_ref, u_ref, part_ref, e_ref)
    y_ref[:, :HALF] = y0[...]
    y_ref[:, HALF:] = v32[HALF : HALF + nrhs, HALF:]
    own_ref[:, :HALF] = own0[...]
    near = jnp.clip(me - NP // 2, 0, NP // 2 - 1)
    rows = pl.ds(pl.multiple_of(near * B, B), B)
    col = HALF + lax.broadcasted_iota(jnp.int32, (B, HALF), 1)
    own_ref[:, HALF:] = jnp.where(col < me * B, v32[rows, HALF:] * dinv_ref[0:1, HALF:], 0.0)

    @pl.when((me >= NP // 2) & (me < NP))
    def _():
        own_ref[:, pl.ds(pl.multiple_of(me * B, B), B)] = lt_ref[me].T


def second(index, parts, state, rhs):
    nrhs = rhs.shape[0]
    na = PIV - HALF
    outs = (
        ((PIV, PIV), BF16),
        ((PIV, PIV), BF16),
        ((NP, B, B), F32),
        ((8, PIV), F32),
        ((nrhs, PIV), F32),
        ((B, PIV), F32),
    )
    return pl.pallas_call(
        second_kernel,
        out_shape=tuple(jax.ShapeDtypeStruct(*o) for o in outs),
        in_specs=[pl.BlockSpec(memory_space=pltpu.SMEM)] + [VMEM_SPEC] * (len(parts) + len(state) + 1),
        out_specs=(VMEM_SPEC,) * len(outs),
        scratch_shapes=[
            pltpu.VMEM((na, na), F32),
            pltpu.VMEM((na + nrhs, PIV), BF16),
            pltpu.VMEM((na + nrhs, PIV), BF16),
            pltpu.VMEM((na + nrhs, PIV), F32),
            pltpu.VMEM((NP, B, B), F32),
            pltpu.VMEM((na + nrhs, B), F32),
            pltpu.VMEM((B, B), F32),
            pltpu.VMEM((B, B), F32),
            pltpu.VMEM((B, B), F32),
        ],
        compiler_params=pltpu.CompilerParams(vmem_limit_bytes=20 * 1024 * 1024),
        cost_estimate=pl.CostEstimate(flops=2 * 10**10, bytes_accessed=2 * 10**7, transcendentals=0),
        name="second",
    )(index, *parts, *state, rhs)


def third_kernel(idx_ref, nf_ref, nl_ref, ff_ref, fl_ref, lh, ll, t_ref, dinv_ref, y_ref, own_ref, tail_ref, b_ref,
                 fac_ref, eli_ref, a21, xh, xl, x32, wh, wl, sem):
    me = idx_ref[0]
    nrhs, order = b_ref.shape
    low = order - PIV
    ypos, zpos = lax.rem(me, 4), jnp.clip(me // 4 - 2, 0, 1)
    copies = []
    for n, (ref, z, c) in enumerate(((nf_ref, zpos, 0), (ff_ref, 1 - zpos, 0), (nl_ref, zpos, HALF), (fl_ref, 1 - zpos, HALF))):
        for d in range(4):
            rows = pl.ds(pl.multiple_of((4 * z + lax.rem(ypos + 4 - d, 4)) * B, B), B)
            copies.append(pltpu.make_async_copy(
                ref.at[pl.ds(d * B, B), :], a21.at[rows, pl.ds(c, HALF)], sem.at[4 * n + d]))
    for copy in copies:
        copy.start()

    inverses = []
    for i in range(NP // 2):
        t0h, t0l = split(t_ref[2 * i])
        t1h, t1l = split(t_ref[2 * i + 1])
        r1 = slice((2 * i + 1) * B, (2 * i + 2) * B)
        c0 = slice(2 * i * B, (2 * i + 1) * B)
        zh, zl = split(dot3_n(lh[r1, c0], ll[r1, c0], t0h, t0l))
        zh, zl = split(-dot3_n(t1h, t1l, zh, zl))
        zero = jnp.zeros((B, B), BF16)
        inverses.append((cat_blocks(t0h, zero, zh, t1h), cat_blocks(t0l, zero, zl, t1l)))
    for copy in copies:
        copy.wait()
    for i in range(NP // 2):
        pc, prev = slice(i * W2, (i + 1) * W2), slice(0, i * W2)
        u = a21[:, pc]
        if i:
            u = u - dot3_t(xh[:, prev], xl[:, prev], lh[pc, prev], ll[pc, prev])
        uh, ul = split(u)
        v = dot3_t(uh, ul, *inverses[i])
        x32[:, pc] = v
        xh[:, pc], xl[:, pc] = split(v)
        wh[:, pc], wl[:, pc] = split(v * dinv_ref[0:1, pc])

    y = y_ref[...]
    yh, yl = split(y)
    eli_ref[:, :PIV] = y
    mine = pl.ds(pl.multiple_of(jnp.maximum(me - NP, 0) * B, B), B)
    qh = jnp.concatenate([xh[mine, :], yh], 0)
    ql = jnp.concatenate([xl[mine, :], yl], 0)
    for c in range(low // W2):
        rows = slice(c * W2, (c + 1) * W2)
        dst = slice(PIV + c * W2, PIV + (c + 1) * W2)
        prod = dot3_t(qh, ql, wh[rows, :], wl[rows, :])
        row = me * B + lax.broadcasted_iota(jnp.int32, (B, W2), 0)
        col = PIV + c * W2 + lax.broadcasted_iota(jnp.int32, (B, W2), 1)
        fac_ref[:, dst] = jnp.where(row >= col, tail_ref[:, rows] - prod[:B], 0.0)
        eli_ref[:, dst] = b_ref[:, dst] - prod[B:]
    lower = me >= NP

    @pl.when(lower)
    def _():
        fac_ref[:, :PIV] = x32[mine, :] * dinv_ref[0:1, :]

    @pl.when(jnp.logical_not(lower))
    def _():
        fac_ref[:, :PIV] = own_ref[...]


def third(index, lower, state, tail, rhs):
    nrhs, order = rhs.shape
    low = order - PIV
    return pl.pallas_call(
        third_kernel,
        out_shape=(
            jax.ShapeDtypeStruct((B, order), F32),
            jax.ShapeDtypeStruct((nrhs, order), F32),
        ),
        in_specs=[pl.BlockSpec(memory_space=pltpu.SMEM)] + [VMEM_SPEC] * (len(lower) + len(state) + 2),
        out_specs=(VMEM_SPEC, VMEM_SPEC),
        scratch_shapes=[
            pltpu.VMEM((low, PIV), F32),
            pltpu.VMEM((low, PIV), BF16),
            pltpu.VMEM((low, PIV), BF16),
            pltpu.VMEM((low, PIV), F32),
            pltpu.VMEM((low, PIV), BF16),
            pltpu.VMEM((low, PIV), BF16),
            pltpu.SemaphoreType.DMA((16,)),
        ],
        compiler_params=pltpu.CompilerParams(vmem_limit_bytes=34 * 1024 * 1024),
        name="third",
    )(index, *lower, *state, tail, rhs)


def shift_y(x, d, zs=(0, 1, 2, 3)):
    return lax.ppermute(x, "front", [(4 * z + y, 4 * z + (y + d) % 4) for z in zs for y in range(4)])


def planes(x, pairs):
    return lax.ppermute(x, "front", [(4 * a + y, 4 * b + y) for a, b in pairs for y in range(4)])


def pick(z, *values):
    return jnp.where(z == 0, values[0], jnp.where(z == 1, values[1], jnp.where(z == 2, values[2], values[3])))


def ring_y(x, zs=(0, 1, 2, 3)):
    return [x] + [shift_y(x, d, zs) for d in (1, 2, 3)]


def local(front_matrix, child_blocks, child_target, child_count, shot_rhs):
    leaves, slots = child_blocks.shape[1:3]
    slot_ids = lax.broadcasted_iota(jnp.int32, (leaves, slots), 1)
    live_code = jnp.where(slot_ids < child_count[0][:, None], child_target[0], -1)
    code_rows = jnp.zeros((leaves, 8, B), F32).at[:, 0, :slots].set(live_code.astype(F32))
    payload = jnp.concatenate([child_blocks[0].reshape(leaves, slots * B, B), code_rows], axis=1)
    arrived = lax.all_to_all(payload, "leaf", split_axis=0, concat_axis=0, tiled=True)
    codes = arrived[:, slots * B, :slots].astype(jnp.int32)
    index = lax.axis_index("front").astype(jnp.int32).reshape(1)
    tail, early, late = assemble(codes, index, arrived, front_matrix[0])
    z = lax.axis_index("front") // 4
    rhs = shot_rhs[0]
    swap = planes(early, ((0, 1), (1, 0)))
    side = planes(early, ((1, 2), (0, 3)))
    cross = planes(early, ((0, 2), (1, 3)))
    near_last = jnp.concatenate(ring_y(late, (2, 3)), 0)
    early_parts = ring_y(jnp.concatenate([pick(z, early, swap, cross, side), pick(z, swap, early, side, cross)], 0))
    late_x, _ = lax.optimization_barrier((late, (swap, side, cross, near_last)))
    to0, to2, to3 = (planes(late_x, ((1, d),)) for d in (0, 2, 3))
    far_last = planes(near_last, ((2, 3), (3, 2)))
    mixed = jnp.concatenate([pick(z, to0, late_x, to2, to3), early], 0)
    mixed, _ = lax.optimization_barrier((mixed, early_parts))
    late_parts = ring_y(mixed)
    state = first(index, early_parts, rhs)
    near_first = jnp.concatenate([part[B:] for part in late_parts], 0)
    near_first, _ = lax.optimization_barrier((near_first, state[6]))
    far_first = planes(near_first, ((2, 3), (3, 2)))
    state = second(index, late_parts, state, rhs)
    lower = [near_first, near_last, far_first, far_last]
    factored, eliminated = third(index, lower, state, tail, rhs)
    tail = eliminated[:, PIV:]
    tail = jnp.where(z < 2, planes(tail, ((2, 1), (3, 0))), tail)
    eliminated = jnp.concatenate([eliminated[:, :PIV], tail], 1)
    return factored[None], eliminated[None]


def solution(mesh):
    return jax.shard_map(
        local,
        mesh=mesh,
        in_specs=(
            P("leaf", "front", None),
            P(("leaf", "front"), None, None, None, None),
            P(("leaf", "front"), None, None),
            P(("leaf", "front"), None),
            P("leaf", None, None),
        ),
        out_specs=(P("leaf", "front", None), P("leaf", None, None)),
        check_vma=False,
    )
```

```python
import jax
import jax.numpy as jnp
from jax import lax
from jax.experimental import pallas as pl
from jax.experimental.pallas import tpu as pltpu
from jax.sharding import PartitionSpec as P

B = 128
PIV = 1024
NP = PIV // B
HALF = PIV // 2
W2 = 2 * B
F32 = jnp.float32
BF16 = jnp.bfloat16


def split(x):
    hi = x.astype(BF16)
    lo = (x - hi.astype(F32)).astype(BF16)
    return hi, lo


def dot_t(a, b):
    return lax.dot_general(a, b, (((1,), (1,)), ((), ())), preferred_element_type=F32)


def dot_n(a, b):
    return lax.dot_general(a, b, (((1,), (0,)), ((), ())), preferred_element_type=F32)


def dot3_t(ah, al, bh, bl):
    return dot_t(ah, bh) + dot_t(al, bh) + dot_t(ah, bl)


def dot3_n(ah, al, bh, bl):
    return dot_n(ah, bh) + dot_n(al, bh) + dot_n(ah, bl)


def pack_kernel(target_ref, count_ref, blocks_ref, out_ref):
    leaves, slots = target_ref.shape[1:]
    spot = lax.broadcasted_iota(jnp.int32, (8, B), 1)
    out_ref[:, : slots * B, :] = blocks_ref[...]
    for s in range(leaves):
        codes = jnp.full((8, B), -1, jnp.int32)
        for j in range(slots):
            code = jnp.where(j < count_ref[0, s], target_ref[0, s, j], -1)
            codes = jnp.where(spot == j, code, codes)
        out_ref[s, slots * B :, :] = codes.astype(F32)


def pack(target, count, blocks):
    leaves, slots = target.shape[1:]
    smem, vmem = pl.BlockSpec(memory_space=pltpu.SMEM), pl.BlockSpec(memory_space=pltpu.VMEM)
    return pl.pallas_call(
        pack_kernel,
        out_shape=jax.ShapeDtypeStruct((leaves, slots * B + 8, B), F32),
        in_specs=[smem, smem, vmem],
        out_specs=vmem,
        compiler_params=pltpu.CompilerParams(vmem_limit_bytes=8 * 1024 * 1024),
        name="pack",
    )(target, count, blocks.reshape(leaves, slots * B, B))


def assemble_kernel(code_ref, idx_ref, recv_ref, front_ref, tail_ref, early_ref, late_ref, out_ref):
    out_ref[...] = front_ref[...]
    for s in range(recv_ref.shape[0]):
        for j in range(code_ref.shape[1]):
            code = code_ref[s, j]

            @pl.when(code >= 0)
            def _(s=s, j=j, code=code):
                cols = pl.ds(pl.multiple_of(code * B, B), B)
                out_ref[:, cols] += recv_ref[s, j * B : (j + 1) * B, :]

    cols = pl.ds(pl.multiple_of(idx_ref[0] * B, B), B)
    square = out_ref[:, cols]
    row = lax.broadcasted_iota(jnp.int32, (B, B), 0)
    col = lax.broadcasted_iota(jnp.int32, (B, B), 1)
    out_ref[:, cols] = jnp.where(row >= col, square, square.T)
    early_ref[...] = out_ref[:, :HALF]
    late_ref[...] = out_ref[:, HALF:PIV]
    tail_ref[...] = out_ref[:, PIV:]


def assemble(codes, index, recv, front):
    rows, order = front.shape
    vmem = pl.BlockSpec(memory_space=pltpu.VMEM)
    return pl.pallas_call(
        assemble_kernel,
        out_shape=(
            jax.ShapeDtypeStruct((rows, order - PIV), F32),
            jax.ShapeDtypeStruct((rows, HALF), F32),
            jax.ShapeDtypeStruct((rows, HALF), F32),
        ),
        in_specs=[pl.BlockSpec(memory_space=pltpu.SMEM)] * 2 + [vmem, vmem],
        out_specs=(vmem, vmem, vmem),
        scratch_shapes=[pltpu.VMEM((rows, order), F32)],
        compiler_params=pltpu.CompilerParams(vmem_limit_bytes=8 * 1024 * 1024),
        name="assemble",
    )(codes, index, recv, front)


def lane(x, c):
    return jnp.broadcast_to(x[:, c : c + 1], (8, B))


def sublane(x, t):
    return jnp.broadcast_to(x[t : t + 1, :], (8, B))


def chain(a_rows, e_rows, store, side):
    sub = lax.broadcasted_iota(jnp.int32, (8, B), 0)
    ahead = None
    for g in range(16):
        if g < len(side):
            side[g]()
        ra, re = a_rows[g], e_rows[g]
        base = 8 * g
        b = ahead or [lane(ra, base + t) for t in range(8)]
        more, far = g < 15, g < 14
        if more:
            na, ne = a_rows[g + 1], e_rows[g + 1]
            c = [lane(na, base + t) for t in range(8)]
            q = [lane(ra, base + 8 + t) for t in range(8)]
            ahead = [lane(na, base + 8 + t) for t in range(8)]
        ga, ge = ra, re
        fa, fe = ra, re
        rcps = []
        for t in range(8):
            r = 1.0 / sublane(b[t], t)
            rcps.append(r)
            m = b[t] * r
            mg = jnp.where(sub == t, 0.0, m)
            mf = jnp.where(sub > t, m, 0.0)
            pa, pe = sublane(fa, t), sublane(fe, t)
            if more:
                mn = c[t] * r
            for u in range(t + 1, 8):
                w = sublane(b[u], t)
                b[u] = b[u] - mg * w
                if more:
                    c[u] = c[u] - mn * w
            if more:
                for u in range(8):
                    w = sublane(q[u], t)
                    q[u] = q[u] - mf * w
                    ahead[u] = ahead[u] - mn * w
                na = na - mn * pa
                ne = ne - mn * pe
            fa = fa - mf * pa
            fe = fe - mf * pe
            if far:
                ga = ga - mg * pa
                ge = ge - mg * pe
        rc = rcps[0]
        for t in range(1, 8):
            rc = jnp.where(sub == t, rcps[t], rc)
        store(g, fa, fe, rc)
        if more:
            a_rows[g + 1], e_rows[g + 1] = na, ne
        if far:
            ga = ga * rc
            ge = ge * rc
            gab = [sublane(ga, t) for t in range(8)]
            geb = [sublane(ge, t) for t in range(8)]
            for i in range(g + 2, 16):
                acc_a, acc_e = a_rows[i], e_rows[i]
                for t in range(8):
                    cc = lane(a_rows[i], base + t)
                    acc_a = acc_a - cc * gab[t]
                    acc_e = acc_e - cc * geb[t]
                a_rows[i], e_rows[i] = acc_a, acc_e


def cat_blocks(a, b, c, d):
    return jnp.concatenate([jnp.concatenate([a, b], 1), jnp.concatenate([c, d], 1)], 0)


def factor_panels(k0, k1, a_ref, b_ref, vh, vl, v32, lh, ll, t_ref, lt_ref, dinv_ref,
                  rest_ref, u_ref, part_ref, e_ref):
    row0 = k0 * B
    na, nrhs = a_ref.shape[0], b_ref.shape[0]
    ri = lax.broadcasted_iota(jnp.int32, (8, B), 0)
    ci = lax.broadcasted_iota(jnp.int32, (8, B), 1)

    def settle(k):
        cols = pl.ds(pl.multiple_of(k * B, B), B)
        th, tl = split(t_ref[k])
        uh, ul = split(rest_ref[...])
        v = dot3_t(uh, ul, th, tl)
        v32[:, cols] = v
        vh[:, cols], vl[:, cols] = split(v)
        lrows = slice(row0, row0 + na)
        lh[lrows, cols], ll[lrows, cols] = split(v[:na] * dinv_ref[0:1, cols])

    def panel(k, _):
        kcols = pl.ds(pl.multiple_of(k * B, B), B)
        acols = pl.ds(pl.multiple_of((k - k0) * B, B), B)
        prev = jnp.maximum(k - 1, k0)
        after = jnp.minimum(k + 1, k1 - 1)
        nabs = pl.ds(pl.multiple_of(after * B, B), B)
        nloc = pl.ds(pl.multiple_of((after - k0) * B, B), B)
        a_rows = [u_ref[8 * i : 8 * i + 8, :] for i in range(16)]
        e_rows = [jnp.where(ri + 8 * i == ci, 1.0, 0.0) for i in range(16)]
        diag = []

        def store(g, fa, fe, rc):
            own = ri + 8 * g == ci
            diag.append(jnp.where(own, fa, 0.0))
            lt_ref[k, 8 * g : 8 * g + 8, :] = jnp.where(own, fa, jnp.where(ri + 8 * g < ci, fa * rc, 0.0))
            e_ref[8 * g : 8 * g + 8, :] = fe

        def update():
            prod = dot3_t(vh[...], vl[...], lh[kcols, :], ll[kcols, :])
            rest_ref[:na, :] = a_ref[:, acols] - prod[:na]
            rest_ref[na:, :] = b_ref[:, acols] - prod[na:]

        def partial():
            part_ref[...] = a_ref[nloc, nloc] - dot3_t(vh[nloc, :], vl[nloc, :], lh[nabs, :], ll[nabs, :])

        side = [lambda: settle(prev), update, partial]
        chain(a_rows, e_rows, store, side)
        total = diag[0]
        for g in range(1, 16):
            total = total + diag[g]
        dinv = 1.0 / jnp.sum(total, axis=0, keepdims=True)
        dinv_ref[0:1, kcols] = dinv
        t = e_ref[...]
        t_ref[k] = t
        th, tl = split(t)
        uh, ul = split(rest_ref[nloc, :])
        v = dot3_t(uh, ul, th, tl)
        v_h, v_l = split(v)
        l_h, l_l = split(v * dinv)
        u_ref[...] = part_ref[...] - dot3_t(v_h, v_l, l_h, l_l)
        return 0

    lax.fori_loop(k0, k1, panel, 0)
    settle(k1 - 1)


def first_kernel(idx_ref, y0_ref, y1_ref, y2_ref, y3_ref, b_ref,
                 vh, vl, lh, ll, t_ref, dinv_ref, y_ref, own_ref,
                 a_ref, v32, lt_ref, rest_ref, u_ref, part_ref, e_ref):
    me = idx_ref[0]
    ypos = lax.rem(me, 4)
    for d, ref in enumerate((y0_ref, y1_ref, y2_ref, y3_ref)):
        src = lax.rem(ypos + 4 - d, 4)
        for z in range(2):
            rows = pl.ds(pl.multiple_of((4 * z + src) * B, B), B)
            a_ref[rows, :] = ref[z * B : (z + 1) * B, :]
    for ref in (vh, vl, lh, ll, rest_ref, dinv_ref):
        ref[...] = jnp.zeros_like(ref)
    t_ref[0] = jnp.zeros((B, B), F32)
    u_ref[...] = a_ref[0:B, 0:B]
    factor_panels(0, NP // 2, a_ref, b_ref.at[:, pl.ds(0, HALF)], vh, vl, v32, lh, ll, t_ref, lt_ref, dinv_ref,
                  rest_ref, u_ref, part_ref, e_ref)
    nrhs = b_ref.shape[0]
    y_ref[...] = v32[PIV : PIV + nrhs, :]
    near = jnp.minimum(me, NP - 1)
    rows = pl.ds(pl.multiple_of(near * B, B), B)
    col = lax.broadcasted_iota(jnp.int32, (B, HALF), 1)
    own_ref[...] = jnp.where(col < near * B, v32[rows, :] * dinv_ref[0:1, :], 0.0)

    @pl.when(me < NP // 2)
    def _():
        own_ref[:, rows] = lt_ref[me].T


VMEM_SPEC = pl.BlockSpec(memory_space=pltpu.VMEM)


def first(index, parts, rhs):
    nrhs = rhs.shape[0]
    outs = (
        ((PIV + nrhs, HALF), BF16),
        ((PIV + nrhs, HALF), BF16),
        ((PIV, HALF), BF16),
        ((PIV, HALF), BF16),
        ((NP // 2, B, B), F32),
        ((8, HALF), F32),
        ((nrhs, HALF), F32),
        ((B, HALF), F32),
    )
    return pl.pallas_call(
        first_kernel,
        out_shape=tuple(jax.ShapeDtypeStruct(*o) for o in outs),
        in_specs=[pl.BlockSpec(memory_space=pltpu.SMEM)] + [VMEM_SPEC] * 5,
        out_specs=(VMEM_SPEC,) * len(outs),
        scratch_shapes=[
            pltpu.VMEM((PIV, HALF), F32),
            pltpu.VMEM((PIV + nrhs, HALF), F32),
            pltpu.VMEM((NP // 2, B, B), F32),
            pltpu.VMEM((PIV + nrhs, B), F32),
            pltpu.VMEM((B, B), F32),
            pltpu.VMEM((B, B), F32),
            pltpu.VMEM((B, B), F32),
        ],
        compiler_params=pltpu.CompilerParams(vmem_limit_bytes=20 * 1024 * 1024),
        cost_estimate=pl.CostEstimate(flops=2 * 10**10, bytes_accessed=2 * 10**7, transcendentals=0),
        name="first",
    )(index, *parts, rhs)


def second_kernel(idx_ref, p0_ref, p1_ref, p2_ref, p3_ref, vh0, vl0, lh0, ll0, t0, dinv0, y0, own0, b_ref,
                  lh, ll, t_ref, dinv_ref, y_ref, own_ref,
                  a_ref, vh, vl, v32, lt_ref, rest_ref, u_ref, part_ref, e_ref):
    me = idx_ref[0]
    nrhs = b_ref.shape[0]
    ypos = lax.rem(me, 4)
    for d, ref in enumerate((p0_ref, p1_ref, p2_ref, p3_ref)):
        rows = pl.ds(pl.multiple_of(lax.rem(ypos + 4 - d, 4) * B, B), B)
        a_ref[rows, :] = ref[...]
    for ref, src in ((vh, vh0), (vl, vl0)):
        ref[:, :HALF] = src[HALF:, :]
        ref[:, HALF:] = jnp.zeros((ref.shape[0], HALF), BF16)
    for ref, src in ((lh, lh0), (ll, ll0)):
        ref[:, :HALF] = src[...]
        ref[:, HALF:] = jnp.zeros((ref.shape[0], HALF), BF16)
    dinv_ref[:, :HALF] = dinv0[...]
    dinv_ref[:, HALF:] = jnp.zeros((dinv_ref.shape[0], HALF), F32)
    t_ref[: NP // 2] = t0[...]
    t_ref[NP // 2] = jnp.zeros((B, B), F32)
    rest_ref[...] = jnp.zeros_like(rest_ref)
    u_ref[...] = a_ref[0:B, 0:B] - dot3_t(
        vh[0:B, :HALF], vl[0:B, :HALF], lh[HALF : HALF + B, :HALF], ll[HALF : HALF + B, :HALF]
    )
    factor_panels(NP // 2, NP, a_ref, b_ref.at[:, pl.ds(HALF, HALF)], vh, vl, v32, lh, ll, t_ref, lt_ref,
                  dinv_ref, rest_ref, u_ref, part_ref, e_ref)
    y_ref[:, :HALF] = y0[...]
    y_ref[:, HALF:] = v32[HALF : HALF + nrhs, HALF:]
    own_ref[:, :HALF] = own0[...]
    near = jnp.clip(me - NP // 2, 0, NP // 2 - 1)
    rows = pl.ds(pl.multiple_of(near * B, B), B)
    col = HALF + lax.broadcasted_iota(jnp.int32, (B, HALF), 1)
    own_ref[:, HALF:] = jnp.where(col < me * B, v32[rows, HALF:] * dinv_ref[0:1, HALF:], 0.0)

    @pl.when((me >= NP // 2) & (me < NP))
    def _():
        own_ref[:, pl.ds(pl.multiple_of(me * B, B), B)] = lt_ref[me].T


def second(index, parts, state, rhs):
    nrhs = rhs.shape[0]
    na = PIV - HALF
    outs = (
        ((PIV, PIV), BF16),
        ((PIV, PIV), BF16),
        ((NP, B, B), F32),
        ((8, PIV), F32),
        ((nrhs, PIV), F32),
        ((B, PIV), F32),
    )
    return pl.pallas_call(
        second_kernel,
        out_shape=tuple(jax.ShapeDtypeStruct(*o) for o in outs),
        in_specs=[pl.BlockSpec(memory_space=pltpu.SMEM)] + [VMEM_SPEC] * (len(parts) + len(state) + 1),
        out_specs=(VMEM_SPEC,) * len(outs),
        scratch_shapes=[
            pltpu.VMEM((na, na), F32),
            pltpu.VMEM((na + nrhs, PIV), BF16),
            pltpu.VMEM((na + nrhs, PIV), BF16),
            pltpu.VMEM((na + nrhs, PIV), F32),
            pltpu.VMEM((NP, B, B), F32),
            pltpu.VMEM((na + nrhs, B), F32),
            pltpu.VMEM((B, B), F32),
            pltpu.VMEM((B, B), F32),
            pltpu.VMEM((B, B), F32),
        ],
        compiler_params=pltpu.CompilerParams(vmem_limit_bytes=20 * 1024 * 1024),
        cost_estimate=pl.CostEstimate(flops=2 * 10**10, bytes_accessed=2 * 10**7, transcendentals=0),
        name="second",
    )(index, *parts, *state, rhs)


def third_kernel(idx_ref, h0, h1, h2, h3, near_ref, far_ref, lh, ll, t_ref, dinv_ref, y_ref, own_ref, tail_ref, b_ref,
                 fac_ref, eli_ref, a21, xh, xl, x32, wh, wl, sem):
    me = idx_ref[0]
    nrhs, order = b_ref.shape
    low = order - PIV
    ypos, zpos = lax.rem(me, 4), jnp.clip(me // 4 - 2, 0, 1)
    copies = []
    for d, ref in enumerate((h0, h1, h2, h3)):
        spot = lax.rem(ypos + 4 - d, 4)
        for n, z in enumerate((zpos, 1 - zpos)):
            rows = pl.ds(pl.multiple_of((4 * z + spot) * B, B), B)
            src = (near_ref, far_ref)[n]
            copies.append(pltpu.make_async_copy(
                ref.at[pl.ds(n * B, B), :], a21.at[rows, pl.ds(0, HALF)], sem.at[2 * d + n]))
            copies.append(pltpu.make_async_copy(
                src.at[pl.ds(d * B, B), :], a21.at[rows, pl.ds(HALF, HALF)], sem.at[8 + 2 * d + n]))
    for copy in copies:
        copy.start()

    inverses = []
    for i in range(NP // 2):
        t0h, t0l = split(t_ref[2 * i])
        t1h, t1l = split(t_ref[2 * i + 1])
        r1 = slice((2 * i + 1) * B, (2 * i + 2) * B)
        c0 = slice(2 * i * B, (2 * i + 1) * B)
        zh, zl = split(dot3_n(lh[r1, c0], ll[r1, c0], t0h, t0l))
        zh, zl = split(-dot3_n(t1h, t1l, zh, zl))
        zero = jnp.zeros((B, B), BF16)
        inverses.append((cat_blocks(t0h, zero, zh, t1h), cat_blocks(t0l, zero, zl, t1l)))
    for copy in copies:
        copy.wait()
    for i in range(NP // 2):
        pc, prev = slice(i * W2, (i + 1) * W2), slice(0, i * W2)
        u = a21[:, pc]
        if i:
            u = u - dot3_t(xh[:, prev], xl[:, prev], lh[pc, prev], ll[pc, prev])
        uh, ul = split(u)
        v = dot3_t(uh, ul, *inverses[i])
        x32[:, pc] = v
        xh[:, pc], xl[:, pc] = split(v)
        wh[:, pc], wl[:, pc] = split(v * dinv_ref[0:1, pc])

    y = y_ref[...]
    yh, yl = split(y)
    eli_ref[:, :PIV] = y
    mine = pl.ds(pl.multiple_of(jnp.maximum(me - NP, 0) * B, B), B)
    n = B + nrhs
    qh = jnp.concatenate([xh[mine, :], yh], 0)
    both = jnp.concatenate([qh, xl[mine, :], yl], 0)
    for c in range(low // W2):
        rows = slice(c * W2, (c + 1) * W2)
        dst = slice(PIV + c * W2, PIV + (c + 1) * W2)
        prod = dot_t(both, wh[rows, :])
        prod = prod[:n] + prod[n:] + dot_t(qh, wl[rows, :])
        row = me * B + lax.broadcasted_iota(jnp.int32, (B, W2), 0)
        col = PIV + c * W2 + lax.broadcasted_iota(jnp.int32, (B, W2), 1)
        fac_ref[:, dst] = jnp.where(row >= col, tail_ref[:, rows] - prod[:B], 0.0)
        eli_ref[:, dst] = b_ref[:, dst] - prod[B:]
    lower = me >= NP

    @pl.when(lower)
    def _():
        fac_ref[:, :PIV] = x32[mine, :] * dinv_ref[0:1, :]

    @pl.when(jnp.logical_not(lower))
    def _():
        fac_ref[:, :PIV] = own_ref[...]


def third(index, lower, state, tail, rhs):
    nrhs, order = rhs.shape
    low = order - PIV
    return pl.pallas_call(
        third_kernel,
        out_shape=(
            jax.ShapeDtypeStruct((B, order), F32),
            jax.ShapeDtypeStruct((nrhs, order), F32),
        ),
        in_specs=[pl.BlockSpec(memory_space=pltpu.SMEM)] + [VMEM_SPEC] * (len(lower) + len(state) + 2),
        out_specs=(VMEM_SPEC, VMEM_SPEC),
        scratch_shapes=[
            pltpu.VMEM((low, PIV), F32),
            pltpu.VMEM((low, PIV), BF16),
            pltpu.VMEM((low, PIV), BF16),
            pltpu.VMEM((low, PIV), F32),
            pltpu.VMEM((low, PIV), BF16),
            pltpu.VMEM((low, PIV), BF16),
            pltpu.SemaphoreType.DMA((16,)),
        ],
        compiler_params=pltpu.CompilerParams(vmem_limit_bytes=34 * 1024 * 1024),
        name="third",
    )(index, *lower, *state, tail, rhs)


def shift_y(x, d, zs=(0, 1, 2, 3)):
    return lax.ppermute(x, "front", [(4 * z + y, 4 * z + (y + d) % 4) for z in zs for y in range(4)])


def planes(x, pairs):
    return lax.ppermute(x, "front", [(4 * a + y, 4 * b + y) for a, b in pairs for y in range(4)])


def pick(z, *values):
    return jnp.where(z == 0, values[0], jnp.where(z == 1, values[1], jnp.where(z == 2, values[2], values[3])))


def ring_y(x, zs=(0, 1, 2, 3)):
    return [x] + [shift_y(x, d, zs) for d in (1, 2, 3)]


def local(front_matrix, child_blocks, child_target, child_count, shot_rhs):
    leaves, slots = child_blocks.shape[1:3]
    payload = pack(child_target, child_count, child_blocks)
    arrived = lax.all_to_all(payload, "leaf", split_axis=0, concat_axis=0, tiled=True)
    codes = arrived[:, slots * B, :slots].astype(jnp.int32)
    index = lax.axis_index("front").astype(jnp.int32).reshape(1)
    tail, early, late = assemble(codes, index, arrived, front_matrix[0])
    z = lax.axis_index("front") // 4
    rhs = shot_rhs[0]
    swap = planes(early, ((0, 1), (1, 0), (2, 3), (3, 2)))
    side = planes(early, ((1, 2), (0, 3)))
    cross = planes(early, ((0, 2), (1, 3)))
    near = jnp.concatenate(ring_y(late, (2, 3)), 0)
    early_parts = ring_y(jnp.concatenate([pick(z, early, swap, cross, side), pick(z, swap, early, side, cross)], 0))
    late_x, _ = lax.optimization_barrier((late, (swap, side, cross)))
    to0, to2, to3 = (planes(late_x, ((1, d),)) for d in (0, 2, 3))
    late_parts = ring_y(pick(z, to0, late_x, to2, to3))
    far = planes(near, ((2, 3), (3, 2)))
    state = first(index, early_parts, rhs)
    pair, _ = lax.optimization_barrier((jnp.concatenate([early, swap], 0), state[6]))
    below = ring_y(pair, (2, 3))
    state = second(index, late_parts, state, rhs)
    factored, eliminated = third(index, below + [near, far], state, tail, rhs)
    tail = eliminated[:, PIV:]
    tail = jnp.where(z < 2, planes(tail, ((2, 1), (3, 0))), tail)
    eliminated = jnp.concatenate([eliminated[:, :PIV], tail], 1)
    return factored[None], eliminated[None]


def solution(mesh):
    return jax.shard_map(
        local,
        mesh=mesh,
        in_specs=(
            P("leaf", "front", None),
            P(("leaf", "front"), None, None, None, None),
            P(("leaf", "front"), None, None),
            P(("leaf", "front"), None),
            P("leaf", None, None),
        ),
        out_specs=(P("leaf", "front", None), P("leaf", None, None)),
        check_vma=False,
    )
```

```python
import jax
import jax.numpy as jnp
from jax import lax
from jax.experimental import pallas as pl
from jax.experimental.pallas import tpu as pltpu
from jax.sharding import PartitionSpec as P

B = 128
PIV = 1024
NP = PIV // B
HALF = PIV // 2
W2 = 2 * B
F32 = jnp.float32
BF16 = jnp.bfloat16


def split(x):
    hi = x.astype(BF16)
    lo = (x - hi.astype(F32)).astype(BF16)
    return hi, lo


def dot_t(a, b):
    return lax.dot_general(a, b, (((1,), (1,)), ((), ())), preferred_element_type=F32)


def dot_n(a, b):
    return lax.dot_general(a, b, (((1,), (0,)), ((), ())), preferred_element_type=F32)


def dot3_t(ah, al, bh, bl):
    return dot_t(ah, bh) + dot_t(al, bh) + dot_t(ah, bl)


def dot3_n(ah, al, bh, bl):
    return dot_n(ah, bh) + dot_n(al, bh) + dot_n(ah, bl)


def assemble_kernel(code_ref, idx_ref, recv_ref, front_ref, tail_ref, early_ref, late_ref, out_ref):
    out_ref[...] = front_ref[...]
    for s in range(recv_ref.shape[0]):
        for j in range(code_ref.shape[1]):
            code = code_ref[s, j]

            @pl.when(code >= 0)
            def _(s=s, j=j, code=code):
                cols = pl.ds(pl.multiple_of(code * B, B), B)
                out_ref[:, cols] += recv_ref[s, j * B : (j + 1) * B, :]

    cols = pl.ds(pl.multiple_of(idx_ref[0] * B, B), B)
    square = out_ref[:, cols]
    row = lax.broadcasted_iota(jnp.int32, (B, B), 0)
    col = lax.broadcasted_iota(jnp.int32, (B, B), 1)
    out_ref[:, cols] = jnp.where(row >= col, square, square.T)
    early_ref[...] = out_ref[:, :HALF]
    late_ref[...] = out_ref[:, HALF:PIV]
    tail_ref[...] = out_ref[:, PIV:]


def assemble(codes, index, recv, front):
    rows, order = front.shape
    vmem = pl.BlockSpec(memory_space=pltpu.VMEM)
    return pl.pallas_call(
        assemble_kernel,
        out_shape=(
            jax.ShapeDtypeStruct((rows, order - PIV), F32),
            jax.ShapeDtypeStruct((rows, HALF), F32),
            jax.ShapeDtypeStruct((rows, HALF), F32),
        ),
        in_specs=[pl.BlockSpec(memory_space=pltpu.SMEM)] * 2 + [vmem, vmem],
        out_specs=(vmem, vmem, vmem),
        scratch_shapes=[pltpu.VMEM((rows, order), F32)],
        compiler_params=pltpu.CompilerParams(vmem_limit_bytes=8 * 1024 * 1024),
        name="assemble",
    )(codes, index, recv, front)


def lane(x, c):
    return jnp.broadcast_to(x[:, c : c + 1], (8, B))


def sublane(x, t):
    return jnp.broadcast_to(x[t : t + 1, :], (8, B))


def chain(a_rows, e_rows, store, side):
    sub = lax.broadcasted_iota(jnp.int32, (8, B), 0)
    ahead = None
    for g in range(16):
        if g < len(side):
            side[g]()
        ra, re = a_rows[g], e_rows[g]
        base = 8 * g
        b = ahead or [lane(ra, base + t) for t in range(8)]
        more, far = g < 15, g < 14
        if more:
            na, ne = a_rows[g + 1], e_rows[g + 1]
            c = [lane(na, base + t) for t in range(8)]
            q = [lane(ra, base + 8 + t) for t in range(8)]
            ahead = [lane(na, base + 8 + t) for t in range(8)]
        ga, ge = ra, re
        fa, fe = ra, re
        rcps = []
        for t in range(8):
            r = 1.0 / sublane(b[t], t)
            rcps.append(r)
            m = b[t] * r
            mg = jnp.where(sub == t, 0.0, m)
            mf = jnp.where(sub > t, m, 0.0)
            pa, pe = sublane(fa, t), sublane(fe, t)
            if more:
                mn = c[t] * r
            for u in range(t + 1, 8):
                w = sublane(b[u], t)
                b[u] = b[u] - mg * w
                if more:
                    c[u] = c[u] - mn * w
            if more:
                for u in range(8):
                    w = sublane(q[u], t)
                    q[u] = q[u] - mf * w
                    ahead[u] = ahead[u] - mn * w
                na = na - mn * pa
                ne = ne - mn * pe
            fa = fa - mf * pa
            fe = fe - mf * pe
            if far:
                ga = ga - mg * pa
                ge = ge - mg * pe
        rc = rcps[0]
        for t in range(1, 8):
            rc = jnp.where(sub == t, rcps[t], rc)
        store(g, fa, fe, rc)
        if more:
            a_rows[g + 1], e_rows[g + 1] = na, ne
        if far:
            ga = ga * rc
            ge = ge * rc
            gab = [sublane(ga, t) for t in range(8)]
            geb = [sublane(ge, t) for t in range(8)]
            for i in range(g + 2, 16):
                acc_a, acc_e = a_rows[i], e_rows[i]
                for t in range(8):
                    cc = lane(a_rows[i], base + t)
                    acc_a = acc_a - cc * gab[t]
                    acc_e = acc_e - cc * geb[t]
                a_rows[i], e_rows[i] = acc_a, acc_e


def cat_blocks(a, b, c, d):
    return jnp.concatenate([jnp.concatenate([a, b], 1), jnp.concatenate([c, d], 1)], 0)


def factor_panels(k0, k1, a_ref, b_ref, vh, vl, v32, lh, ll, t_ref, lt_ref, dinv_ref,
                  rest_ref, u_ref, part_ref, e_ref):
    row0 = k0 * B
    na, nrhs = a_ref.shape[0], b_ref.shape[0]
    ri = lax.broadcasted_iota(jnp.int32, (8, B), 0)
    ci = lax.broadcasted_iota(jnp.int32, (8, B), 1)

    def settle(k):
        cols = pl.ds(pl.multiple_of(k * B, B), B)
        th, tl = split(t_ref[k])
        uh, ul = split(rest_ref[...])
        v = dot3_t(uh, ul, th, tl)
        v32[:, cols] = v
        vh[:, cols], vl[:, cols] = split(v)
        lrows = slice(row0, row0 + na)
        lh[lrows, cols], ll[lrows, cols] = split(v[:na] * dinv_ref[0:1, cols])

    def panel(k, _):
        kcols = pl.ds(pl.multiple_of(k * B, B), B)
        acols = pl.ds(pl.multiple_of((k - k0) * B, B), B)
        prev = jnp.maximum(k - 1, k0)
        after = jnp.minimum(k + 1, k1 - 1)
        nabs = pl.ds(pl.multiple_of(after * B, B), B)
        nloc = pl.ds(pl.multiple_of((after - k0) * B, B), B)
        a_rows = [u_ref[8 * i : 8 * i + 8, :] for i in range(16)]
        e_rows = [jnp.where(ri + 8 * i == ci, 1.0, 0.0) for i in range(16)]
        diag = []

        def store(g, fa, fe, rc):
            own = ri + 8 * g == ci
            diag.append(jnp.where(own, fa, 0.0))
            lt_ref[k, 8 * g : 8 * g + 8, :] = jnp.where(own, fa, jnp.where(ri + 8 * g < ci, fa * rc, 0.0))
            e_ref[8 * g : 8 * g + 8, :] = fe

        def update():
            prod = dot3_t(vh[...], vl[...], lh[kcols, :], ll[kcols, :])
            rest_ref[:na, :] = a_ref[:, acols] - prod[:na]
            rest_ref[na:, :] = b_ref[:, acols] - prod[na:]

        def partial():
            part_ref[...] = a_ref[nloc, nloc] - dot3_t(vh[nloc, :], vl[nloc, :], lh[nabs, :], ll[nabs, :])

        side = [lambda: settle(prev), update, partial]
        chain(a_rows, e_rows, store, side)
        total = diag[0]
        for g in range(1, 16):
            total = total + diag[g]
        dinv = 1.0 / jnp.sum(total, axis=0, keepdims=True)
        dinv_ref[0:1, kcols] = dinv
        t = e_ref[...]
        t_ref[k] = t
        th, tl = split(t)
        uh, ul = split(rest_ref[nloc, :])
        v = dot3_t(uh, ul, th, tl)
        v_h, v_l = split(v)
        l_h, l_l = split(v * dinv)
        u_ref[...] = part_ref[...] - dot3_t(v_h, v_l, l_h, l_l)
        return 0

    lax.fori_loop(k0, k1, panel, 0)
    settle(k1 - 1)


def first_kernel(idx_ref, y0_ref, y1_ref, y2_ref, y3_ref, b_ref,
                 vh, vl, lh, ll, t_ref, dinv_ref, y_ref, own_ref,
                 a_ref, v32, lt_ref, rest_ref, u_ref, part_ref, e_ref):
    me = idx_ref[0]
    ypos = lax.rem(me, 4)
    for d, ref in enumerate((y0_ref, y1_ref, y2_ref, y3_ref)):
        src = lax.rem(ypos + 4 - d, 4)
        for z in range(2):
            rows = pl.ds(pl.multiple_of((4 * z + src) * B, B), B)
            a_ref[rows, :] = ref[z * B : (z + 1) * B, :]
    for ref in (vh, vl, lh, ll, rest_ref, dinv_ref):
        ref[...] = jnp.zeros_like(ref)
    t_ref[0] = jnp.zeros((B, B), F32)
    u_ref[...] = a_ref[0:B, 0:B]
    factor_panels(0, NP // 2, a_ref, b_ref.at[:, pl.ds(0, HALF)], vh, vl, v32, lh, ll, t_ref, lt_ref, dinv_ref,
                  rest_ref, u_ref, part_ref, e_ref)
    nrhs = b_ref.shape[0]
    y_ref[...] = v32[PIV : PIV + nrhs, :]
    near = jnp.minimum(me, NP - 1)
    rows = pl.ds(pl.multiple_of(near * B, B), B)
    col = lax.broadcasted_iota(jnp.int32, (B, HALF), 1)
    own_ref[...] = jnp.where(col < near * B, v32[rows, :] * dinv_ref[0:1, :], 0.0)

    @pl.when(me < NP // 2)
    def _():
        own_ref[:, rows] = lt_ref[me].T


VMEM_SPEC = pl.BlockSpec(memory_space=pltpu.VMEM)


def first(index, parts, rhs):
    nrhs = rhs.shape[0]
    outs = (
        ((PIV + nrhs, HALF), BF16),
        ((PIV + nrhs, HALF), BF16),
        ((PIV, HALF), BF16),
        ((PIV, HALF), BF16),
        ((NP // 2, B, B), F32),
        ((8, HALF), F32),
        ((nrhs, HALF), F32),
        ((B, HALF), F32),
    )
    return pl.pallas_call(
        first_kernel,
        out_shape=tuple(jax.ShapeDtypeStruct(*o) for o in outs),
        in_specs=[pl.BlockSpec(memory_space=pltpu.SMEM)] + [VMEM_SPEC] * 5,
        out_specs=(VMEM_SPEC,) * len(outs),
        scratch_shapes=[
            pltpu.VMEM((PIV, HALF), F32),
            pltpu.VMEM((PIV + nrhs, HALF), F32),
            pltpu.VMEM((NP // 2, B, B), F32),
            pltpu.VMEM((PIV + nrhs, B), F32),
            pltpu.VMEM((B, B), F32),
            pltpu.VMEM((B, B), F32),
            pltpu.VMEM((B, B), F32),
        ],
        compiler_params=pltpu.CompilerParams(vmem_limit_bytes=20 * 1024 * 1024),
        cost_estimate=pl.CostEstimate(flops=2 * 10**10, bytes_accessed=2 * 10**7, transcendentals=0),
        name="first",
    )(index, *parts, rhs)


def second_kernel(idx_ref, p0_ref, p1_ref, p2_ref, p3_ref, vh0, vl0, lh0, ll0, t0, dinv0, y0, own0, b_ref,
                  lh, ll, t_ref, dinv_ref, y_ref, own_ref,
                  a_ref, vh, vl, v32, lt_ref, rest_ref, u_ref, part_ref, e_ref):
    me = idx_ref[0]
    nrhs = b_ref.shape[0]
    ypos = lax.rem(me, 4)
    for d, ref in enumerate((p0_ref, p1_ref, p2_ref, p3_ref)):
        rows = pl.ds(pl.multiple_of(lax.rem(ypos + 4 - d, 4) * B, B), B)
        a_ref[rows, :] = ref[:B, :]
    for ref, src in ((vh, vh0), (vl, vl0)):
        ref[:, :HALF] = src[HALF:, :]
        ref[:, HALF:] = jnp.zeros((ref.shape[0], HALF), BF16)
    for ref, src in ((lh, lh0), (ll, ll0)):
        ref[:, :HALF] = src[...]
        ref[:, HALF:] = jnp.zeros((ref.shape[0], HALF), BF16)
    dinv_ref[:, :HALF] = dinv0[...]
    dinv_ref[:, HALF:] = jnp.zeros((dinv_ref.shape[0], HALF), F32)
    t_ref[: NP // 2] = t0[...]
    t_ref[NP // 2] = jnp.zeros((B, B), F32)
    rest_ref[...] = jnp.zeros_like(rest_ref)
    u_ref[...] = a_ref[0:B, 0:B] - dot3_t(
        vh[0:B, :HALF], vl[0:B, :HALF], lh[HALF : HALF + B, :HALF], ll[HALF : HALF + B, :HALF]
    )
    factor_panels(NP // 2, NP, a_ref, b_ref.at[:, pl.ds(HALF, HALF)], vh, vl, v32, lh, ll, t_ref, lt_ref,
                  dinv_ref, rest_ref, u_ref, part_ref, e_ref)
    y_ref[:, :HALF] = y0[...]
    y_ref[:, HALF:] = v32[HALF : HALF + nrhs, HALF:]
    own_ref[:, :HALF] = own0[...]
    near = jnp.clip(me - NP // 2, 0, NP // 2 - 1)
    rows = pl.ds(pl.multiple_of(near * B, B), B)
    col = HALF + lax.broadcasted_iota(jnp.int32, (B, HALF), 1)
    own_ref[:, HALF:] = jnp.where(col < me * B, v32[rows, HALF:] * dinv_ref[0:1, HALF:], 0.0)

    @pl.when((me >= NP // 2) & (me < NP))
    def _():
        own_ref[:, pl.ds(pl.multiple_of(me * B, B), B)] = lt_ref[me].T


def second(index, parts, state, rhs):
    nrhs = rhs.shape[0]
    na = PIV - HALF
    outs = (
        ((PIV, PIV), BF16),
        ((PIV, PIV), BF16),
        ((NP, B, B), F32),
        ((8, PIV), F32),
        ((nrhs, PIV), F32),
        ((B, PIV), F32),
    )
    return pl.pallas_call(
        second_kernel,
        out_shape=tuple(jax.ShapeDtypeStruct(*o) for o in outs),
        in_specs=[pl.BlockSpec(memory_space=pltpu.SMEM)] + [VMEM_SPEC] * (len(parts) + len(state) + 1),
        out_specs=(VMEM_SPEC,) * len(outs),
        scratch_shapes=[
            pltpu.VMEM((na, na), F32),
            pltpu.VMEM((na + nrhs, PIV), BF16),
            pltpu.VMEM((na + nrhs, PIV), BF16),
            pltpu.VMEM((na + nrhs, PIV), F32),
            pltpu.VMEM((NP, B, B), F32),
            pltpu.VMEM((na + nrhs, B), F32),
            pltpu.VMEM((B, B), F32),
            pltpu.VMEM((B, B), F32),
            pltpu.VMEM((B, B), F32),
        ],
        compiler_params=pltpu.CompilerParams(vmem_limit_bytes=20 * 1024 * 1024),
        cost_estimate=pl.CostEstimate(flops=2 * 10**10, bytes_accessed=2 * 10**7, transcendentals=0),
        name="second",
    )(index, *parts, *state, rhs)


def third_kernel(idx_ref, h0, h1, h2, h3, near_ref, far_ref, lh, ll, t_ref, dinv_ref, y_ref, own_ref, tail_ref, b_ref,
                 fac_ref, eli_ref, a21, xh, xl, x32, wh, wl, sem):
    me = idx_ref[0]
    nrhs, order = b_ref.shape
    low = order - PIV
    ypos, zpos = lax.rem(me, 4), jnp.clip(me // 4 - 2, 0, 1)
    copies = []
    for d, ref in enumerate((h0, h1, h2, h3)):
        spot = lax.rem(ypos + 4 - d, 4)
        for n, z in enumerate((zpos, 1 - zpos)):
            rows = pl.ds(pl.multiple_of((4 * z + spot) * B, B), B)
            src = (near_ref, far_ref)[n]
            copies.append(pltpu.make_async_copy(
                ref.at[pl.ds((n + 1) * B, B), :], a21.at[rows, pl.ds(0, HALF)], sem.at[2 * d + n]))
            copies.append(pltpu.make_async_copy(
                src.at[pl.ds(d * B, B), :], a21.at[rows, pl.ds(HALF, HALF)], sem.at[8 + 2 * d + n]))
    for copy in copies:
        copy.start()

    inverses = []
    for i in range(NP // 2):
        t0h, t0l = split(t_ref[2 * i])
        t1h, t1l = split(t_ref[2 * i + 1])
        r1 = slice((2 * i + 1) * B, (2 * i + 2) * B)
        c0 = slice(2 * i * B, (2 * i + 1) * B)
        zh, zl = split(dot3_n(lh[r1, c0], ll[r1, c0], t0h, t0l))
        zh, zl = split(-dot3_n(t1h, t1l, zh, zl))
        zero = jnp.zeros((B, B), BF16)
        inverses.append((cat_blocks(t0h, zero, zh, t1h), cat_blocks(t0l, zero, zl, t1l)))
    for copy in copies:
        copy.wait()
    for i in range(NP // 2):
        pc, prev = slice(i * W2, (i + 1) * W2), slice(0, i * W2)
        u = a21[:, pc]
        if i:
            u = u - dot3_t(xh[:, prev], xl[:, prev], lh[pc, prev], ll[pc, prev])
        uh, ul = split(u)
        v = dot3_t(uh, ul, *inverses[i])
        x32[:, pc] = v
        xh[:, pc], xl[:, pc] = split(v)
        wh[:, pc], wl[:, pc] = split(v * dinv_ref[0:1, pc])

    y = y_ref[...]
    yh, yl = split(y)
    eli_ref[:, :PIV] = y
    mine = pl.ds(pl.multiple_of(jnp.maximum(me - NP, 0) * B, B), B)
    n = B + nrhs
    qh = jnp.concatenate([xh[mine, :], yh], 0)
    both = jnp.concatenate([qh, xl[mine, :], yl], 0)
    for c in range(low // W2):
        rows = slice(c * W2, (c + 1) * W2)
        dst = slice(PIV + c * W2, PIV + (c + 1) * W2)
        prod = dot_t(both, wh[rows, :])
        prod = prod[:n] + prod[n:] + dot_t(qh, wl[rows, :])
        row = me * B + lax.broadcasted_iota(jnp.int32, (B, W2), 0)
        col = PIV + c * W2 + lax.broadcasted_iota(jnp.int32, (B, W2), 1)
        fac_ref[:, dst] = jnp.where(row >= col, tail_ref[:, rows] - prod[:B], 0.0)
        eli_ref[:, dst] = b_ref[:, dst] - prod[B:]
    lower = me >= NP

    @pl.when(lower)
    def _():
        fac_ref[:, :PIV] = x32[mine, :] * dinv_ref[0:1, :]

    @pl.when(jnp.logical_not(lower))
    def _():
        fac_ref[:, :PIV] = own_ref[...]


def third(index, lower, state, tail, rhs):
    nrhs, order = rhs.shape
    low = order - PIV
    return pl.pallas_call(
        third_kernel,
        out_shape=(
            jax.ShapeDtypeStruct((B, order), F32),
            jax.ShapeDtypeStruct((nrhs, order), F32),
        ),
        in_specs=[pl.BlockSpec(memory_space=pltpu.SMEM)] + [VMEM_SPEC] * (len(lower) + len(state) + 2),
        out_specs=(VMEM_SPEC, VMEM_SPEC),
        scratch_shapes=[
            pltpu.VMEM((low, PIV), F32),
            pltpu.VMEM((low, PIV), BF16),
            pltpu.VMEM((low, PIV), BF16),
            pltpu.VMEM((low, PIV), F32),
            pltpu.VMEM((low, PIV), BF16),
            pltpu.VMEM((low, PIV), BF16),
            pltpu.SemaphoreType.DMA((16,)),
        ],
        compiler_params=pltpu.CompilerParams(vmem_limit_bytes=34 * 1024 * 1024),
        name="third",
    )(index, *lower, *state, tail, rhs)


def shift_y(x, d, zs=(0, 1, 2, 3)):
    return lax.ppermute(x, "front", [(4 * z + y, 4 * z + (y + d) % 4) for z in zs for y in range(4)])


def planes(x, pairs):
    return lax.ppermute(x, "front", [(4 * a + y, 4 * b + y) for a, b in pairs for y in range(4)])


def pick(z, *values):
    return jnp.where(z == 0, values[0], jnp.where(z == 1, values[1], jnp.where(z == 2, values[2], values[3])))


def ring_y(x, zs=(0, 1, 2, 3)):
    return [x] + [shift_y(x, d, zs) for d in (1, 2, 3)]


def local(front_matrix, child_blocks, child_target, child_count, shot_rhs):
    leaves, slots = child_blocks.shape[1:3]
    slot_ids = lax.broadcasted_iota(jnp.int32, (leaves, slots), 1)
    live_code = jnp.where(slot_ids < child_count[0][:, None], child_target[0], -1)
    code_rows = jnp.zeros((leaves, 8, B), F32).at[:, 0, :slots].set(live_code.astype(F32))
    payload = jnp.concatenate([child_blocks[0].reshape(leaves, slots * B, B), code_rows], axis=1)
    arrived = lax.all_to_all(payload, "leaf", split_axis=0, concat_axis=0, tiled=True)
    codes = arrived[:, slots * B, :slots].astype(jnp.int32)
    index = lax.axis_index("front").astype(jnp.int32).reshape(1)
    tail, early, late = assemble(codes, index, arrived, front_matrix[0])
    z = lax.axis_index("front") // 4
    rhs = shot_rhs[0]
    swap = planes(early, ((0, 1), (1, 0), (2, 3), (3, 2)))
    side = planes(early, ((1, 2), (0, 3)))
    cross = planes(early, ((0, 2), (1, 3)))
    near = jnp.concatenate(ring_y(late, (2, 3)), 0)
    early_parts = ring_y(jnp.concatenate([pick(z, early, swap, cross, side), pick(z, swap, early, side, cross)], 0))
    late_x, _ = lax.optimization_barrier((late, (swap, side, cross)))
    to0, to2, to3 = (planes(late_x, ((1, d),)) for d in (0, 2, 3))
    late_parts = ring_y(jnp.concatenate([pick(z, to0, late_x, to2, to3), early, swap], 0))
    far = planes(near, ((2, 3), (3, 2)))
    state = first(index, early_parts, rhs)
    state = second(index, late_parts, state, rhs)
    factored, eliminated = third(index, late_parts + [near, far], state, tail, rhs)
    tail = eliminated[:, PIV:]
    tail = jnp.where(z < 2, planes(tail, ((2, 1), (3, 0))), tail)
    eliminated = jnp.concatenate([eliminated[:, :PIV], tail], 1)
    return factored[None], eliminated[None]


def solution(mesh):
    return jax.shard_map(
        local,
        mesh=mesh,
        in_specs=(
            P("leaf", "front", None),
            P(("leaf", "front"), None, None, None, None),
            P(("leaf", "front"), None, None),
            P(("leaf", "front"), None),
            P("leaf", None, None),
        ),
        out_specs=(P("leaf", "front", None), P("leaf", None, None)),
        check_vma=False,
    )
```

```python
import jax
import jax.numpy as jnp
from jax import lax
from jax.experimental import pallas as pl
from jax.experimental.pallas import tpu as pltpu
from jax.sharding import PartitionSpec as P

B = 128
PIV = 1024
NP = PIV // B
HALF = PIV // 2
W2 = 2 * B
F32 = jnp.float32
BF16 = jnp.bfloat16


def split(x):
    hi = x.astype(BF16)
    lo = (x - hi.astype(F32)).astype(BF16)
    return hi, lo


def dot_t(a, b):
    return lax.dot_general(a, b, (((1,), (1,)), ((), ())), preferred_element_type=F32)


def dot_n(a, b):
    return lax.dot_general(a, b, (((1,), (0,)), ((), ())), preferred_element_type=F32)


def dot3_t(ah, al, bh, bl):
    return dot_t(ah, bh) + dot_t(al, bh) + dot_t(ah, bl)


def dot3_n(ah, al, bh, bl):
    return dot_n(ah, bh) + dot_n(al, bh) + dot_n(ah, bl)


def assemble_kernel(code_ref, idx_ref, recv_ref, front_ref, tail_ref, early_ref, late_ref, out_ref):
    out_ref[...] = front_ref[...]
    for s in range(recv_ref.shape[0]):
        for j in range(code_ref.shape[1]):
            code = code_ref[s, j]

            @pl.when(code >= 0)
            def _(s=s, j=j, code=code):
                cols = pl.ds(pl.multiple_of(code * B, B), B)
                out_ref[:, cols] += recv_ref[s, j * B : (j + 1) * B, :]

    cols = pl.ds(pl.multiple_of(idx_ref[0] * B, B), B)
    square = out_ref[:, cols]
    row = lax.broadcasted_iota(jnp.int32, (B, B), 0)
    col = lax.broadcasted_iota(jnp.int32, (B, B), 1)
    out_ref[:, cols] = jnp.where(row >= col, square, square.T)
    early_ref[...] = out_ref[:, :HALF]
    late_ref[...] = out_ref[:, HALF:PIV]
    tail_ref[...] = out_ref[:, PIV:]


def assemble(codes, index, recv, front):
    rows, order = front.shape
    vmem = pl.BlockSpec(memory_space=pltpu.VMEM)
    return pl.pallas_call(
        assemble_kernel,
        out_shape=(
            jax.ShapeDtypeStruct((rows, order - PIV), F32),
            jax.ShapeDtypeStruct((rows, HALF), F32),
            jax.ShapeDtypeStruct((rows, HALF), F32),
        ),
        in_specs=[pl.BlockSpec(memory_space=pltpu.SMEM)] * 2 + [vmem, vmem],
        out_specs=(vmem, vmem, vmem),
        scratch_shapes=[pltpu.VMEM((rows, order), F32)],
        compiler_params=pltpu.CompilerParams(vmem_limit_bytes=8 * 1024 * 1024),
        name="assemble",
    )(codes, index, recv, front)


def lane(x, c):
    return jnp.broadcast_to(x[:, c : c + 1], (8, B))


def sublane(x, t):
    return jnp.broadcast_to(x[t : t + 1, :], (8, B))


def chain(a_rows, e_rows, store, side):
    sub = lax.broadcasted_iota(jnp.int32, (8, B), 0)
    ahead = None
    for g in range(16):
        if g < len(side):
            side[g]()
        ra, re = a_rows[g], e_rows[g]
        base = 8 * g
        b = ahead or [lane(ra, base + t) for t in range(8)]
        more, far = g < 15, g < 14
        if more:
            na, ne = a_rows[g + 1], e_rows[g + 1]
            c = [lane(na, base + t) for t in range(8)]
            q = [lane(ra, base + 8 + t) for t in range(8)]
            ahead = [lane(na, base + 8 + t) for t in range(8)]
        ga, ge = ra, re
        fa, fe = ra, re
        rcps = []
        for t in range(8):
            r = 1.0 / sublane(b[t], t)
            rcps.append(r)
            m = b[t] * r
            mg = jnp.where(sub == t, 0.0, m)
            mf = jnp.where(sub > t, m, 0.0)
            pa, pe = sublane(fa, t), sublane(fe, t)
            if more:
                mn = c[t] * r
            for u in range(t + 1, 8):
                w = sublane(b[u], t)
                b[u] = b[u] - mg * w
                if more:
                    c[u] = c[u] - mn * w
            if more:
                for u in range(8):
                    w = sublane(q[u], t)
                    q[u] = q[u] - mf * w
                    ahead[u] = ahead[u] - mn * w
                na = na - mn * pa
                ne = ne - mn * pe
            fa = fa - mf * pa
            fe = fe - mf * pe
            if far:
                ga = ga - mg * pa
                ge = ge - mg * pe
        rc = rcps[0]
        for t in range(1, 8):
            rc = jnp.where(sub == t, rcps[t], rc)
        store(g, fa, fe, rc)
        if more:
            a_rows[g + 1], e_rows[g + 1] = na, ne
        if far:
            ga = ga * rc
            ge = ge * rc
            gab = [sublane(ga, t) for t in range(8)]
            geb = [sublane(ge, t) for t in range(8)]
            for i in range(g + 2, 16):
                acc_a, acc_e = a_rows[i], e_rows[i]
                for t in range(8):
                    cc = lane(a_rows[i], base + t)
                    acc_a = acc_a - cc * gab[t]
                    acc_e = acc_e - cc * geb[t]
                a_rows[i], e_rows[i] = acc_a, acc_e


def cat_blocks(a, b, c, d):
    return jnp.concatenate([jnp.concatenate([a, b], 1), jnp.concatenate([c, d], 1)], 0)


def factor_panels(k0, k1, a_ref, b_ref, vh, vl, v32, lh, ll, t_ref, lt_ref, dinv_ref,
                  rest_ref, u_ref, part_ref, e_ref):
    row0 = k0 * B
    na, nrhs = a_ref.shape[0], b_ref.shape[0]
    ri = lax.broadcasted_iota(jnp.int32, (8, B), 0)
    ci = lax.broadcasted_iota(jnp.int32, (8, B), 1)

    def settle(k):
        cols = pl.ds(pl.multiple_of(k * B, B), B)
        th, tl = split(t_ref[k])
        uh, ul = split(rest_ref[...])
        v = dot3_t(uh, ul, th, tl)
        v32[:, cols] = v
        vh[:, cols], vl[:, cols] = split(v)
        lrows = slice(row0, row0 + na)
        lh[lrows, cols], ll[lrows, cols] = split(v[:na] * dinv_ref[0:1, cols])

    def panel(k, _):
        kcols = pl.ds(pl.multiple_of(k * B, B), B)
        acols = pl.ds(pl.multiple_of((k - k0) * B, B), B)
        prev = jnp.maximum(k - 1, k0)
        after = jnp.minimum(k + 1, k1 - 1)
        nabs = pl.ds(pl.multiple_of(after * B, B), B)
        nloc = pl.ds(pl.multiple_of((after - k0) * B, B), B)
        a_rows = [u_ref[8 * i : 8 * i + 8, :] for i in range(16)]
        e_rows = [jnp.where(ri + 8 * i == ci, 1.0, 0.0) for i in range(16)]
        diag = []

        def store(g, fa, fe, rc):
            own = ri + 8 * g == ci
            diag.append(jnp.where(own, fa, 0.0))
            lt_ref[k, 8 * g : 8 * g + 8, :] = jnp.where(own, fa, jnp.where(ri + 8 * g < ci, fa * rc, 0.0))
            e_ref[8 * g : 8 * g + 8, :] = fe

        def update():
            prod = dot3_t(vh[...], vl[...], lh[kcols, :], ll[kcols, :])
            rest_ref[:na, :] = a_ref[:, acols] - prod[:na]
            rest_ref[na:, :] = b_ref[:, acols] - prod[na:]

        def partial():
            part_ref[...] = a_ref[nloc, nloc] - dot3_t(vh[nloc, :], vl[nloc, :], lh[nabs, :], ll[nabs, :])

        side = [lambda: settle(prev), update, partial]
        chain(a_rows, e_rows, store, side)
        total = diag[0]
        for g in range(1, 16):
            total = total + diag[g]
        dinv = 1.0 / jnp.sum(total, axis=0, keepdims=True)
        dinv_ref[0:1, kcols] = dinv
        t = e_ref[...]
        t_ref[k] = t
        th, tl = split(t)
        uh, ul = split(rest_ref[nloc, :])
        v = dot3_t(uh, ul, th, tl)
        v_h, v_l = split(v)
        l_h, l_l = split(v * dinv)
        u_ref[...] = part_ref[...] - dot3_t(v_h, v_l, l_h, l_l)
        return 0

    lax.fori_loop(k0, k1, panel, 0)
    settle(k1 - 1)


def first_kernel(idx_ref, y0_ref, y1_ref, y2_ref, y3_ref, b_ref,
                 vh, vl, lh, ll, t_ref, dinv_ref, y_ref, own_ref,
                 a_ref, v32, lt_ref, rest_ref, u_ref, part_ref, e_ref):
    me = idx_ref[0]
    ypos = lax.rem(me, 4)
    for d, ref in enumerate((y0_ref, y1_ref, y2_ref, y3_ref)):
        src = lax.rem(ypos + 4 - d, 4)
        for z in range(2):
            rows = pl.ds(pl.multiple_of((4 * z + src) * B, B), B)
            a_ref[rows, :] = ref[z * B : (z + 1) * B, :]
    for ref in (vh, vl, lh, ll, rest_ref, dinv_ref):
        ref[...] = jnp.zeros_like(ref)
    t_ref[0] = jnp.zeros((B, B), F32)
    u_ref[...] = a_ref[0:B, 0:B]
    factor_panels(0, NP // 2, a_ref, b_ref.at[:, pl.ds(0, HALF)], vh, vl, v32, lh, ll, t_ref, lt_ref, dinv_ref,
                  rest_ref, u_ref, part_ref, e_ref)
    nrhs = b_ref.shape[0]
    y_ref[...] = v32[PIV : PIV + nrhs, :]
    near = jnp.minimum(me, NP - 1)
    rows = pl.ds(pl.multiple_of(near * B, B), B)
    col = lax.broadcasted_iota(jnp.int32, (B, HALF), 1)
    own_ref[...] = jnp.where(col < near * B, v32[rows, :] * dinv_ref[0:1, :], 0.0)

    @pl.when(me < NP // 2)
    def _():
        own_ref[:, rows] = lt_ref[me].T


VMEM_SPEC = pl.BlockSpec(memory_space=pltpu.VMEM)


def first(index, parts, rhs):
    nrhs = rhs.shape[0]
    outs = (
        ((PIV + nrhs, HALF), BF16),
        ((PIV + nrhs, HALF), BF16),
        ((PIV, HALF), BF16),
        ((PIV, HALF), BF16),
        ((NP // 2, B, B), F32),
        ((8, HALF), F32),
        ((nrhs, HALF), F32),
        ((B, HALF), F32),
    )
    return pl.pallas_call(
        first_kernel,
        out_shape=tuple(jax.ShapeDtypeStruct(*o) for o in outs),
        in_specs=[pl.BlockSpec(memory_space=pltpu.SMEM)] + [VMEM_SPEC] * 5,
        out_specs=(VMEM_SPEC,) * len(outs),
        scratch_shapes=[
            pltpu.VMEM((PIV, HALF), F32),
            pltpu.VMEM((PIV + nrhs, HALF), F32),
            pltpu.VMEM((NP // 2, B, B), F32),
            pltpu.VMEM((PIV + nrhs, B), F32),
            pltpu.VMEM((B, B), F32),
            pltpu.VMEM((B, B), F32),
            pltpu.VMEM((B, B), F32),
        ],
        compiler_params=pltpu.CompilerParams(vmem_limit_bytes=20 * 1024 * 1024),
        cost_estimate=pl.CostEstimate(flops=2 * 10**10, bytes_accessed=2 * 10**7, transcendentals=0),
        name="first",
    )(index, *parts, rhs)


def second_kernel(idx_ref, p0_ref, p1_ref, p2_ref, p3_ref, vh0, vl0, lh0, ll0, t0, dinv0, y0, own0, b_ref,
                  lh, ll, t_ref, dinv_ref, y_ref, own_ref,
                  a_ref, vh, vl, v32, lt_ref, rest_ref, u_ref, part_ref, e_ref):
    me = idx_ref[0]
    nrhs = b_ref.shape[0]
    ypos = lax.rem(me, 4)
    for d, ref in enumerate((p0_ref, p1_ref, p2_ref, p3_ref)):
        rows = pl.ds(pl.multiple_of(lax.rem(ypos + 4 - d, 4) * B, B), B)
        a_ref[rows, :] = ref[:B, :]
    for ref, src in ((vh, vh0), (vl, vl0)):
        ref[:, :HALF] = src[HALF:, :]
        ref[:, HALF:] = jnp.zeros((ref.shape[0], HALF), BF16)
    for ref, src in ((lh, lh0), (ll, ll0)):
        ref[:, :HALF] = src[...]
        ref[:, HALF:] = jnp.zeros((ref.shape[0], HALF), BF16)
    dinv_ref[:, :HALF] = dinv0[...]
    dinv_ref[:, HALF:] = jnp.zeros((dinv_ref.shape[0], HALF), F32)
    t_ref[: NP // 2] = t0[...]
    t_ref[NP // 2] = jnp.zeros((B, B), F32)
    rest_ref[...] = jnp.zeros_like(rest_ref)
    u_ref[...] = a_ref[0:B, 0:B] - dot3_t(
        vh[0:B, :HALF], vl[0:B, :HALF], lh[HALF : HALF + B, :HALF], ll[HALF : HALF + B, :HALF]
    )
    factor_panels(NP // 2, NP, a_ref, b_ref.at[:, pl.ds(HALF, HALF)], vh, vl, v32, lh, ll, t_ref, lt_ref,
                  dinv_ref, rest_ref, u_ref, part_ref, e_ref)
    y_ref[:, :HALF] = y0[...]
    y_ref[:, HALF:] = v32[HALF : HALF + nrhs, HALF:]
    own_ref[:, :HALF] = own0[...]
    near = jnp.clip(me - NP // 2, 0, NP // 2 - 1)
    rows = pl.ds(pl.multiple_of(near * B, B), B)
    col = HALF + lax.broadcasted_iota(jnp.int32, (B, HALF), 1)
    own_ref[:, HALF:] = jnp.where(col < me * B, v32[rows, HALF:] * dinv_ref[0:1, HALF:], 0.0)

    @pl.when((me >= NP // 2) & (me < NP))
    def _():
        own_ref[:, pl.ds(pl.multiple_of(me * B, B), B)] = lt_ref[me].T


def second(index, parts, state, rhs):
    nrhs = rhs.shape[0]
    na = PIV - HALF
    outs = (
        ((PIV, PIV), BF16),
        ((PIV, PIV), BF16),
        ((NP, B, B), F32),
        ((8, PIV), F32),
        ((nrhs, PIV), F32),
        ((B, PIV), F32),
    )
    return pl.pallas_call(
        second_kernel,
        out_shape=tuple(jax.ShapeDtypeStruct(*o) for o in outs),
        in_specs=[pl.BlockSpec(memory_space=pltpu.SMEM)] + [VMEM_SPEC] * (len(parts) + len(state) + 1),
        out_specs=(VMEM_SPEC,) * len(outs),
        scratch_shapes=[
            pltpu.VMEM((na, na), F32),
            pltpu.VMEM((na + nrhs, PIV), BF16),
            pltpu.VMEM((na + nrhs, PIV), BF16),
            pltpu.VMEM((na + nrhs, PIV), F32),
            pltpu.VMEM((NP, B, B), F32),
            pltpu.VMEM((na + nrhs, B), F32),
            pltpu.VMEM((B, B), F32),
            pltpu.VMEM((B, B), F32),
            pltpu.VMEM((B, B), F32),
        ],
        compiler_params=pltpu.CompilerParams(vmem_limit_bytes=20 * 1024 * 1024),
        cost_estimate=pl.CostEstimate(flops=2 * 10**10, bytes_accessed=2 * 10**7, transcendentals=0),
        name="second",
    )(index, *parts, *state, rhs)


def third_kernel(idx_ref, nf_ref, nl_ref, ff_ref, fl_ref, lh, ll, t_ref, dinv_ref, y_ref, own_ref, tail_ref, b_ref,
                 fac_ref, eli_ref, a21, xh, xl, x32, wh, wl, sem):
    me = idx_ref[0]
    nrhs, order = b_ref.shape
    low = order - PIV
    ypos, zpos = lax.rem(me, 4), jnp.clip(me // 4 - 2, 0, 1)
    copies = []
    for n, (ref, z, c) in enumerate(((nf_ref, zpos, 0), (ff_ref, 1 - zpos, 0), (nl_ref, zpos, HALF), (fl_ref, 1 - zpos, HALF))):
        for d in range(4):
            rows = pl.ds(pl.multiple_of((4 * z + lax.rem(ypos + 4 - d, 4)) * B, B), B)
            copies.append(pltpu.make_async_copy(
                ref.at[pl.ds(d * B, B), :], a21.at[rows, pl.ds(c, HALF)], sem.at[4 * n + d]))
    for copy in copies:
        copy.start()

    inverses = []
    for i in range(NP // 2):
        t0h, t0l = split(t_ref[2 * i])
        t1h, t1l = split(t_ref[2 * i + 1])
        r1 = slice((2 * i + 1) * B, (2 * i + 2) * B)
        c0 = slice(2 * i * B, (2 * i + 1) * B)
        zh, zl = split(dot3_n(lh[r1, c0], ll[r1, c0], t0h, t0l))
        zh, zl = split(-dot3_n(t1h, t1l, zh, zl))
        zero = jnp.zeros((B, B), BF16)
        inverses.append((cat_blocks(t0h, zero, zh, t1h), cat_blocks(t0l, zero, zl, t1l)))
    for copy in copies:
        copy.wait()
    for i in range(NP // 2):
        pc, prev = slice(i * W2, (i + 1) * W2), slice(0, i * W2)
        u = a21[:, pc]
        if i:
            u = u - dot3_t(xh[:, prev], xl[:, prev], lh[pc, prev], ll[pc, prev])
        uh, ul = split(u)
        v = dot3_t(uh, ul, *inverses[i])
        x32[:, pc] = v
        xh[:, pc], xl[:, pc] = split(v)
        wh[:, pc], wl[:, pc] = split(v * dinv_ref[0:1, pc])

    y = y_ref[...]
    yh, yl = split(y)
    eli_ref[:, :PIV] = y
    mine = pl.ds(pl.multiple_of(jnp.maximum(me - NP, 0) * B, B), B)
    n = B + nrhs
    qh = jnp.concatenate([xh[mine, :], yh], 0)
    both = jnp.concatenate([qh, xl[mine, :], yl], 0)
    for c in range(low // W2):
        rows = slice(c * W2, (c + 1) * W2)
        dst = slice(PIV + c * W2, PIV + (c + 1) * W2)
        prod = dot_t(both, wh[rows, :])
        prod = prod[:n] + prod[n:] + dot_t(qh, wl[rows, :])
        row = me * B + lax.broadcasted_iota(jnp.int32, (B, W2), 0)
        col = PIV + c * W2 + lax.broadcasted_iota(jnp.int32, (B, W2), 1)
        fac_ref[:, dst] = jnp.where(row >= col, tail_ref[:, rows] - prod[:B], 0.0)
        eli_ref[:, dst] = b_ref[:, dst] - prod[B:]
    lower = me >= NP

    @pl.when(lower)
    def _():
        fac_ref[:, :PIV] = x32[mine, :] * dinv_ref[0:1, :]

    @pl.when(jnp.logical_not(lower))
    def _():
        fac_ref[:, :PIV] = own_ref[...]


def third(index, lower, state, tail, rhs):
    nrhs, order = rhs.shape
    low = order - PIV
    return pl.pallas_call(
        third_kernel,
        out_shape=(
            jax.ShapeDtypeStruct((B, order), F32),
            jax.ShapeDtypeStruct((nrhs, order), F32),
        ),
        in_specs=[pl.BlockSpec(memory_space=pltpu.SMEM)] + [VMEM_SPEC] * (len(lower) + len(state) + 2),
        out_specs=(VMEM_SPEC, VMEM_SPEC),
        scratch_shapes=[
            pltpu.VMEM((low, PIV), F32),
            pltpu.VMEM((low, PIV), BF16),
            pltpu.VMEM((low, PIV), BF16),
            pltpu.VMEM((low, PIV), F32),
            pltpu.VMEM((low, PIV), BF16),
            pltpu.VMEM((low, PIV), BF16),
            pltpu.SemaphoreType.DMA((16,)),
        ],
        compiler_params=pltpu.CompilerParams(vmem_limit_bytes=34 * 1024 * 1024),
        name="third",
    )(index, *lower, *state, tail, rhs)


def shift_y(x, d, zs=(0, 1, 2, 3)):
    return lax.ppermute(x, "front", [(4 * z + y, 4 * z + (y + d) % 4) for z in zs for y in range(4)])


def planes(x, pairs):
    return lax.ppermute(x, "front", [(4 * a + y, 4 * b + y) for a, b in pairs for y in range(4)])


def pick(z, *values):
    return jnp.where(z == 0, values[0], jnp.where(z == 1, values[1], jnp.where(z == 2, values[2], values[3])))


def ring_y(x, zs=(0, 1, 2, 3)):
    return [x] + [shift_y(x, d, zs) for d in (1, 2, 3)]


def local(front_matrix, child_blocks, child_target, child_count, shot_rhs):
    leaves, slots = child_blocks.shape[1:3]
    slot_ids = lax.broadcasted_iota(jnp.int32, (leaves, slots), 1)
    live_code = jnp.where(slot_ids < child_count[0][:, None], child_target[0], -1)
    code_rows = jnp.zeros((leaves, 8, B), F32).at[:, 0, :slots].set(live_code.astype(F32))
    payload = jnp.concatenate([child_blocks[0].reshape(leaves, slots * B, B), code_rows], axis=1)
    arrived = lax.all_to_all(payload, "leaf", split_axis=0, concat_axis=0, tiled=True)
    codes = arrived[:, slots * B, :slots].astype(jnp.int32)
    index = lax.axis_index("front").astype(jnp.int32).reshape(1)
    tail, early, late = assemble(codes, index, arrived, front_matrix[0])
    z = lax.axis_index("front") // 4
    rhs = shot_rhs[0]
    swap = planes(early, ((0, 1), (1, 0)))
    side = planes(early, ((1, 2), (0, 3)))
    cross = planes(early, ((0, 2), (1, 3)))
    near_last = jnp.concatenate(ring_y(late, (2, 3)), 0)
    early_parts = ring_y(jnp.concatenate([pick(z, early, swap, cross, side), pick(z, swap, early, side, cross)], 0))
    late_x, _ = lax.optimization_barrier((late, (swap, side, cross)))
    to0, to2, to3 = (planes(late_x, ((1, d),)) for d in (0, 2, 3))
    far_last = planes(near_last, ((2, 3), (3, 2)))
    mixed = jnp.concatenate([pick(z, to0, late_x, to2, to3), early], 0)
    late_parts = ring_y(mixed)
    state = first(index, early_parts, rhs)
    near_first = jnp.concatenate([part[B:] for part in late_parts], 0)
    near_first, _ = lax.optimization_barrier((near_first, state[6]))
    far_first = planes(near_first, ((2, 3), (3, 2)))
    state = second(index, late_parts, state, rhs)
    lower = [near_first, near_last, far_first, far_last]
    factored, eliminated = third(index, lower, state, tail, rhs)
    tail = eliminated[:, PIV:]
    tail = jnp.where(z < 2, planes(tail, ((2, 1), (3, 0))), tail)
    eliminated = jnp.concatenate([eliminated[:, :PIV], tail], 1)
    return factored[None], eliminated[None]


def solution(mesh):
    return jax.shard_map(
        local,
        mesh=mesh,
        in_specs=(
            P("leaf", "front", None),
            P(("leaf", "front"), None, None, None, None),
            P(("leaf", "front"), None, None),
            P(("leaf", "front"), None),
            P("leaf", None, None),
        ),
        out_specs=(P("leaf", "front", None), P("leaf", None, None)),
        check_vma=False,
    )
```

```python
import jax
import jax.numpy as jnp
from jax import lax
from jax.experimental import pallas as pl
from jax.experimental.pallas import tpu as pltpu
from jax.sharding import PartitionSpec as P

B = 128
PIV = 1024
NP = PIV // B
HALF = PIV // 2
W2 = 2 * B
F32 = jnp.float32
BF16 = jnp.bfloat16


def split(x):
    hi = x.astype(BF16)
    lo = (x - hi.astype(F32)).astype(BF16)
    return hi, lo


def dot_t(a, b):
    return lax.dot_general(a, b, (((1,), (1,)), ((), ())), preferred_element_type=F32)


def dot_n(a, b):
    return lax.dot_general(a, b, (((1,), (0,)), ((), ())), preferred_element_type=F32)


def dot3_t(ah, al, bh, bl):
    return dot_t(ah, bh) + dot_t(al, bh) + dot_t(ah, bl)


def dot3_n(ah, al, bh, bl):
    return dot_n(ah, bh) + dot_n(al, bh) + dot_n(ah, bl)


def assemble_kernel(code_ref, idx_ref, recv_ref, front_ref, tail_ref, early_ref, late_ref, out_ref):
    out_ref[...] = front_ref[...]
    for s in range(recv_ref.shape[0]):
        for j in range(code_ref.shape[1]):
            code = code_ref[s, j]

            @pl.when(code >= 0)
            def _(s=s, j=j, code=code):
                cols = pl.ds(pl.multiple_of(code * B, B), B)
                out_ref[:, cols] += recv_ref[s, j * B : (j + 1) * B, :]

    cols = pl.ds(pl.multiple_of(idx_ref[0] * B, B), B)
    square = out_ref[:, cols]
    row = lax.broadcasted_iota(jnp.int32, (B, B), 0)
    col = lax.broadcasted_iota(jnp.int32, (B, B), 1)
    out_ref[:, cols] = jnp.where(row >= col, square, square.T)
    early_ref[...] = out_ref[:, :HALF]
    late_ref[...] = out_ref[:, HALF:PIV]
    tail_ref[...] = out_ref[:, PIV:]


def assemble(codes, index, recv, front):
    rows, order = front.shape
    vmem = pl.BlockSpec(memory_space=pltpu.VMEM)
    return pl.pallas_call(
        assemble_kernel,
        out_shape=(
            jax.ShapeDtypeStruct((rows, order - PIV), F32),
            jax.ShapeDtypeStruct((rows, HALF), F32),
            jax.ShapeDtypeStruct((rows, HALF), F32),
        ),
        in_specs=[pl.BlockSpec(memory_space=pltpu.SMEM)] * 2 + [vmem, vmem],
        out_specs=(vmem, vmem, vmem),
        scratch_shapes=[pltpu.VMEM((rows, order), F32)],
        compiler_params=pltpu.CompilerParams(vmem_limit_bytes=8 * 1024 * 1024),
        name="assemble",
    )(codes, index, recv, front)


def lane(x, c):
    return jnp.broadcast_to(x[:, c : c + 1], (8, B))


def sublane(x, t):
    return jnp.broadcast_to(x[t : t + 1, :], (8, B))


def chain(a_rows, e_rows, store, side):
    sub = lax.broadcasted_iota(jnp.int32, (8, B), 0)
    ahead = None
    for g in range(16):
        if g < len(side):
            side[g]()
        ra, re = a_rows[g], e_rows[g]
        base = 8 * g
        b = ahead or [lane(ra, base + t) for t in range(8)]
        more, far = g < 15, g < 14
        if more:
            na, ne = a_rows[g + 1], e_rows[g + 1]
            c = [lane(na, base + t) for t in range(8)]
            q = [lane(ra, base + 8 + t) for t in range(8)]
            ahead = [lane(na, base + 8 + t) for t in range(8)]
        ga, ge = ra, re
        fa, fe = ra, re
        rcps = []
        for t in range(8):
            r = 1.0 / sublane(b[t], t)
            rcps.append(r)
            m = b[t] * r
            mg = jnp.where(sub == t, 0.0, m)
            mf = jnp.where(sub > t, m, 0.0)
            pa, pe = sublane(fa, t), sublane(fe, t)
            if more:
                mn = c[t] * r
            for u in range(t + 1, 8):
                w = sublane(b[u], t)
                b[u] = b[u] - mg * w
                if more:
                    c[u] = c[u] - mn * w
            if more:
                for u in range(8):
                    w = sublane(q[u], t)
                    q[u] = q[u] - mf * w
                    ahead[u] = ahead[u] - mn * w
                na = na - mn * pa
                ne = ne - mn * pe
            fa = fa - mf * pa
            fe = fe - mf * pe
            if far:
                ga = ga - mg * pa
                ge = ge - mg * pe
        rc = rcps[0]
        for t in range(1, 8):
            rc = jnp.where(sub == t, rcps[t], rc)
        store(g, fa, fe, rc)
        if more:
            a_rows[g + 1], e_rows[g + 1] = na, ne
        if far:
            ga = ga * rc
            ge = ge * rc
            gab = [sublane(ga, t) for t in range(8)]
            geb = [sublane(ge, t) for t in range(8)]
            for i in range(g + 2, 16):
                acc_a, acc_e = a_rows[i], e_rows[i]
                for t in range(8):
                    cc = lane(a_rows[i], base + t)
                    acc_a = acc_a - cc * gab[t]
                    acc_e = acc_e - cc * geb[t]
                a_rows[i], e_rows[i] = acc_a, acc_e


def cat_blocks(a, b, c, d):
    return jnp.concatenate([jnp.concatenate([a, b], 1), jnp.concatenate([c, d], 1)], 0)


def factor_panels(k0, k1, a_ref, b_ref, vh, vl, v32, lh, ll, t_ref, lt_ref, dinv_ref,
                  rest_ref, u_ref, part_ref, e_ref):
    row0 = k0 * B
    na, nrhs = a_ref.shape[0], b_ref.shape[0]
    ri = lax.broadcasted_iota(jnp.int32, (8, B), 0)
    ci = lax.broadcasted_iota(jnp.int32, (8, B), 1)

    def settle(k):
        cols = pl.ds(pl.multiple_of(k * B, B), B)
        th, tl = split(t_ref[k])
        uh, ul = split(rest_ref[...])
        v = dot3_t(uh, ul, th, tl)
        v32[:, cols] = v
        vh[:, cols], vl[:, cols] = split(v)
        lrows = slice(row0, row0 + na)
        lh[lrows, cols], ll[lrows, cols] = split(v[:na] * dinv_ref[0:1, cols])

    def panel(k, _):
        kcols = pl.ds(pl.multiple_of(k * B, B), B)
        acols = pl.ds(pl.multiple_of((k - k0) * B, B), B)
        prev = jnp.maximum(k - 1, k0)
        after = jnp.minimum(k + 1, k1 - 1)
        nabs = pl.ds(pl.multiple_of(after * B, B), B)
        nloc = pl.ds(pl.multiple_of((after - k0) * B, B), B)
        a_rows = [u_ref[8 * i : 8 * i + 8, :] for i in range(16)]
        e_rows = [jnp.where(ri + 8 * i == ci, 1.0, 0.0) for i in range(16)]
        diag = []

        def store(g, fa, fe, rc):
            own = ri + 8 * g == ci
            diag.append(jnp.where(own, fa, 0.0))
            lt_ref[k, 8 * g : 8 * g + 8, :] = jnp.where(own, fa, jnp.where(ri + 8 * g < ci, fa * rc, 0.0))
            e_ref[8 * g : 8 * g + 8, :] = fe

        def update():
            prod = dot3_t(vh[...], vl[...], lh[kcols, :], ll[kcols, :])
            rest_ref[:na, :] = a_ref[:, acols] - prod[:na]
            rest_ref[na:, :] = b_ref[:, acols] - prod[na:]

        def partial():
            part_ref[...] = a_ref[nloc, nloc] - dot3_t(vh[nloc, :], vl[nloc, :], lh[nabs, :], ll[nabs, :])

        side = [lambda: settle(prev), update, partial]
        chain(a_rows, e_rows, store, side)
        total = diag[0]
        for g in range(1, 16):
            total = total + diag[g]
        dinv = 1.0 / jnp.sum(total, axis=0, keepdims=True)
        dinv_ref[0:1, kcols] = dinv
        t = e_ref[...]
        t_ref[k] = t
        th, tl = split(t)
        uh, ul = split(rest_ref[nloc, :])
        v = dot3_t(uh, ul, th, tl)
        v_h, v_l = split(v)
        l_h, l_l = split(v * dinv)
        u_ref[...] = part_ref[...] - dot3_t(v_h, v_l, l_h, l_l)
        return 0

    lax.fori_loop(k0, k1, panel, 0)
    settle(k1 - 1)


def first_kernel(idx_ref, y0_ref, y1_ref, y2_ref, y3_ref, b_ref,
                 vh, vl, lh, ll, t_ref, dinv_ref, y_ref, own_ref,
                 a_ref, v32, lt_ref, rest_ref, u_ref, part_ref, e_ref):
    me = idx_ref[0]
    ypos = lax.rem(me, 4)
    for d, ref in enumerate((y0_ref, y1_ref, y2_ref, y3_ref)):
        src = lax.rem(ypos + 4 - d, 4)
        for z in range(2):
            rows = pl.ds(pl.multiple_of((4 * z + src) * B, B), B)
            a_ref[rows, :] = ref[z * B : (z + 1) * B, :]
    for ref in (vh, vl, lh, ll, rest_ref, dinv_ref):
        ref[...] = jnp.zeros_like(ref)
    t_ref[0] = jnp.zeros((B, B), F32)
    u_ref[...] = a_ref[0:B, 0:B]
    factor_panels(0, NP // 2, a_ref, b_ref.at[:, pl.ds(0, HALF)], vh, vl, v32, lh, ll, t_ref, lt_ref, dinv_ref,
                  rest_ref, u_ref, part_ref, e_ref)
    nrhs = b_ref.shape[0]
    y_ref[...] = v32[PIV : PIV + nrhs, :]
    near = jnp.minimum(me, NP - 1)
    rows = pl.ds(pl.multiple_of(near * B, B), B)
    col = lax.broadcasted_iota(jnp.int32, (B, HALF), 1)
    own_ref[...] = jnp.where(col < near * B, v32[rows, :] * dinv_ref[0:1, :], 0.0)

    @pl.when(me < NP // 2)
    def _():
        own_ref[:, rows] = lt_ref[me].T


VMEM_SPEC = pl.BlockSpec(memory_space=pltpu.VMEM)


def first(index, parts, rhs):
    nrhs = rhs.shape[0]
    outs = (
        ((PIV + nrhs, HALF), BF16),
        ((PIV + nrhs, HALF), BF16),
        ((PIV, HALF), BF16),
        ((PIV, HALF), BF16),
        ((NP // 2, B, B), F32),
        ((8, HALF), F32),
        ((nrhs, HALF), F32),
        ((B, HALF), F32),
    )
    return pl.pallas_call(
        first_kernel,
        out_shape=tuple(jax.ShapeDtypeStruct(*o) for o in outs),
        in_specs=[pl.BlockSpec(memory_space=pltpu.SMEM)] + [VMEM_SPEC] * 5,
        out_specs=(VMEM_SPEC,) * len(outs),
        scratch_shapes=[
            pltpu.VMEM((PIV, HALF), F32),
            pltpu.VMEM((PIV + nrhs, HALF), F32),
            pltpu.VMEM((NP // 2, B, B), F32),
            pltpu.VMEM((PIV + nrhs, B), F32),
            pltpu.VMEM((B, B), F32),
            pltpu.VMEM((B, B), F32),
            pltpu.VMEM((B, B), F32),
        ],
        compiler_params=pltpu.CompilerParams(vmem_limit_bytes=20 * 1024 * 1024),
        cost_estimate=pl.CostEstimate(flops=2 * 10**10, bytes_accessed=2 * 10**7, transcendentals=0),
        name="first",
    )(index, *parts, rhs)


def second_kernel(idx_ref, p0_ref, p1_ref, p2_ref, p3_ref, vh0, vl0, lh0, ll0, t0, dinv0, y0, own0, b_ref,
                  lh, ll, t_ref, dinv_ref, y_ref, own_ref,
                  a_ref, vh, vl, v32, lt_ref, rest_ref, u_ref, part_ref, e_ref):
    me = idx_ref[0]
    nrhs = b_ref.shape[0]
    ypos = lax.rem(me, 4)
    for d, ref in enumerate((p0_ref, p1_ref, p2_ref, p3_ref)):
        rows = pl.ds(pl.multiple_of(lax.rem(ypos + 4 - d, 4) * B, B), B)
        a_ref[rows, :] = ref[:B, :]
    for ref, src in ((vh, vh0), (vl, vl0)):
        ref[:, :HALF] = src[HALF:, :]
        ref[:, HALF:] = jnp.zeros((ref.shape[0], HALF), BF16)
    for ref, src in ((lh, lh0), (ll, ll0)):
        ref[:, :HALF] = src[...]
        ref[:, HALF:] = jnp.zeros((ref.shape[0], HALF), BF16)
    dinv_ref[:, :HALF] = dinv0[...]
    dinv_ref[:, HALF:] = jnp.zeros((dinv_ref.shape[0], HALF), F32)
    t_ref[: NP // 2] = t0[...]
    t_ref[NP // 2] = jnp.zeros((B, B), F32)
    rest_ref[...] = jnp.zeros_like(rest_ref)
    u_ref[...] = a_ref[0:B, 0:B] - dot3_t(
        vh[0:B, :HALF], vl[0:B, :HALF], lh[HALF : HALF + B, :HALF], ll[HALF : HALF + B, :HALF]
    )
    factor_panels(NP // 2, NP, a_ref, b_ref.at[:, pl.ds(HALF, HALF)], vh, vl, v32, lh, ll, t_ref, lt_ref,
                  dinv_ref, rest_ref, u_ref, part_ref, e_ref)
    y_ref[:, :HALF] = y0[...]
    y_ref[:, HALF:] = v32[HALF : HALF + nrhs, HALF:]
    own_ref[:, :HALF] = own0[...]
    near = jnp.clip(me - NP // 2, 0, NP // 2 - 1)
    rows = pl.ds(pl.multiple_of(near * B, B), B)
    col = HALF + lax.broadcasted_iota(jnp.int32, (B, HALF), 1)
    own_ref[:, HALF:] = jnp.where(col < me * B, v32[rows, HALF:] * dinv_ref[0:1, HALF:], 0.0)

    @pl.when((me >= NP // 2) & (me < NP))
    def _():
        own_ref[:, pl.ds(pl.multiple_of(me * B, B), B)] = lt_ref[me].T


def second(index, parts, state, rhs):
    nrhs = rhs.shape[0]
    na = PIV - HALF
    outs = (
        ((PIV, PIV), BF16),
        ((PIV, PIV), BF16),
        ((NP, B, B), F32),
        ((8, PIV), F32),
        ((nrhs, PIV), F32),
        ((B, PIV), F32),
    )
    return pl.pallas_call(
        second_kernel,
        out_shape=tuple(jax.ShapeDtypeStruct(*o) for o in outs),
        in_specs=[pl.BlockSpec(memory_space=pltpu.SMEM)] + [VMEM_SPEC] * (len(parts) + len(state) + 1),
        out_specs=(VMEM_SPEC,) * len(outs),
        scratch_shapes=[
            pltpu.VMEM((na, na), F32),
            pltpu.VMEM((na + nrhs, PIV), BF16),
            pltpu.VMEM((na + nrhs, PIV), BF16),
            pltpu.VMEM((na + nrhs, PIV), F32),
            pltpu.VMEM((NP, B, B), F32),
            pltpu.VMEM((na + nrhs, B), F32),
            pltpu.VMEM((B, B), F32),
            pltpu.VMEM((B, B), F32),
            pltpu.VMEM((B, B), F32),
        ],
        compiler_params=pltpu.CompilerParams(vmem_limit_bytes=20 * 1024 * 1024),
        cost_estimate=pl.CostEstimate(flops=2 * 10**10, bytes_accessed=2 * 10**7, transcendentals=0),
        name="second",
    )(index, *parts, *state, rhs)


def place_rows(me, near_ref, far_ref, a21, sem):
    ypos, zpos = lax.rem(me, 4), jnp.clip(me // 4 - 2, 0, 1)
    copies = []
    for n, (ref, z) in enumerate(((near_ref, zpos), (far_ref, 1 - zpos))):
        for d in range(4):
            rows = pl.ds(pl.multiple_of((4 * z + lax.rem(ypos + 4 - d, 4)) * B, B), B)
            copies.append(pltpu.make_async_copy(ref.at[pl.ds(d * B, B), :], a21.at[rows, :], sem.at[4 * n + d]))
    for copy in copies:
        copy.start()
    return copies


def pair_inverse(i, lh, ll, t_ref):
    t0h, t0l = split(t_ref[2 * i])
    t1h, t1l = split(t_ref[2 * i + 1])
    r1 = slice((2 * i + 1) * B, (2 * i + 2) * B)
    c0 = slice(2 * i * B, (2 * i + 1) * B)
    zh, zl = split(dot3_n(lh[r1, c0], ll[r1, c0], t0h, t0l))
    zh, zl = split(-dot3_n(t1h, t1l, zh, zl))
    zero = jnp.zeros((B, B), BF16)
    return cat_blocks(t0h, zero, zh, t1h), cat_blocks(t0l, zero, zl, t1l)


def solve_half(half, inverses, a21, known, lh, ll, dinv_ref, xh, xl, x32, wh, wl):
    base = half * HALF
    for i in range(2):
        lc, pc = slice(i * W2, (i + 1) * W2), slice(base + i * W2, base + (i + 1) * W2)
        u = a21[:, lc]
        if known:
            u = u - dot3_t(known[0][...], known[1][...], lh[pc, :HALF], ll[pc, :HALF])
        if i:
            u = u - dot3_t(xh[:, :W2], xl[:, :W2], lh[pc, base : base + W2], ll[pc, base : base + W2])
        uh, ul = split(u)
        v = dot3_t(uh, ul, *inverses[i])
        x32[:, lc] = v
        xh[:, lc], xl[:, lc] = split(v)
        wh[:, lc], wl[:, lc] = split(v * dinv_ref[0:1, pc])


def third_kernel(idx_ref, near_ref, far_ref, lh, ll, t_ref, dinv_ref, xh, xl, wh, wl, own_ref, a21, x32, sem):
    me = idx_ref[0]
    copies = place_rows(me, near_ref, far_ref, a21, sem)
    inverses = [pair_inverse(i, lh, ll, t_ref) for i in range(2)]
    for copy in copies:
        copy.wait()
    solve_half(0, inverses, a21, None, lh, ll, dinv_ref, xh, xl, x32, wh, wl)
    mine = pl.ds(pl.multiple_of(jnp.maximum(me - NP, 0) * B, B), B)
    own_ref[...] = x32[mine, :] * dinv_ref[0:1, :HALF]


def third(index, near, far, state):
    low = 2 * near.shape[0]
    outs = (((low, HALF), BF16),) * 4 + (((B, HALF), F32),)
    return pl.pallas_call(
        third_kernel,
        out_shape=tuple(jax.ShapeDtypeStruct(*o) for o in outs),
        in_specs=[pl.BlockSpec(memory_space=pltpu.SMEM)] + [VMEM_SPEC] * 6,
        out_specs=(VMEM_SPEC,) * len(outs),
        scratch_shapes=[
            pltpu.VMEM((low, HALF), F32),
            pltpu.VMEM((low, HALF), F32),
            pltpu.SemaphoreType.DMA((8,)),
        ],
        compiler_params=pltpu.CompilerParams(vmem_limit_bytes=16 * 1024 * 1024),
        cost_estimate=pl.CostEstimate(flops=5 * 10**9, bytes_accessed=10**7, transcendentals=0),
        name="third",
    )(index, near, far, *state[:4])


def fourth_kernel(idx_ref, near_ref, far_ref, xh0, xl0, wh0, wl0, lown_ref, lh, ll, t_ref, dinv_ref, y_ref, own_ref,
                  tail_ref, b_ref, fac_ref, eli_ref, a21, xh, xl, x32, wh, wl, sem):
    me = idx_ref[0]
    nrhs, order = b_ref.shape
    low = order - PIV
    copies = place_rows(me, near_ref, far_ref, a21, sem)
    inverses = [pair_inverse(i, lh, ll, t_ref) for i in range(2, 4)]
    for copy in copies:
        copy.wait()
    solve_half(1, inverses, a21, (xh0, xl0), lh, ll, dinv_ref, xh, xl, x32, wh, wl)
    y = y_ref[...]
    yh, yl = split(y)
    eli_ref[:, :PIV] = y
    mine = pl.ds(pl.multiple_of(jnp.maximum(me - NP, 0) * B, B), B)
    n = B + nrhs
    hi = [jnp.concatenate([x[mine, :], yh[:, c]], 0) for x, c in ((xh0, slice(0, HALF)), (xh, slice(HALF, PIV)))]
    lo = [jnp.concatenate([x[mine, :], yl[:, c]], 0) for x, c in ((xl0, slice(0, HALF)), (xl, slice(HALF, PIV)))]
    both = [jnp.concatenate([h, m], 0) for h, m in zip(hi, lo)]
    for c in range(low // W2):
        rows = slice(c * W2, (c + 1) * W2)
        dst = slice(PIV + c * W2, PIV + (c + 1) * W2)
        prod = dot_t(both[0], wh0[rows, :]) + dot_t(both[1], wh[rows, :])
        prod = prod[:n] + prod[n:] + dot_t(hi[0], wl0[rows, :]) + dot_t(hi[1], wl[rows, :])
        row = me * B + lax.broadcasted_iota(jnp.int32, (B, W2), 0)
        col = PIV + c * W2 + lax.broadcasted_iota(jnp.int32, (B, W2), 1)
        fac_ref[:, dst] = jnp.where(row >= col, tail_ref[:, rows] - prod[:B], 0.0)
        eli_ref[:, dst] = b_ref[:, dst] - prod[B:]
    lower = me >= NP

    @pl.when(lower)
    def _():
        fac_ref[:, :HALF] = lown_ref[...]
        fac_ref[:, HALF:PIV] = x32[mine, :] * dinv_ref[0:1, HALF:]

    @pl.when(jnp.logical_not(lower))
    def _():
        fac_ref[:, :PIV] = own_ref[...]


def fourth(index, near, far, solved, state, tail, rhs):
    nrhs, order = rhs.shape
    low = order - PIV
    return pl.pallas_call(
        fourth_kernel,
        out_shape=(
            jax.ShapeDtypeStruct((B, order), F32),
            jax.ShapeDtypeStruct((nrhs, order), F32),
        ),
        in_specs=[pl.BlockSpec(memory_space=pltpu.SMEM)] + [VMEM_SPEC] * (len(solved) + len(state) + 4),
        out_specs=(VMEM_SPEC, VMEM_SPEC),
        scratch_shapes=[
            pltpu.VMEM((low, HALF), F32),
            pltpu.VMEM((low, HALF), BF16),
            pltpu.VMEM((low, HALF), BF16),
            pltpu.VMEM((low, HALF), F32),
            pltpu.VMEM((low, HALF), BF16),
            pltpu.VMEM((low, HALF), BF16),
            pltpu.SemaphoreType.DMA((8,)),
        ],
        compiler_params=pltpu.CompilerParams(vmem_limit_bytes=24 * 1024 * 1024),
        name="fourth",
    )(index, near, far, *solved, *state, tail, rhs)


def shift_y(x, d, zs=(0, 1, 2, 3)):
    return lax.ppermute(x, "front", [(4 * z + y, 4 * z + (y + d) % 4) for z in zs for y in range(4)])


def planes(x, pairs):
    return lax.ppermute(x, "front", [(4 * a + y, 4 * b + y) for a, b in pairs for y in range(4)])


def pick(z, *values):
    return jnp.where(z == 0, values[0], jnp.where(z == 1, values[1], jnp.where(z == 2, values[2], values[3])))


def ring_y(x, zs=(0, 1, 2, 3)):
    return [x] + [shift_y(x, d, zs) for d in (1, 2, 3)]


def local(front_matrix, child_blocks, child_target, child_count, shot_rhs):
    leaves, slots = child_blocks.shape[1:3]
    slot_ids = lax.broadcasted_iota(jnp.int32, (leaves, slots), 1)
    live_code = jnp.where(slot_ids < child_count[0][:, None], child_target[0], -1)
    code_rows = jnp.zeros((leaves, 8, B), F32).at[:, 0, :slots].set(live_code.astype(F32))
    payload = jnp.concatenate([child_blocks[0].reshape(leaves, slots * B, B), code_rows], axis=1)
    arrived = lax.all_to_all(payload, "leaf", split_axis=0, concat_axis=0, tiled=True)
    codes = arrived[:, slots * B, :slots].astype(jnp.int32)
    index = lax.axis_index("front").astype(jnp.int32).reshape(1)
    tail, early, late = assemble(codes, index, arrived, front_matrix[0])
    z = lax.axis_index("front") // 4
    rhs = shot_rhs[0]
    swap = planes(early, ((0, 1), (1, 0)))
    side = planes(early, ((1, 2), (0, 3)))
    cross = planes(early, ((0, 2), (1, 3)))
    near_first = jnp.concatenate(ring_y(early, (2, 3)), 0)
    early_parts = ring_y(jnp.concatenate([pick(z, early, swap, cross, side), pick(z, swap, early, side, cross)], 0))
    late_x, _ = lax.optimization_barrier((late, (swap, side, cross)))
    to0, to2, to3 = (planes(late_x, ((1, d),)) for d in (0, 2, 3))
    far_first = planes(near_first, ((2, 3), (3, 2)))
    mixed = jnp.concatenate([pick(z, to0, late_x, to2, to3), late], 0)
    late_parts = ring_y(mixed)
    state = first(index, early_parts, rhs)
    near_last = jnp.concatenate([part[B:] for part in late_parts], 0)
    near_last, _ = lax.optimization_barrier((near_last, state[6]))
    far_last = planes(near_last, ((2, 3), (3, 2)))
    state = second(index, late_parts, state, rhs)
    solved = third(index, near_first, far_first, state)
    factored, eliminated = fourth(index, near_last, far_last, solved, state, tail, rhs)
    tail = eliminated[:, PIV:]
    tail = jnp.where(z < 2, planes(tail, ((2, 1), (3, 0))), tail)
    eliminated = jnp.concatenate([eliminated[:, :PIV], tail], 1)
    return factored[None], eliminated[None]


def solution(mesh):
    return jax.shard_map(
        local,
        mesh=mesh,
        in_specs=(
            P("leaf", "front", None),
            P(("leaf", "front"), None, None, None, None),
            P(("leaf", "front"), None, None),
            P(("leaf", "front"), None),
            P("leaf", None, None),
        ),
        out_specs=(P("leaf", "front", None), P("leaf", None, None)),
        check_vma=False,
    )
```

```python
import jax
import jax.numpy as jnp
from jax import lax
from jax.experimental import pallas as pl
from jax.experimental.pallas import tpu as pltpu
from jax.sharding import PartitionSpec as P

B = 128
PIV = 1024
NP = PIV // B
HALF = PIV // 2
W2 = 2 * B
AHEAD = HALF + B
F32 = jnp.float32
BF16 = jnp.bfloat16


def split(x):
    hi = x.astype(BF16)
    lo = (x - hi.astype(F32)).astype(BF16)
    return hi, lo


def dot_t(a, b):
    return lax.dot_general(a, b, (((1,), (1,)), ((), ())), preferred_element_type=F32)


def dot_n(a, b):
    return lax.dot_general(a, b, (((1,), (0,)), ((), ())), preferred_element_type=F32)


def dot3_t(ah, al, bh, bl):
    return dot_t(ah, bh) + dot_t(al, bh) + dot_t(ah, bl)


def dot3_n(ah, al, bh, bl):
    return dot_n(ah, bh) + dot_n(al, bh) + dot_n(ah, bl)


def assemble_kernel(code_ref, idx_ref, recv_ref, front_ref, tail_ref, early_ref, late_ref, ahead_ref, out_ref):
    out_ref[...] = front_ref[...]
    for s in range(recv_ref.shape[0]):
        for j in range(code_ref.shape[1]):
            code = code_ref[s, j]

            @pl.when(code >= 0)
            def _(s=s, j=j, code=code):
                cols = pl.ds(pl.multiple_of(code * B, B), B)
                out_ref[:, cols] += recv_ref[s, j * B : (j + 1) * B, :]

    cols = pl.ds(pl.multiple_of(idx_ref[0] * B, B), B)
    square = out_ref[:, cols]
    row = lax.broadcasted_iota(jnp.int32, (B, B), 0)
    col = lax.broadcasted_iota(jnp.int32, (B, B), 1)
    out_ref[:, cols] = jnp.where(row >= col, square, square.T)
    early_ref[...] = out_ref[:, :HALF]
    late_ref[...] = out_ref[:, HALF:PIV]
    ahead_ref[...] = out_ref[:, :AHEAD]
    tail_ref[...] = out_ref[:, PIV:]


def assemble(codes, index, recv, front):
    rows, order = front.shape
    vmem = pl.BlockSpec(memory_space=pltpu.VMEM)
    return pl.pallas_call(
        assemble_kernel,
        out_shape=(
            jax.ShapeDtypeStruct((rows, order - PIV), F32),
            jax.ShapeDtypeStruct((rows, HALF), F32),
            jax.ShapeDtypeStruct((rows, HALF), F32),
            jax.ShapeDtypeStruct((rows, AHEAD), F32),
        ),
        in_specs=[pl.BlockSpec(memory_space=pltpu.SMEM)] * 2 + [vmem, vmem],
        out_specs=(vmem, vmem, vmem, vmem),
        scratch_shapes=[pltpu.VMEM((rows, order), F32)],
        compiler_params=pltpu.CompilerParams(vmem_limit_bytes=8 * 1024 * 1024),
        name="assemble",
    )(codes, index, recv, front)


def lane(x, c):
    return jnp.broadcast_to(x[:, c : c + 1], (8, B))


def sublane(x, t):
    return jnp.broadcast_to(x[t : t + 1, :], (8, B))


def chain(a_rows, e_rows, store, side):
    sub = lax.broadcasted_iota(jnp.int32, (8, B), 0)
    ahead = None
    for g in range(16):
        if g < len(side):
            side[g]()
        ra, re = a_rows[g], e_rows[g]
        base = 8 * g
        b = ahead or [lane(ra, base + t) for t in range(8)]
        more, far = g < 15, g < 14
        if more:
            na, ne = a_rows[g + 1], e_rows[g + 1]
            c = [lane(na, base + t) for t in range(8)]
            q = [lane(ra, base + 8 + t) for t in range(8)]
            ahead = [lane(na, base + 8 + t) for t in range(8)]
        ga, ge = ra, re
        fa, fe = ra, re
        rcps = []
        for t in range(8):
            r = 1.0 / sublane(b[t], t)
            rcps.append(r)
            m = b[t] * r
            mg = jnp.where(sub == t, 0.0, m)
            mf = jnp.where(sub > t, m, 0.0)
            pa, pe = sublane(fa, t), sublane(fe, t)
            if more:
                mn = c[t] * r
            for u in range(t + 1, 8):
                w = sublane(b[u], t)
                b[u] = b[u] - mg * w
                if more:
                    c[u] = c[u] - mn * w
            if more:
                for u in range(8):
                    w = sublane(q[u], t)
                    q[u] = q[u] - mf * w
                    ahead[u] = ahead[u] - mn * w
                na = na - mn * pa
                ne = ne - mn * pe
            fa = fa - mf * pa
            fe = fe - mf * pe
            if far:
                ga = ga - mg * pa
                ge = ge - mg * pe
        rc = rcps[0]
        for t in range(1, 8):
            rc = jnp.where(sub == t, rcps[t], rc)
        store(g, fa, fe, rc)
        if more:
            a_rows[g + 1], e_rows[g + 1] = na, ne
        if far:
            ga = ga * rc
            ge = ge * rc
            gab = [sublane(ga, t) for t in range(8)]
            geb = [sublane(ge, t) for t in range(8)]
            for i in range(g + 2, 16):
                acc_a, acc_e = a_rows[i], e_rows[i]
                for t in range(8):
                    cc = lane(a_rows[i], base + t)
                    acc_a = acc_a - cc * gab[t]
                    acc_e = acc_e - cc * geb[t]
                a_rows[i], e_rows[i] = acc_a, acc_e


def cat_blocks(a, b, c, d):
    return jnp.concatenate([jnp.concatenate([a, b], 1), jnp.concatenate([c, d], 1)], 0)


def factor_panels(k0, k1, a_ref, b_ref, vh, vl, v32, lh, ll, t_ref, lt_ref, dinv_ref,
                  rest_ref, u_ref, part_ref, e_ref):
    row0 = k0 * B
    na, nrhs = a_ref.shape[0], b_ref.shape[0]
    ri = lax.broadcasted_iota(jnp.int32, (8, B), 0)
    ci = lax.broadcasted_iota(jnp.int32, (8, B), 1)

    def settle(k):
        cols = pl.ds(pl.multiple_of(k * B, B), B)
        th, tl = split(t_ref[k])
        uh, ul = split(rest_ref[...])
        v = dot3_t(uh, ul, th, tl)
        v32[:, cols] = v
        vh[:, cols], vl[:, cols] = split(v)
        lrows = slice(row0, row0 + na)
        lh[lrows, cols], ll[lrows, cols] = split(v[:na] * dinv_ref[0:1, cols])

    def panel(k, _):
        kcols = pl.ds(pl.multiple_of(k * B, B), B)
        acols = pl.ds(pl.multiple_of((k - k0) * B, B), B)
        prev = jnp.maximum(k - 1, k0)
        after = jnp.minimum(k + 1, k1 - 1)
        nabs = pl.ds(pl.multiple_of(after * B, B), B)
        nloc = pl.ds(pl.multiple_of((after - k0) * B, B), B)
        a_rows = [u_ref[8 * i : 8 * i + 8, :] for i in range(16)]
        e_rows = [jnp.where(ri + 8 * i == ci, 1.0, 0.0) for i in range(16)]
        diag = []

        def store(g, fa, fe, rc):
            own = ri + 8 * g == ci
            diag.append(jnp.where(own, fa, 0.0))
            lt_ref[k, 8 * g : 8 * g + 8, :] = jnp.where(own, fa, jnp.where(ri + 8 * g < ci, fa * rc, 0.0))
            e_ref[8 * g : 8 * g + 8, :] = fe

        def update():
            prod = dot3_t(vh[...], vl[...], lh[kcols, :], ll[kcols, :])
            rest_ref[:na, :] = a_ref[:, acols] - prod[:na]
            rest_ref[na:, :] = b_ref[:, acols] - prod[na:]

        def partial():
            part_ref[...] = a_ref[nloc, nloc] - dot3_t(vh[nloc, :], vl[nloc, :], lh[nabs, :], ll[nabs, :])

        side = [lambda: settle(prev), update, partial]
        chain(a_rows, e_rows, store, side)
        total = diag[0]
        for g in range(1, 16):
            total = total + diag[g]
        dinv = 1.0 / jnp.sum(total, axis=0, keepdims=True)
        dinv_ref[0:1, kcols] = dinv
        t = e_ref[...]
        t_ref[k] = t
        th, tl = split(t)
        uh, ul = split(rest_ref[nloc, :])
        v = dot3_t(uh, ul, th, tl)
        v_h, v_l = split(v)
        l_h, l_l = split(v * dinv)
        u_ref[...] = part_ref[...] - dot3_t(v_h, v_l, l_h, l_l)
        return 0

    lax.fori_loop(k0, k1, panel, 0)
    settle(k1 - 1)


def first_kernel(idx_ref, y0_ref, y1_ref, y2_ref, y3_ref, b_ref,
                 vh, vl, lh, ll, t_ref, dinv_ref, y_ref, own_ref,
                 a_ref, v32, lt_ref, rest_ref, u_ref, part_ref, e_ref):
    me = idx_ref[0]
    ypos = lax.rem(me, 4)
    for d, ref in enumerate((y0_ref, y1_ref, y2_ref, y3_ref)):
        src = lax.rem(ypos + 4 - d, 4)
        for z in range(2):
            rows = pl.ds(pl.multiple_of((4 * z + src) * B, B), B)
            a_ref[rows, :] = ref[z * B : (z + 1) * B, :]
    for ref in (vh, vl, lh, ll, rest_ref, dinv_ref):
        ref[...] = jnp.zeros_like(ref)
    t_ref[0] = jnp.zeros((B, B), F32)
    u_ref[...] = a_ref[0:B, 0:B]
    factor_panels(0, NP // 2, a_ref, b_ref.at[:, pl.ds(0, HALF)], vh, vl, v32, lh, ll, t_ref, lt_ref, dinv_ref,
                  rest_ref, u_ref, part_ref, e_ref)
    nrhs = b_ref.shape[0]
    y_ref[...] = v32[PIV : PIV + nrhs, :]
    near = jnp.minimum(me, NP - 1)
    rows = pl.ds(pl.multiple_of(near * B, B), B)
    col = lax.broadcasted_iota(jnp.int32, (B, HALF), 1)
    own_ref[...] = jnp.where(col < near * B, v32[rows, :] * dinv_ref[0:1, :], 0.0)

    @pl.when(me < NP // 2)
    def _():
        own_ref[:, rows] = lt_ref[me].T


VMEM_SPEC = pl.BlockSpec(memory_space=pltpu.VMEM)


def first(index, parts, rhs):
    nrhs = rhs.shape[0]
    outs = (
        ((PIV + nrhs, HALF), BF16),
        ((PIV + nrhs, HALF), BF16),
        ((PIV, HALF), BF16),
        ((PIV, HALF), BF16),
        ((NP // 2, B, B), F32),
        ((8, HALF), F32),
        ((nrhs, HALF), F32),
        ((B, HALF), F32),
    )
    return pl.pallas_call(
        first_kernel,
        out_shape=tuple(jax.ShapeDtypeStruct(*o) for o in outs),
        in_specs=[pl.BlockSpec(memory_space=pltpu.SMEM)] + [VMEM_SPEC] * 5,
        out_specs=(VMEM_SPEC,) * len(outs),
        scratch_shapes=[
            pltpu.VMEM((PIV, HALF), F32),
            pltpu.VMEM((PIV + nrhs, HALF), F32),
            pltpu.VMEM((NP // 2, B, B), F32),
            pltpu.VMEM((PIV + nrhs, B), F32),
            pltpu.VMEM((B, B), F32),
            pltpu.VMEM((B, B), F32),
            pltpu.VMEM((B, B), F32),
        ],
        compiler_params=pltpu.CompilerParams(vmem_limit_bytes=20 * 1024 * 1024),
        cost_estimate=pl.CostEstimate(flops=2 * 10**10, bytes_accessed=2 * 10**7, transcendentals=0),
        name="first",
    )(index, *parts, rhs)


def second_kernel(idx_ref, p0_ref, p1_ref, p2_ref, p3_ref, vh0, vl0, lh0, ll0, t0, dinv0, y0, own0, b_ref,
                  lh, ll, t_ref, dinv_ref, y_ref, own_ref,
                  a_ref, vh, vl, v32, lt_ref, rest_ref, u_ref, part_ref, e_ref):
    me = idx_ref[0]
    nrhs = b_ref.shape[0]
    ypos = lax.rem(me, 4)
    for d, ref in enumerate((p0_ref, p1_ref, p2_ref, p3_ref)):
        rows = pl.ds(pl.multiple_of(lax.rem(ypos + 4 - d, 4) * B, B), B)
        a_ref[rows, :] = ref[:, :HALF]
    for ref, src in ((vh, vh0), (vl, vl0)):
        ref[:, :HALF] = src[HALF:, :]
        ref[:, HALF:] = jnp.zeros((ref.shape[0], HALF), BF16)
    for ref, src in ((lh, lh0), (ll, ll0)):
        ref[:, :HALF] = src[...]
        ref[:, HALF:] = jnp.zeros((ref.shape[0], HALF), BF16)
    dinv_ref[:, :HALF] = dinv0[...]
    dinv_ref[:, HALF:] = jnp.zeros((dinv_ref.shape[0], HALF), F32)
    t_ref[: NP // 2] = t0[...]
    t_ref[NP // 2] = jnp.zeros((B, B), F32)
    rest_ref[...] = jnp.zeros_like(rest_ref)
    u_ref[...] = a_ref[0:B, 0:B] - dot3_t(
        vh[0:B, :HALF], vl[0:B, :HALF], lh[HALF : HALF + B, :HALF], ll[HALF : HALF + B, :HALF]
    )
    factor_panels(NP // 2, NP, a_ref, b_ref.at[:, pl.ds(HALF, HALF)], vh, vl, v32, lh, ll, t_ref, lt_ref,
                  dinv_ref, rest_ref, u_ref, part_ref, e_ref)
    y_ref[:, :HALF] = y0[...]
    y_ref[:, HALF:] = v32[HALF : HALF + nrhs, HALF:]
    own_ref[:, :HALF] = own0[...]
    near = jnp.clip(me - NP // 2, 0, NP // 2 - 1)
    rows = pl.ds(pl.multiple_of(near * B, B), B)
    col = HALF + lax.broadcasted_iota(jnp.int32, (B, HALF), 1)
    own_ref[:, HALF:] = jnp.where(col < me * B, v32[rows, HALF:] * dinv_ref[0:1, HALF:], 0.0)

    @pl.when((me >= NP // 2) & (me < NP))
    def _():
        own_ref[:, pl.ds(pl.multiple_of(me * B, B), B)] = lt_ref[me].T


def second(index, parts, state, rhs):
    nrhs = rhs.shape[0]
    na = PIV - HALF
    outs = (
        ((PIV, PIV), BF16),
        ((PIV, PIV), BF16),
        ((NP, B, B), F32),
        ((8, PIV), F32),
        ((nrhs, PIV), F32),
        ((B, PIV), F32),
    )
    return pl.pallas_call(
        second_kernel,
        out_shape=tuple(jax.ShapeDtypeStruct(*o) for o in outs),
        in_specs=[pl.BlockSpec(memory_space=pltpu.SMEM)] + [VMEM_SPEC] * (len(parts) + len(state) + 1),
        out_specs=(VMEM_SPEC,) * len(outs),
        scratch_shapes=[
            pltpu.VMEM((na, na), F32),
            pltpu.VMEM((na + nrhs, PIV), BF16),
            pltpu.VMEM((na + nrhs, PIV), BF16),
            pltpu.VMEM((na + nrhs, PIV), F32),
            pltpu.VMEM((NP, B, B), F32),
            pltpu.VMEM((na + nrhs, B), F32),
            pltpu.VMEM((B, B), F32),
            pltpu.VMEM((B, B), F32),
            pltpu.VMEM((B, B), F32),
        ],
        compiler_params=pltpu.CompilerParams(vmem_limit_bytes=20 * 1024 * 1024),
        cost_estimate=pl.CostEstimate(flops=2 * 10**10, bytes_accessed=2 * 10**7, transcendentals=0),
        name="second",
    )(index, *parts, *state, rhs)


def place_rows(me, near_ref, far_ref, cols, a21, start, sem):
    ypos, zpos = lax.rem(me, 4), jnp.clip(me // 4 - 2, 0, 1)
    dst = pl.ds(start, cols.size)
    copies = []
    for n, (ref, z) in enumerate(((near_ref, zpos), (far_ref, 1 - zpos))):
        for d in range(4):
            rows = pl.ds(pl.multiple_of((4 * z + lax.rem(ypos + 4 - d, 4)) * B, B), B)
            copies.append(pltpu.make_async_copy(
                ref.at[pl.ds(d * B, B), cols], a21.at[rows, dst], sem.at[4 * n + d]))
    for copy in copies:
        copy.start()
    return copies


def pair_inverse(i, lh, ll, t_ref):
    t0h, t0l = split(t_ref[2 * i])
    t1h, t1l = split(t_ref[2 * i + 1])
    r1 = slice((2 * i + 1) * B, (2 * i + 2) * B)
    c0 = slice(2 * i * B, (2 * i + 1) * B)
    zh, zl = split(dot3_n(lh[r1, c0], ll[r1, c0], t0h, t0l))
    zh, zl = split(-dot3_n(t1h, t1l, zh, zl))
    zero = jnp.zeros((B, B), BF16)
    return cat_blocks(t0h, zero, zh, t1h), cat_blocks(t0l, zero, zl, t1l)


def solve_half(half, inverses, a21, known, lh, ll, dinv_ref, xh, xl, x32, wh, wl):
    base = half * HALF
    for i in range(2):
        lc, pc = slice(i * W2, (i + 1) * W2), slice(base + i * W2, base + (i + 1) * W2)
        u = a21[:, lc]
        if known:
            u = u - dot3_t(known[0][...], known[1][...], lh[pc, :HALF], ll[pc, :HALF])
        if i:
            u = u - dot3_t(xh[:, :W2], xl[:, :W2], lh[pc, base : base + W2], ll[pc, base : base + W2])
        uh, ul = split(u)
        v = dot3_t(uh, ul, *inverses[i])
        x32[:, lc] = v
        xh[:, lc], xl[:, lc] = split(v)
        wh[:, lc], wl[:, lc] = split(v * dinv_ref[0:1, pc])


def third_kernel(idx_ref, near_ref, far_ref, lh, ll, t_ref, dinv_ref, xh, xl, wh, wl, own_ref, a21, x32, sem):
    me = idx_ref[0]
    copies = place_rows(me, near_ref, far_ref, pl.ds(0, HALF), a21, 0, sem)
    inverses = [pair_inverse(i, lh, ll, t_ref) for i in range(2)]
    for copy in copies:
        copy.wait()
    solve_half(0, inverses, a21, None, lh, ll, dinv_ref, xh, xl, x32, wh, wl)
    mine = pl.ds(pl.multiple_of(jnp.maximum(me - NP, 0) * B, B), B)
    own_ref[...] = x32[mine, :] * dinv_ref[0:1, :HALF]


def third(index, near, far, state):
    low = 2 * near.shape[0]
    outs = (((low, HALF), BF16),) * 4 + (((B, HALF), F32),)
    return pl.pallas_call(
        third_kernel,
        out_shape=tuple(jax.ShapeDtypeStruct(*o) for o in outs),
        in_specs=[pl.BlockSpec(memory_space=pltpu.SMEM)] + [VMEM_SPEC] * 6,
        out_specs=(VMEM_SPEC,) * len(outs),
        scratch_shapes=[
            pltpu.VMEM((low, HALF), F32),
            pltpu.VMEM((low, HALF), F32),
            pltpu.SemaphoreType.DMA((8,)),
        ],
        compiler_params=pltpu.CompilerParams(vmem_limit_bytes=16 * 1024 * 1024),
        cost_estimate=pl.CostEstimate(flops=5 * 10**9, bytes_accessed=10**7, transcendentals=0),
        name="third",
    )(index, near, far, *state[:4])


def fourth_kernel(idx_ref, near0_ref, far0_ref, near_ref, far_ref, xh0, xl0, wh0, wl0, lown_ref, lh, ll, t_ref, dinv_ref, y_ref, own_ref,
                  tail_ref, b_ref, fac_ref, eli_ref, a21, xh, xl, x32, wh, wl, sem):
    me = idx_ref[0]
    nrhs, order = b_ref.shape
    low = order - PIV
    copies = place_rows(me, near0_ref, far0_ref, pl.ds(HALF, AHEAD - HALF), a21, 0, sem.at[0])
    copies += place_rows(me, near_ref, far_ref, pl.ds(0, PIV - AHEAD), a21, AHEAD - HALF, sem.at[1])
    inverses = [pair_inverse(i, lh, ll, t_ref) for i in range(2, 4)]
    for copy in copies:
        copy.wait()
    solve_half(1, inverses, a21, (xh0, xl0), lh, ll, dinv_ref, xh, xl, x32, wh, wl)
    y = y_ref[...]
    yh, yl = split(y)
    eli_ref[:, :PIV] = y
    mine = pl.ds(pl.multiple_of(jnp.maximum(me - NP, 0) * B, B), B)
    n = B + nrhs
    hi = [jnp.concatenate([x[mine, :], yh[:, c]], 0) for x, c in ((xh0, slice(0, HALF)), (xh, slice(HALF, PIV)))]
    lo = [jnp.concatenate([x[mine, :], yl[:, c]], 0) for x, c in ((xl0, slice(0, HALF)), (xl, slice(HALF, PIV)))]
    both = [jnp.concatenate([h, m], 0) for h, m in zip(hi, lo)]
    for c in range(low // W2):
        rows = slice(c * W2, (c + 1) * W2)
        dst = slice(PIV + c * W2, PIV + (c + 1) * W2)
        prod = dot_t(both[0], wh0[rows, :]) + dot_t(both[1], wh[rows, :])
        prod = prod[:n] + prod[n:] + dot_t(hi[0], wl0[rows, :]) + dot_t(hi[1], wl[rows, :])
        row = me * B + lax.broadcasted_iota(jnp.int32, (B, W2), 0)
        col = PIV + c * W2 + lax.broadcasted_iota(jnp.int32, (B, W2), 1)
        fac_ref[:, dst] = jnp.where(row >= col, tail_ref[:, rows] - prod[:B], 0.0)
        eli_ref[:, dst] = b_ref[:, dst] - prod[B:]
    lower = me >= NP

    @pl.when(lower)
    def _():
        fac_ref[:, :HALF] = lown_ref[...]
        fac_ref[:, HALF:PIV] = x32[mine, :] * dinv_ref[0:1, HALF:]

    @pl.when(jnp.logical_not(lower))
    def _():
        fac_ref[:, :PIV] = own_ref[...]


def fourth(index, sent, solved, state, tail, rhs):
    nrhs, order = rhs.shape
    low = order - PIV
    return pl.pallas_call(
        fourth_kernel,
        out_shape=(
            jax.ShapeDtypeStruct((B, order), F32),
            jax.ShapeDtypeStruct((nrhs, order), F32),
        ),
        in_specs=[pl.BlockSpec(memory_space=pltpu.SMEM)] + [VMEM_SPEC] * (len(sent) + len(solved) + len(state) + 2),
        out_specs=(VMEM_SPEC, VMEM_SPEC),
        scratch_shapes=[
            pltpu.VMEM((low, HALF), F32),
            pltpu.VMEM((low, HALF), BF16),
            pltpu.VMEM((low, HALF), BF16),
            pltpu.VMEM((low, HALF), F32),
            pltpu.VMEM((low, HALF), BF16),
            pltpu.VMEM((low, HALF), BF16),
            pltpu.SemaphoreType.DMA((2, 8)),
        ],
        compiler_params=pltpu.CompilerParams(vmem_limit_bytes=24 * 1024 * 1024),
        name="fourth",
    )(index, *sent, *solved, *state, tail, rhs)


def shift_y(x, d, zs=(0, 1, 2, 3)):
    return lax.ppermute(x, "front", [(4 * z + y, 4 * z + (y + d) % 4) for z in zs for y in range(4)])


def planes(x, pairs):
    return lax.ppermute(x, "front", [(4 * a + y, 4 * b + y) for a, b in pairs for y in range(4)])


def pick(z, *values):
    return jnp.where(z == 0, values[0], jnp.where(z == 1, values[1], jnp.where(z == 2, values[2], values[3])))


def ring_y(x, zs=(0, 1, 2, 3)):
    return [x] + [shift_y(x, d, zs) for d in (1, 2, 3)]


def local(front_matrix, child_blocks, child_target, child_count, shot_rhs):
    leaves, slots = child_blocks.shape[1:3]
    slot_ids = lax.broadcasted_iota(jnp.int32, (leaves, slots), 1)
    live_code = jnp.where(slot_ids < child_count[0][:, None], child_target[0], -1)
    code_rows = jnp.zeros((leaves, 8, B), F32).at[:, 0, :slots].set(live_code.astype(F32))
    payload = jnp.concatenate([child_blocks[0].reshape(leaves, slots * B, B), code_rows], axis=1)
    arrived = lax.all_to_all(payload, "leaf", split_axis=0, concat_axis=0, tiled=True)
    codes = arrived[:, slots * B, :slots].astype(jnp.int32)
    index = lax.axis_index("front").astype(jnp.int32).reshape(1)
    tail, early, late, ahead = assemble(codes, index, arrived, front_matrix[0])
    z = lax.axis_index("front") // 4
    rhs = shot_rhs[0]
    swap = planes(early, ((0, 1), (1, 0)))
    side = planes(early, ((1, 2), (0, 3)))
    cross = planes(early, ((0, 2), (1, 3)))
    near_first = jnp.concatenate(ring_y(ahead, (2, 3)), 0)
    early_parts = ring_y(jnp.concatenate([pick(z, early, swap, cross, side), pick(z, swap, early, side, cross)], 0))
    late_x, _ = lax.optimization_barrier((late, (swap, side, cross)))
    to0, to2, to3 = (planes(late_x, ((1, d),)) for d in (0, 2, 3))
    far_first = planes(near_first, ((2, 3), (3, 2)))
    mixed = jnp.concatenate([pick(z, to0, late_x, to2, to3), late[:, AHEAD - HALF :]], 1)
    late_parts = ring_y(mixed)
    state = first(index, early_parts, rhs)
    near_last = jnp.concatenate([part[:, HALF:] for part in late_parts], 0)
    near_last, _ = lax.optimization_barrier((near_last, state[6]))
    far_last = planes(near_last, ((2, 3), (3, 2)))
    state = second(index, late_parts, state, rhs)
    solved = third(index, near_first, far_first, state)
    factored, eliminated = fourth(index, (near_first, far_first, near_last, far_last), solved, state, tail, rhs)
    tail = eliminated[:, PIV:]
    tail = jnp.where(z < 2, planes(tail, ((2, 1), (3, 0))), tail)
    eliminated = jnp.concatenate([eliminated[:, :PIV], tail], 1)
    return factored[None], eliminated[None]


def solution(mesh):
    return jax.shard_map(
        local,
        mesh=mesh,
        in_specs=(
            P("leaf", "front", None),
            P(("leaf", "front"), None, None, None, None),
            P(("leaf", "front"), None, None),
            P(("leaf", "front"), None),
            P("leaf", None, None),
        ),
        out_specs=(P("leaf", "front", None), P("leaf", None, None)),
        check_vma=False,
    )
```

```python
import jax
import jax.numpy as jnp
from jax import lax
from jax.experimental import pallas as pl
from jax.experimental.pallas import tpu as pltpu
from jax.sharding import PartitionSpec as P

B = 128
PIV = 1024
NP = PIV // B
HALF = PIV // 2
W2 = 2 * B
F32 = jnp.float32
BF16 = jnp.bfloat16


def split(x):
    hi = x.astype(BF16)
    lo = (x - hi.astype(F32)).astype(BF16)
    return hi, lo


def dot_t(a, b):
    return lax.dot_general(a, b, (((1,), (1,)), ((), ())), preferred_element_type=F32)


def dot_n(a, b):
    return lax.dot_general(a, b, (((1,), (0,)), ((), ())), preferred_element_type=F32)


def dot3_t(ah, al, bh, bl):
    return dot_t(ah, bh) + dot_t(al, bh) + dot_t(ah, bl)


def dot3_n(ah, al, bh, bl):
    return dot_n(ah, bh) + dot_n(al, bh) + dot_n(ah, bl)


def assemble_kernel(code_ref, idx_ref, recv_ref, front_ref, tail_ref, early_ref, late_ref, out_ref):
    out_ref[...] = front_ref[...]
    for s in range(recv_ref.shape[0]):
        for j in range(code_ref.shape[1]):
            code = code_ref[s, j]

            @pl.when(code >= 0)
            def _(s=s, j=j, code=code):
                cols = pl.ds(pl.multiple_of(code * B, B), B)
                out_ref[:, cols] += recv_ref[s, j * B : (j + 1) * B, :]

    cols = pl.ds(pl.multiple_of(idx_ref[0] * B, B), B)
    square = out_ref[:, cols]
    row = lax.broadcasted_iota(jnp.int32, (B, B), 0)
    col = lax.broadcasted_iota(jnp.int32, (B, B), 1)
    out_ref[:, cols] = jnp.where(row >= col, square, square.T)
    early_ref[...] = out_ref[:, :HALF]
    late_ref[...] = out_ref[:, HALF:PIV]
    tail_ref[...] = out_ref[:, PIV:]


def assemble(codes, index, recv, front):
    rows, order = front.shape
    vmem = pl.BlockSpec(memory_space=pltpu.VMEM)
    return pl.pallas_call(
        assemble_kernel,
        out_shape=(
            jax.ShapeDtypeStruct((rows, order - PIV), F32),
            jax.ShapeDtypeStruct((rows, HALF), F32),
            jax.ShapeDtypeStruct((rows, HALF), F32),
        ),
        in_specs=[pl.BlockSpec(memory_space=pltpu.SMEM)] * 2 + [vmem, vmem],
        out_specs=(vmem, vmem, vmem),
        scratch_shapes=[pltpu.VMEM((rows, order), F32)],
        compiler_params=pltpu.CompilerParams(vmem_limit_bytes=8 * 1024 * 1024),
        name="assemble",
    )(codes, index, recv, front)


def lane(x, c):
    return jnp.broadcast_to(x[:, c : c + 1], (8, B))


def sublane(x, t):
    return jnp.broadcast_to(x[t : t + 1, :], (8, B))


def chain(a_rows, e_rows, store, side):
    sub = lax.broadcasted_iota(jnp.int32, (8, B), 0)
    ahead = None
    for g in range(16):
        if g < len(side):
            side[g]()
        ra, re = a_rows[g], e_rows[g]
        base = 8 * g
        b = ahead or [lane(ra, base + t) for t in range(8)]
        more, far = g < 15, g < 14
        if more:
            na, ne = a_rows[g + 1], e_rows[g + 1]
            c = [lane(na, base + t) for t in range(8)]
            q = [lane(ra, base + 8 + t) for t in range(8)]
            ahead = [lane(na, base + 8 + t) for t in range(8)]
        ga, ge = ra, re
        fa, fe = ra, re
        rcps = []
        for t in range(8):
            r = 1.0 / sublane(b[t], t)
            rcps.append(r)
            m = b[t] * r
            mg = jnp.where(sub == t, 0.0, m)
            mf = jnp.where(sub > t, m, 0.0)
            pa, pe = sublane(fa, t), sublane(fe, t)
            if more:
                mn = c[t] * r
            for u in range(t + 1, 8):
                w = sublane(b[u], t)
                b[u] = b[u] - mg * w
                if more:
                    c[u] = c[u] - mn * w
            if more:
                for u in range(8):
                    w = sublane(q[u], t)
                    q[u] = q[u] - mf * w
                    ahead[u] = ahead[u] - mn * w
                na = na - mn * pa
                ne = ne - mn * pe
            fa = fa - mf * pa
            fe = fe - mf * pe
            if far:
                ga = ga - mg * pa
                ge = ge - mg * pe
        rc = rcps[0]
        for t in range(1, 8):
            rc = jnp.where(sub == t, rcps[t], rc)
        store(g, fa, fe, rc)
        if more:
            a_rows[g + 1], e_rows[g + 1] = na, ne
        if far:
            ga = ga * rc
            ge = ge * rc
            gab = [sublane(ga, t) for t in range(8)]
            geb = [sublane(ge, t) for t in range(8)]
            for i in range(g + 2, 16):
                acc_a, acc_e = a_rows[i], e_rows[i]
                for t in range(8):
                    cc = lane(a_rows[i], base + t)
                    acc_a = acc_a - cc * gab[t]
                    acc_e = acc_e - cc * geb[t]
                a_rows[i], e_rows[i] = acc_a, acc_e


def cat_blocks(a, b, c, d):
    return jnp.concatenate([jnp.concatenate([a, b], 1), jnp.concatenate([c, d], 1)], 0)


def factor_panels(k0, k1, a_ref, b_ref, vh, vl, v32, lh, ll, t_ref, lt_ref, dinv_ref,
                  rest_ref, u_ref, part_ref, e_ref):
    row0 = k0 * B
    na, nrhs = a_ref.shape[0], b_ref.shape[0]
    ri = lax.broadcasted_iota(jnp.int32, (8, B), 0)
    ci = lax.broadcasted_iota(jnp.int32, (8, B), 1)

    def settle(k):
        cols = pl.ds(pl.multiple_of(k * B, B), B)
        th, tl = split(t_ref[k])
        uh, ul = split(rest_ref[...])
        v = dot3_t(uh, ul, th, tl)
        v32[:, cols] = v
        vh[:, cols], vl[:, cols] = split(v)
        lrows = slice(row0, row0 + na)
        lh[lrows, cols], ll[lrows, cols] = split(v[:na] * dinv_ref[0:1, cols])

    def panel(k, _):
        kcols = pl.ds(pl.multiple_of(k * B, B), B)
        acols = pl.ds(pl.multiple_of((k - k0) * B, B), B)
        prev = jnp.maximum(k - 1, k0)
        after = jnp.minimum(k + 1, k1 - 1)
        nabs = pl.ds(pl.multiple_of(after * B, B), B)
        nloc = pl.ds(pl.multiple_of((after - k0) * B, B), B)
        a_rows = [u_ref[8 * i : 8 * i + 8, :] for i in range(16)]
        e_rows = [jnp.where(ri + 8 * i == ci, 1.0, 0.0) for i in range(16)]
        diag = []

        def store(g, fa, fe, rc):
            own = ri + 8 * g == ci
            diag.append(jnp.where(own, fa, 0.0))
            lt_ref[k, 8 * g : 8 * g + 8, :] = jnp.where(own, fa, jnp.where(ri + 8 * g < ci, fa * rc, 0.0))
            e_ref[8 * g : 8 * g + 8, :] = fe

        def update():
            prod = dot3_t(vh[...], vl[...], lh[kcols, :], ll[kcols, :])
            rest_ref[:na, :] = a_ref[:, acols] - prod[:na]
            rest_ref[na:, :] = b_ref[:, acols] - prod[na:]

        def partial():
            part_ref[...] = a_ref[nloc, nloc] - dot3_t(vh[nloc, :], vl[nloc, :], lh[nabs, :], ll[nabs, :])

        side = [lambda: settle(prev), update, partial]
        chain(a_rows, e_rows, store, side)
        total = diag[0]
        for g in range(1, 16):
            total = total + diag[g]
        dinv = 1.0 / jnp.sum(total, axis=0, keepdims=True)
        dinv_ref[0:1, kcols] = dinv
        t = e_ref[...]
        t_ref[k] = t
        th, tl = split(t)
        uh, ul = split(rest_ref[nloc, :])
        v = dot3_t(uh, ul, th, tl)
        v_h, v_l = split(v)
        l_h, l_l = split(v * dinv)
        u_ref[...] = part_ref[...] - dot3_t(v_h, v_l, l_h, l_l)
        return 0

    lax.fori_loop(k0, k1, panel, 0)
    settle(k1 - 1)


def first_kernel(idx_ref, y0_ref, y1_ref, y2_ref, y3_ref, b_ref,
                 vh, vl, lh, ll, t_ref, dinv_ref, y_ref, own_ref,
                 a_ref, v32, lt_ref, rest_ref, u_ref, part_ref, e_ref):
    me = idx_ref[0]
    ypos = lax.rem(me, 4)
    for d, ref in enumerate((y0_ref, y1_ref, y2_ref, y3_ref)):
        src = lax.rem(ypos + 4 - d, 4)
        for z in range(2):
            rows = pl.ds(pl.multiple_of((4 * z + src) * B, B), B)
            a_ref[rows, :] = ref[z * B : (z + 1) * B, :]
    for ref in (vh, vl, lh, ll, rest_ref, dinv_ref):
        ref[...] = jnp.zeros_like(ref)
    t_ref[0] = jnp.zeros((B, B), F32)
    u_ref[...] = a_ref[0:B, 0:B]
    factor_panels(0, NP // 2, a_ref, b_ref.at[:, pl.ds(0, HALF)], vh, vl, v32, lh, ll, t_ref, lt_ref, dinv_ref,
                  rest_ref, u_ref, part_ref, e_ref)
    nrhs = b_ref.shape[0]
    y_ref[...] = v32[PIV : PIV + nrhs, :]
    near = jnp.minimum(me, NP - 1)
    rows = pl.ds(pl.multiple_of(near * B, B), B)
    col = lax.broadcasted_iota(jnp.int32, (B, HALF), 1)
    own_ref[...] = jnp.where(col < near * B, v32[rows, :] * dinv_ref[0:1, :], 0.0)

    @pl.when(me < NP // 2)
    def _():
        own_ref[:, rows] = lt_ref[me].T


VMEM_SPEC = pl.BlockSpec(memory_space=pltpu.VMEM)


def first(index, parts, rhs):
    nrhs = rhs.shape[0]
    outs = (
        ((PIV + nrhs, HALF), BF16),
        ((PIV + nrhs, HALF), BF16),
        ((PIV, HALF), BF16),
        ((PIV, HALF), BF16),
        ((NP // 2, B, B), F32),
        ((8, HALF), F32),
        ((nrhs, HALF), F32),
        ((B, HALF), F32),
    )
    return pl.pallas_call(
        first_kernel,
        out_shape=tuple(jax.ShapeDtypeStruct(*o) for o in outs),
        in_specs=[pl.BlockSpec(memory_space=pltpu.SMEM)] + [VMEM_SPEC] * 5,
        out_specs=(VMEM_SPEC,) * len(outs),
        scratch_shapes=[
            pltpu.VMEM((PIV, HALF), F32),
            pltpu.VMEM((PIV + nrhs, HALF), F32),
            pltpu.VMEM((NP // 2, B, B), F32),
            pltpu.VMEM((PIV + nrhs, B), F32),
            pltpu.VMEM((B, B), F32),
            pltpu.VMEM((B, B), F32),
            pltpu.VMEM((B, B), F32),
        ],
        compiler_params=pltpu.CompilerParams(vmem_limit_bytes=20 * 1024 * 1024),
        cost_estimate=pl.CostEstimate(flops=2 * 10**10, bytes_accessed=2 * 10**7, transcendentals=0),
        name="first",
    )(index, *parts, rhs)


def second_kernel(idx_ref, p0_ref, p1_ref, p2_ref, p3_ref, vh0, vl0, lh0, ll0, t0, dinv0, y0, own0, b_ref,
                  lh, ll, t_ref, dinv_ref, y_ref, own_ref,
                  a_ref, vh, vl, v32, lt_ref, rest_ref, u_ref, part_ref, e_ref):
    me = idx_ref[0]
    nrhs = b_ref.shape[0]
    ypos = lax.rem(me, 4)
    for d, ref in enumerate((p0_ref, p1_ref, p2_ref, p3_ref)):
        rows = pl.ds(pl.multiple_of(lax.rem(ypos + 4 - d, 4) * B, B), B)
        a_ref[rows, :] = ref[:B, :]
    for ref, src in ((vh, vh0), (vl, vl0)):
        ref[:, :HALF] = src[HALF:, :]
        ref[:, HALF:] = jnp.zeros((ref.shape[0], HALF), BF16)
    for ref, src in ((lh, lh0), (ll, ll0)):
        ref[:, :HALF] = src[...]
        ref[:, HALF:] = jnp.zeros((ref.shape[0], HALF), BF16)
    dinv_ref[:, :HALF] = dinv0[...]
    dinv_ref[:, HALF:] = jnp.zeros((dinv_ref.shape[0], HALF), F32)
    t_ref[: NP // 2] = t0[...]
    t_ref[NP // 2] = jnp.zeros((B, B), F32)
    rest_ref[...] = jnp.zeros_like(rest_ref)
    u_ref[...] = a_ref[0:B, 0:B] - dot3_t(
        vh[0:B, :HALF], vl[0:B, :HALF], lh[HALF : HALF + B, :HALF], ll[HALF : HALF + B, :HALF]
    )
    factor_panels(NP // 2, NP, a_ref, b_ref.at[:, pl.ds(HALF, HALF)], vh, vl, v32, lh, ll, t_ref, lt_ref,
                  dinv_ref, rest_ref, u_ref, part_ref, e_ref)
    y_ref[:, :HALF] = y0[...]
    y_ref[:, HALF:] = v32[HALF : HALF + nrhs, HALF:]
    own_ref[:, :HALF] = own0[...]
    near = jnp.clip(me - NP // 2, 0, NP // 2 - 1)
    rows = pl.ds(pl.multiple_of(near * B, B), B)
    col = HALF + lax.broadcasted_iota(jnp.int32, (B, HALF), 1)
    own_ref[:, HALF:] = jnp.where(col < me * B, v32[rows, HALF:] * dinv_ref[0:1, HALF:], 0.0)

    @pl.when((me >= NP // 2) & (me < NP))
    def _():
        own_ref[:, pl.ds(pl.multiple_of(me * B, B), B)] = lt_ref[me].T


def second(index, parts, state, rhs):
    nrhs = rhs.shape[0]
    na = PIV - HALF
    outs = (
        ((PIV, PIV), BF16),
        ((PIV, PIV), BF16),
        ((NP, B, B), F32),
        ((8, PIV), F32),
        ((nrhs, PIV), F32),
        ((B, PIV), F32),
    )
    return pl.pallas_call(
        second_kernel,
        out_shape=tuple(jax.ShapeDtypeStruct(*o) for o in outs),
        in_specs=[pl.BlockSpec(memory_space=pltpu.SMEM)] + [VMEM_SPEC] * (len(parts) + len(state) + 1),
        out_specs=(VMEM_SPEC,) * len(outs),
        scratch_shapes=[
            pltpu.VMEM((na, na), F32),
            pltpu.VMEM((na + nrhs, PIV), BF16),
            pltpu.VMEM((na + nrhs, PIV), BF16),
            pltpu.VMEM((na + nrhs, PIV), F32),
            pltpu.VMEM((NP, B, B), F32),
            pltpu.VMEM((na + nrhs, B), F32),
            pltpu.VMEM((B, B), F32),
            pltpu.VMEM((B, B), F32),
            pltpu.VMEM((B, B), F32),
        ],
        compiler_params=pltpu.CompilerParams(vmem_limit_bytes=20 * 1024 * 1024),
        cost_estimate=pl.CostEstimate(flops=2 * 10**10, bytes_accessed=2 * 10**7, transcendentals=0),
        name="second",
    )(index, *parts, *state, rhs)


def place_rows(me, near_ref, far_ref, a21, sem):
    ypos, zpos = lax.rem(me, 4), jnp.clip(me // 4 - 2, 0, 1)
    copies = []
    for n, (ref, z) in enumerate(((near_ref, zpos), (far_ref, 1 - zpos))):
        for d in range(4):
            rows = pl.ds(pl.multiple_of((4 * z + lax.rem(ypos + 4 - d, 4)) * B, B), B)
            copies.append(pltpu.make_async_copy(ref.at[pl.ds(d * B, B), :], a21.at[rows, :], sem.at[4 * n + d]))
    for copy in copies:
        copy.start()
    return copies


def pair_inverse(i, lh, ll, t_ref):
    t0h, t0l = split(t_ref[2 * i])
    t1h, t1l = split(t_ref[2 * i + 1])
    r1 = slice((2 * i + 1) * B, (2 * i + 2) * B)
    c0 = slice(2 * i * B, (2 * i + 1) * B)
    zh, zl = split(dot3_n(lh[r1, c0], ll[r1, c0], t0h, t0l))
    zh, zl = split(-dot3_n(t1h, t1l, zh, zl))
    zero = jnp.zeros((B, B), BF16)
    return cat_blocks(t0h, zero, zh, t1h), cat_blocks(t0l, zero, zl, t1l)


def solve_half(half, inverses, a21, known, lh, ll, dinv_ref, xh, xl, x32, wh, wl):
    base = half * HALF
    for i in range(2):
        lc, pc = slice(i * W2, (i + 1) * W2), slice(base + i * W2, base + (i + 1) * W2)
        u = a21[:, lc]
        if known is not None:
            u = u - known[:, lc]
        if i:
            u = u - dot3_t(xh[:, :W2], xl[:, :W2], lh[pc, base : base + W2], ll[pc, base : base + W2])
        uh, ul = split(u)
        v = dot3_t(uh, ul, *inverses[i])
        x32[:, lc] = v
        xh[:, lc], xl[:, lc] = split(v)
        wh[:, lc], wl[:, lc] = split(v * dinv_ref[0:1, pc])


def products(mine, xh, xl, wh, wl, y):
    yh, yl = split(y)
    hi = jnp.concatenate([xh[mine, :], yh], 0)
    both = jnp.concatenate([hi, xl[mine, :], yl], 0)
    n = hi.shape[0]
    for c in range(wh.shape[0] // W2):
        rows = slice(c * W2, (c + 1) * W2)
        prod = dot_t(both, wh[rows, :])
        yield c, prod[:n] + prod[n:] + dot_t(hi, wl[rows, :])


def third_kernel(idx_ref, near_ref, far_ref, lh, ll, t_ref, dinv_ref, y_ref, next_ref, prod_ref, own_ref,
                 a21, xh, xl, x32, wh, wl, sem):
    me = idx_ref[0]
    copies = place_rows(me, near_ref, far_ref, a21, sem)
    inverses = [pair_inverse(i, lh, ll, t_ref) for i in range(2)]
    for copy in copies:
        copy.wait()
    solve_half(0, inverses, a21, None, lh, ll, dinv_ref, xh, xl, x32, wh, wl)
    next_ref[...] = dot3_t(xh[...], xl[...], lh[HALF:, :HALF], ll[HALF:, :HALF])
    mine = pl.ds(pl.multiple_of(jnp.maximum(me - NP, 0) * B, B), B)
    for c, prod in products(mine, xh, xl, wh, wl, y_ref[:, :HALF]):
        prod_ref[:, c * W2 : (c + 1) * W2] = prod
    own_ref[...] = x32[mine, :] * dinv_ref[0:1, :HALF]


def third(index, near, far, state):
    low = 2 * near.shape[0]
    nrhs = state[4].shape[0]
    outs = ((low, HALF), (B + nrhs, low), (B, HALF))
    return pl.pallas_call(
        third_kernel,
        out_shape=tuple(jax.ShapeDtypeStruct(o, F32) for o in outs),
        in_specs=[pl.BlockSpec(memory_space=pltpu.SMEM)] + [VMEM_SPEC] * 7,
        out_specs=(VMEM_SPEC,) * len(outs),
        scratch_shapes=[
            pltpu.VMEM((low, HALF), F32),
            pltpu.VMEM((low, HALF), BF16),
            pltpu.VMEM((low, HALF), BF16),
            pltpu.VMEM((low, HALF), F32),
            pltpu.VMEM((low, HALF), BF16),
            pltpu.VMEM((low, HALF), BF16),
            pltpu.SemaphoreType.DMA((8,)),
        ],
        compiler_params=pltpu.CompilerParams(vmem_limit_bytes=24 * 1024 * 1024),
        cost_estimate=pl.CostEstimate(flops=5 * 10**9, bytes_accessed=10**7, transcendentals=0),
        name="third",
    )(index, near, far, *state[:5])


def fourth_kernel(idx_ref, near_ref, far_ref, next_ref, prod_ref, lown_ref, lh, ll, t_ref, dinv_ref, y_ref, own_ref,
                  tail_ref, b_ref, fac_ref, eli_ref, a21, xh, xl, x32, wh, wl, sem):
    me = idx_ref[0]
    nrhs, order = b_ref.shape
    low = order - PIV
    copies = place_rows(me, near_ref, far_ref, a21, sem)
    inverses = [pair_inverse(i, lh, ll, t_ref) for i in range(2, 4)]
    for copy in copies:
        copy.wait()
    solve_half(1, inverses, a21, next_ref, lh, ll, dinv_ref, xh, xl, x32, wh, wl)
    eli_ref[:, :PIV] = y_ref[...]
    mine = pl.ds(pl.multiple_of(jnp.maximum(me - NP, 0) * B, B), B)
    for c, prod in products(mine, xh, xl, wh, wl, y_ref[:, HALF:]):
        rows = slice(c * W2, (c + 1) * W2)
        dst = slice(PIV + c * W2, PIV + (c + 1) * W2)
        prod = prod + prod_ref[:, rows]
        row = me * B + lax.broadcasted_iota(jnp.int32, (B, W2), 0)
        col = PIV + c * W2 + lax.broadcasted_iota(jnp.int32, (B, W2), 1)
        fac_ref[:, dst] = jnp.where(row >= col, tail_ref[:, rows] - prod[:B], 0.0)
        eli_ref[:, dst] = b_ref[:, dst] - prod[B:]
    lower = me >= NP

    @pl.when(lower)
    def _():
        fac_ref[:, :HALF] = lown_ref[...]
        fac_ref[:, HALF:PIV] = x32[mine, :] * dinv_ref[0:1, HALF:]

    @pl.when(jnp.logical_not(lower))
    def _():
        fac_ref[:, :PIV] = own_ref[...]


def fourth(index, near, far, solved, state, tail, rhs):
    nrhs, order = rhs.shape
    low = order - PIV
    return pl.pallas_call(
        fourth_kernel,
        out_shape=(
            jax.ShapeDtypeStruct((B, order), F32),
            jax.ShapeDtypeStruct((nrhs, order), F32),
        ),
        in_specs=[pl.BlockSpec(memory_space=pltpu.SMEM)] + [VMEM_SPEC] * (len(solved) + len(state) + 4),
        out_specs=(VMEM_SPEC, VMEM_SPEC),
        scratch_shapes=[
            pltpu.VMEM((low, HALF), F32),
            pltpu.VMEM((low, HALF), BF16),
            pltpu.VMEM((low, HALF), BF16),
            pltpu.VMEM((low, HALF), F32),
            pltpu.VMEM((low, HALF), BF16),
            pltpu.VMEM((low, HALF), BF16),
            pltpu.SemaphoreType.DMA((8,)),
        ],
        compiler_params=pltpu.CompilerParams(vmem_limit_bytes=24 * 1024 * 1024),
        name="fourth",
    )(index, near, far, *solved, *state, tail, rhs)


def shift_y(x, d, zs=(0, 1, 2, 3)):
    return lax.ppermute(x, "front", [(4 * z + y, 4 * z + (y + d) % 4) for z in zs for y in range(4)])


def planes(x, pairs):
    return lax.ppermute(x, "front", [(4 * a + y, 4 * b + y) for a, b in pairs for y in range(4)])


def pick(z, *values):
    return jnp.where(z == 0, values[0], jnp.where(z == 1, values[1], jnp.where(z == 2, values[2], values[3])))


def ring_y(x, zs=(0, 1, 2, 3)):
    return [x] + [shift_y(x, d, zs) for d in (1, 2, 3)]


def local(front_matrix, child_blocks, child_target, child_count, shot_rhs):
    leaves, slots = child_blocks.shape[1:3]
    slot_ids = lax.broadcasted_iota(jnp.int32, (leaves, slots), 1)
    live_code = jnp.where(slot_ids < child_count[0][:, None], child_target[0], -1)
    code_rows = jnp.zeros((leaves, 8, B), F32).at[:, 0, :slots].set(live_code.astype(F32))
    payload = jnp.concatenate([child_blocks[0].reshape(leaves, slots * B, B), code_rows], axis=1)
    arrived = lax.all_to_all(payload, "leaf", split_axis=0, concat_axis=0, tiled=True)
    codes = arrived[:, slots * B, :slots].astype(jnp.int32)
    index = lax.axis_index("front").astype(jnp.int32).reshape(1)
    tail, early, late = assemble(codes, index, arrived, front_matrix[0])
    z = lax.axis_index("front") // 4
    rhs = shot_rhs[0]
    swap = planes(early, ((0, 1), (1, 0)))
    side = planes(early, ((1, 2), (0, 3)))
    cross = planes(early, ((0, 2), (1, 3)))
    near_first = jnp.concatenate(ring_y(early, (2, 3)), 0)
    early_parts = ring_y(jnp.concatenate([pick(z, early, swap, cross, side), pick(z, swap, early, side, cross)], 0))
    late_x, _ = lax.optimization_barrier((late, (swap, side, cross)))
    to0, to2, to3 = (planes(late_x, ((1, d),)) for d in (0, 2, 3))
    far_first = planes(near_first, ((2, 3), (3, 2)))
    mixed = jnp.concatenate([pick(z, to0, late_x, to2, to3), late], 0)
    late_parts = ring_y(mixed)
    state = first(index, early_parts, rhs)
    near_last = jnp.concatenate([part[B:] for part in late_parts], 0)
    near_last, _ = lax.optimization_barrier((near_last, state[6]))
    far_last = planes(near_last, ((2, 3), (3, 2)))
    state = second(index, late_parts, state, rhs)
    solved = third(index, near_first, far_first, state)
    factored, eliminated = fourth(index, near_last, far_last, solved, state, tail, rhs)
    tail = eliminated[:, PIV:]
    tail = jnp.where(z < 2, planes(tail, ((2, 1), (3, 0))), tail)
    eliminated = jnp.concatenate([eliminated[:, :PIV], tail], 1)
    return factored[None], eliminated[None]


def solution(mesh):
    return jax.shard_map(
        local,
        mesh=mesh,
        in_specs=(
            P("leaf", "front", None),
            P(("leaf", "front"), None, None, None, None),
            P(("leaf", "front"), None, None),
            P(("leaf", "front"), None),
            P("leaf", None, None),
        ),
        out_specs=(P("leaf", "front", None), P("leaf", None, None)),
        check_vma=False,
    )
```

```python
import jax
import jax.numpy as jnp
from jax import lax
from jax.experimental import pallas as pl
from jax.experimental.pallas import tpu as pltpu
from jax.sharding import PartitionSpec as P

B = 128
PIV = 1024
NP = PIV // B
HALF = PIV // 2
W2 = 2 * B
F32 = jnp.float32
BF16 = jnp.bfloat16


def split(x):
    hi = x.astype(BF16)
    lo = (x - hi.astype(F32)).astype(BF16)
    return hi, lo


def dot_t(a, b):
    return lax.dot_general(a, b, (((1,), (1,)), ((), ())), preferred_element_type=F32)


def dot_n(a, b):
    return lax.dot_general(a, b, (((1,), (0,)), ((), ())), preferred_element_type=F32)


def dot3_t(ah, al, bh, bl):
    if ah.shape[1] == B:
        return dot_t(jnp.concatenate([ah, al, ah], 1), jnp.concatenate([bh, bh, bl], 1))
    return dot_t(ah, bh) + dot_t(al, bh) + dot_t(ah, bl)


def dot3_n(ah, al, bh, bl):
    return dot_n(ah, bh) + dot_n(al, bh) + dot_n(ah, bl)


def assemble_kernel(code_ref, idx_ref, recv_ref, front_ref, tail_ref, early_ref, late_ref, out_ref):
    out_ref[...] = front_ref[...]
    for s in range(recv_ref.shape[0]):
        for j in range(code_ref.shape[1]):
            code = code_ref[s, j]

            @pl.when(code >= 0)
            def _(s=s, j=j, code=code):
                cols = pl.ds(pl.multiple_of(code * B, B), B)
                out_ref[:, cols] += recv_ref[s, j * B : (j + 1) * B, :]

    cols = pl.ds(pl.multiple_of(idx_ref[0] * B, B), B)
    square = out_ref[:, cols]
    row = lax.broadcasted_iota(jnp.int32, (B, B), 0)
    col = lax.broadcasted_iota(jnp.int32, (B, B), 1)
    out_ref[:, cols] = jnp.where(row >= col, square, square.T)
    early_ref[...] = out_ref[:, :HALF]
    late_ref[...] = out_ref[:, HALF:PIV]
    tail_ref[...] = out_ref[:, PIV:]


def assemble(codes, index, recv, front):
    rows, order = front.shape
    vmem = pl.BlockSpec(memory_space=pltpu.VMEM)
    return pl.pallas_call(
        assemble_kernel,
        out_shape=(
            jax.ShapeDtypeStruct((rows, order - PIV), F32),
            jax.ShapeDtypeStruct((rows, HALF), F32),
            jax.ShapeDtypeStruct((rows, HALF), F32),
        ),
        in_specs=[pl.BlockSpec(memory_space=pltpu.SMEM)] * 2 + [vmem, vmem],
        out_specs=(vmem, vmem, vmem),
        scratch_shapes=[pltpu.VMEM((rows, order), F32)],
        compiler_params=pltpu.CompilerParams(vmem_limit_bytes=8 * 1024 * 1024),
        name="assemble",
    )(codes, index, recv, front)


def lane(x, c):
    return jnp.broadcast_to(x[:, c : c + 1], (8, B))


def sublane(x, t):
    return jnp.broadcast_to(x[t : t + 1, :], (8, B))


def chain(a_rows, e_rows, store, side):
    sub = lax.broadcasted_iota(jnp.int32, (8, B), 0)
    ahead = None
    for g in range(16):
        if g < len(side):
            side[g]()
        ra, re = a_rows[g], e_rows[g]
        base = 8 * g
        b = ahead or [lane(ra, base + t) for t in range(8)]
        more, far = g < 15, g < 14
        if more:
            na, ne = a_rows[g + 1], e_rows[g + 1]
            c = [lane(na, base + t) for t in range(8)]
            q = [lane(ra, base + 8 + t) for t in range(8)]
            ahead = [lane(na, base + 8 + t) for t in range(8)]
        ga, ge = ra, re
        fa, fe = ra, re
        rcps = []
        for t in range(8):
            r = 1.0 / sublane(b[t], t)
            rcps.append(r)
            m = b[t] * r
            mg = jnp.where(sub == t, 0.0, m)
            mf = jnp.where(sub > t, m, 0.0)
            pa, pe = sublane(fa, t), sublane(fe, t)
            if more:
                mn = c[t] * r
            for u in range(t + 1, 8):
                w = sublane(b[u], t)
                b[u] = b[u] - mg * w
                if more:
                    c[u] = c[u] - mn * w
            if more:
                for u in range(8):
                    w = sublane(q[u], t)
                    q[u] = q[u] - mf * w
                    ahead[u] = ahead[u] - mn * w
                na = na - mn * pa
                ne = ne - mn * pe
            fa = fa - mf * pa
            fe = fe - mf * pe
            if far:
                ga = ga - mg * pa
                ge = ge - mg * pe
        rc = rcps[0]
        for t in range(1, 8):
            rc = jnp.where(sub == t, rcps[t], rc)
        store(g, fa, fe, rc)
        if more:
            a_rows[g + 1], e_rows[g + 1] = na, ne
        if far:
            ga = ga * rc
            ge = ge * rc
            gab = [sublane(ga, t) for t in range(8)]
            geb = [sublane(ge, t) for t in range(8)]
            for i in range(g + 2, 16):
                acc_a, acc_e = a_rows[i], e_rows[i]
                for t in range(8):
                    cc = lane(a_rows[i], base + t)
                    acc_a = acc_a - cc * gab[t]
                    acc_e = acc_e - cc * geb[t]
                a_rows[i], e_rows[i] = acc_a, acc_e


def cat_blocks(a, b, c, d):
    return jnp.concatenate([jnp.concatenate([a, b], 1), jnp.concatenate([c, d], 1)], 0)


def factor_panels(k0, k1, a_ref, b_ref, vh, vl, v32, lh, ll, t_ref, lt_ref, dinv_ref,
                  rest_ref, u_ref, part_ref, e_ref):
    row0 = k0 * B
    na, nrhs = a_ref.shape[0], b_ref.shape[0]
    ri = lax.broadcasted_iota(jnp.int32, (8, B), 0)
    ci = lax.broadcasted_iota(jnp.int32, (8, B), 1)

    def settle(k):
        cols = pl.ds(pl.multiple_of(k * B, B), B)
        th, tl = split(t_ref[k])
        uh, ul = split(rest_ref[...])
        v = dot3_t(uh, ul, th, tl)
        v32[:, cols] = v
        vh[:, cols], vl[:, cols] = split(v)
        lrows = slice(row0, row0 + na)
        lh[lrows, cols], ll[lrows, cols] = split(v[:na] * dinv_ref[0:1, cols])

    def panel(k, _):
        kcols = pl.ds(pl.multiple_of(k * B, B), B)
        acols = pl.ds(pl.multiple_of((k - k0) * B, B), B)
        prev = jnp.maximum(k - 1, k0)
        after = jnp.minimum(k + 1, k1 - 1)
        nabs = pl.ds(pl.multiple_of(after * B, B), B)
        nloc = pl.ds(pl.multiple_of((after - k0) * B, B), B)
        a_rows = [u_ref[8 * i : 8 * i + 8, :] for i in range(16)]
        e_rows = [jnp.where(ri + 8 * i == ci, 1.0, 0.0) for i in range(16)]
        diag = []

        def store(g, fa, fe, rc):
            own = ri + 8 * g == ci
            diag.append(jnp.where(own, fa, 0.0))
            lt_ref[k, 8 * g : 8 * g + 8, :] = jnp.where(own, fa, jnp.where(ri + 8 * g < ci, fa * rc, 0.0))
            e_ref[8 * g : 8 * g + 8, :] = fe

        def update():
            prod = dot3_t(vh[...], vl[...], lh[kcols, :], ll[kcols, :])
            rest_ref[:na, :] = a_ref[:, acols] - prod[:na]
            rest_ref[na:, :] = b_ref[:, acols] - prod[na:]

        def partial():
            part_ref[...] = a_ref[nloc, nloc] - dot3_t(vh[nloc, :], vl[nloc, :], lh[nabs, :], ll[nabs, :])

        side = [lambda: settle(prev), update, partial]
        chain(a_rows, e_rows, store, side)
        total = diag[0]
        for g in range(1, 16):
            total = total + diag[g]
        dinv = 1.0 / jnp.sum(total, axis=0, keepdims=True)
        dinv_ref[0:1, kcols] = dinv
        t = e_ref[...]
        t_ref[k] = t
        th, tl = split(t)
        uh, ul = split(rest_ref[nloc, :])
        v = dot3_t(uh, ul, th, tl)
        v_h, v_l = split(v)
        l_h, l_l = split(v * dinv)
        u_ref[...] = part_ref[...] - dot3_t(v_h, v_l, l_h, l_l)
        return 0

    lax.fori_loop(k0, k1, panel, 0)
    settle(k1 - 1)


def first_kernel(idx_ref, y0_ref, y1_ref, y2_ref, y3_ref, b_ref,
                 vh, vl, lh, ll, t_ref, dinv_ref, y_ref, own_ref,
                 a_ref, v32, lt_ref, rest_ref, u_ref, part_ref, e_ref):
    me = idx_ref[0]
    ypos = lax.rem(me, 4)
    for d, ref in enumerate((y0_ref, y1_ref, y2_ref, y3_ref)):
        src = lax.rem(ypos + 4 - d, 4)
        for z in range(2):
            rows = pl.ds(pl.multiple_of((4 * z + src) * B, B), B)
            a_ref[rows, :] = ref[z * B : (z + 1) * B, :]
    for ref in (vh, vl, lh, ll, rest_ref, dinv_ref):
        ref[...] = jnp.zeros_like(ref)
    t_ref[0] = jnp.zeros((B, B), F32)
    u_ref[...] = a_ref[0:B, 0:B]
    factor_panels(0, NP // 2, a_ref, b_ref.at[:, pl.ds(0, HALF)], vh, vl, v32, lh, ll, t_ref, lt_ref, dinv_ref,
                  rest_ref, u_ref, part_ref, e_ref)
    nrhs = b_ref.shape[0]
    y_ref[...] = v32[PIV : PIV + nrhs, :]
    near = jnp.minimum(me, NP - 1)
    rows = pl.ds(pl.multiple_of(near * B, B), B)
    col = lax.broadcasted_iota(jnp.int32, (B, HALF), 1)
    own_ref[...] = jnp.where(col < near * B, v32[rows, :] * dinv_ref[0:1, :], 0.0)

    @pl.when(me < NP // 2)
    def _():
        own_ref[:, rows] = lt_ref[me].T


VMEM_SPEC = pl.BlockSpec(memory_space=pltpu.VMEM)


def first(index, parts, rhs):
    nrhs = rhs.shape[0]
    outs = (
        ((PIV + nrhs, HALF), BF16),
        ((PIV + nrhs, HALF), BF16),
        ((PIV, HALF), BF16),
        ((PIV, HALF), BF16),
        ((NP // 2, B, B), F32),
        ((8, HALF), F32),
        ((nrhs, HALF), F32),
        ((B, HALF), F32),
    )
    return pl.pallas_call(
        first_kernel,
        out_shape=tuple(jax.ShapeDtypeStruct(*o) for o in outs),
        in_specs=[pl.BlockSpec(memory_space=pltpu.SMEM)] + [VMEM_SPEC] * 5,
        out_specs=(VMEM_SPEC,) * len(outs),
        scratch_shapes=[
            pltpu.VMEM((PIV, HALF), F32),
            pltpu.VMEM((PIV + nrhs, HALF), F32),
            pltpu.VMEM((NP // 2, B, B), F32),
            pltpu.VMEM((PIV + nrhs, B), F32),
            pltpu.VMEM((B, B), F32),
            pltpu.VMEM((B, B), F32),
            pltpu.VMEM((B, B), F32),
        ],
        compiler_params=pltpu.CompilerParams(vmem_limit_bytes=20 * 1024 * 1024),
        cost_estimate=pl.CostEstimate(flops=2 * 10**10, bytes_accessed=2 * 10**7, transcendentals=0),
        name="first",
    )(index, *parts, rhs)


def second_kernel(idx_ref, p0_ref, p1_ref, p2_ref, p3_ref, vh0, vl0, lh0, ll0, t0, dinv0, y0, own0, b_ref,
                  lh, ll, t_ref, dinv_ref, y_ref, own_ref,
                  a_ref, vh, vl, v32, lt_ref, rest_ref, u_ref, part_ref, e_ref):
    me = idx_ref[0]
    nrhs = b_ref.shape[0]
    ypos = lax.rem(me, 4)
    for d, ref in enumerate((p0_ref, p1_ref, p2_ref, p3_ref)):
        rows = pl.ds(pl.multiple_of(lax.rem(ypos + 4 - d, 4) * B, B), B)
        a_ref[rows, :] = ref[:B, :]
    for ref, src in ((vh, vh0), (vl, vl0)):
        ref[:, :HALF] = src[HALF:, :]
        ref[:, HALF:] = jnp.zeros((ref.shape[0], HALF), BF16)
    for ref, src in ((lh, lh0), (ll, ll0)):
        ref[:, :HALF] = src[...]
        ref[:, HALF:] = jnp.zeros((ref.shape[0], HALF), BF16)
    dinv_ref[:, :HALF] = dinv0[...]
    dinv_ref[:, HALF:] = jnp.zeros((dinv_ref.shape[0], HALF), F32)
    t_ref[: NP // 2] = t0[...]
    t_ref[NP // 2] = jnp.zeros((B, B), F32)
    rest_ref[...] = jnp.zeros_like(rest_ref)
    u_ref[...] = a_ref[0:B, 0:B] - dot3_t(
        vh[0:B, :HALF], vl[0:B, :HALF], lh[HALF : HALF + B, :HALF], ll[HALF : HALF + B, :HALF]
    )
    factor_panels(NP // 2, NP, a_ref, b_ref.at[:, pl.ds(HALF, HALF)], vh, vl, v32, lh, ll, t_ref, lt_ref,
                  dinv_ref, rest_ref, u_ref, part_ref, e_ref)
    y_ref[:, :HALF] = y0[...]
    y_ref[:, HALF:] = v32[HALF : HALF + nrhs, HALF:]
    own_ref[:, :HALF] = own0[...]
    near = jnp.clip(me - NP // 2, 0, NP // 2 - 1)
    rows = pl.ds(pl.multiple_of(near * B, B), B)
    col = HALF + lax.broadcasted_iota(jnp.int32, (B, HALF), 1)
    own_ref[:, HALF:] = jnp.where(col < me * B, v32[rows, HALF:] * dinv_ref[0:1, HALF:], 0.0)

    @pl.when((me >= NP // 2) & (me < NP))
    def _():
        own_ref[:, pl.ds(pl.multiple_of(me * B, B), B)] = lt_ref[me].T


def second(index, parts, state, rhs):
    nrhs = rhs.shape[0]
    na = PIV - HALF
    outs = (
        ((PIV, PIV), BF16),
        ((PIV, PIV), BF16),
        ((NP, B, B), F32),
        ((8, PIV), F32),
        ((nrhs, PIV), F32),
        ((B, PIV), F32),
    )
    return pl.pallas_call(
        second_kernel,
        out_shape=tuple(jax.ShapeDtypeStruct(*o) for o in outs),
        in_specs=[pl.BlockSpec(memory_space=pltpu.SMEM)] + [VMEM_SPEC] * (len(parts) + len(state) + 1),
        out_specs=(VMEM_SPEC,) * len(outs),
        scratch_shapes=[
            pltpu.VMEM((na, na), F32),
            pltpu.VMEM((na + nrhs, PIV), BF16),
            pltpu.VMEM((na + nrhs, PIV), BF16),
            pltpu.VMEM((na + nrhs, PIV), F32),
            pltpu.VMEM((NP, B, B), F32),
            pltpu.VMEM((na + nrhs, B), F32),
            pltpu.VMEM((B, B), F32),
            pltpu.VMEM((B, B), F32),
            pltpu.VMEM((B, B), F32),
        ],
        compiler_params=pltpu.CompilerParams(vmem_limit_bytes=20 * 1024 * 1024),
        cost_estimate=pl.CostEstimate(flops=2 * 10**10, bytes_accessed=2 * 10**7, transcendentals=0),
        name="second",
    )(index, *parts, *state, rhs)


def place_rows(me, near_ref, far_ref, a21, sem):
    ypos, zpos = lax.rem(me, 4), jnp.clip(me // 4 - 2, 0, 1)
    copies = []
    for n, (ref, z) in enumerate(((near_ref, zpos), (far_ref, 1 - zpos))):
        for d in range(4):
            rows = pl.ds(pl.multiple_of((4 * z + lax.rem(ypos + 4 - d, 4)) * B, B), B)
            copies.append(pltpu.make_async_copy(ref.at[pl.ds(d * B, B), :], a21.at[rows, :], sem.at[4 * n + d]))
    for copy in copies:
        copy.start()
    return copies


def pair_inverse(i, lh, ll, t_ref):
    t0h, t0l = split(t_ref[2 * i])
    t1h, t1l = split(t_ref[2 * i + 1])
    r1 = slice((2 * i + 1) * B, (2 * i + 2) * B)
    c0 = slice(2 * i * B, (2 * i + 1) * B)
    zh, zl = split(dot3_n(lh[r1, c0], ll[r1, c0], t0h, t0l))
    zh, zl = split(-dot3_n(t1h, t1l, zh, zl))
    zero = jnp.zeros((B, B), BF16)
    return cat_blocks(t0h, zero, zh, t1h), cat_blocks(t0l, zero, zl, t1l)


def solve_half(half, inverses, a21, known, lh, ll, dinv_ref, xh, xl, x32, wh, wl):
    base = half * HALF
    for i in range(2):
        lc, pc = slice(i * W2, (i + 1) * W2), slice(base + i * W2, base + (i + 1) * W2)
        u = a21[:, lc]
        if known is not None:
            u = u - known[:, lc]
        if i:
            u = u - dot3_t(xh[:, :W2], xl[:, :W2], lh[pc, base : base + W2], ll[pc, base : base + W2])
        uh, ul = split(u)
        v = dot3_t(uh, ul, *inverses[i])
        x32[:, lc] = v
        xh[:, lc], xl[:, lc] = split(v)
        wh[:, lc], wl[:, lc] = split(v * dinv_ref[0:1, pc])


def products(mine, xh, xl, wh, wl, y):
    yh, yl = split(y)
    hi = jnp.concatenate([xh[mine, :], yh], 0)
    both = jnp.concatenate([hi, xl[mine, :], yl], 0)
    n = hi.shape[0]
    for c in range(wh.shape[0] // W2):
        rows = slice(c * W2, (c + 1) * W2)
        prod = dot_t(both, wh[rows, :])
        yield c, prod[:n] + prod[n:] + dot_t(hi, wl[rows, :])


def third_kernel(idx_ref, near_ref, far_ref, lh, ll, t_ref, dinv_ref, y_ref, next_ref, prod_ref, own_ref,
                 a21, xh, xl, x32, wh, wl, sem):
    me = idx_ref[0]
    copies = place_rows(me, near_ref, far_ref, a21, sem)
    inverses = [pair_inverse(i, lh, ll, t_ref) for i in range(2)]
    for copy in copies:
        copy.wait()
    solve_half(0, inverses, a21, None, lh, ll, dinv_ref, xh, xl, x32, wh, wl)
    next_ref[...] = dot3_t(xh[...], xl[...], lh[HALF:, :HALF], ll[HALF:, :HALF])
    mine = pl.ds(pl.multiple_of(jnp.maximum(me - NP, 0) * B, B), B)
    for c, prod in products(mine, xh, xl, wh, wl, y_ref[:, :HALF]):
        prod_ref[:, c * W2 : (c + 1) * W2] = prod
    own_ref[...] = x32[mine, :] * dinv_ref[0:1, :HALF]


def third(index, near, far, state):
    low = 2 * near.shape[0]
    nrhs = state[4].shape[0]
    outs = ((low, HALF), (B + nrhs, low), (B, HALF))
    return pl.pallas_call(
        third_kernel,
        out_shape=tuple(jax.ShapeDtypeStruct(o, F32) for o in outs),
        in_specs=[pl.BlockSpec(memory_space=pltpu.SMEM)] + [VMEM_SPEC] * 7,
        out_specs=(VMEM_SPEC,) * len(outs),
        scratch_shapes=[
            pltpu.VMEM((low, HALF), F32),
            pltpu.VMEM((low, HALF), BF16),
            pltpu.VMEM((low, HALF), BF16),
            pltpu.VMEM((low, HALF), F32),
            pltpu.VMEM((low, HALF), BF16),
            pltpu.VMEM((low, HALF), BF16),
            pltpu.SemaphoreType.DMA((8,)),
        ],
        compiler_params=pltpu.CompilerParams(vmem_limit_bytes=24 * 1024 * 1024),
        cost_estimate=pl.CostEstimate(flops=5 * 10**9, bytes_accessed=10**7, transcendentals=0),
        name="third",
    )(index, near, far, *state[:5])


def fourth_kernel(idx_ref, near_ref, far_ref, next_ref, prod_ref, lown_ref, lh, ll, t_ref, dinv_ref, y_ref, own_ref,
                  tail_ref, b_ref, fac_ref, eli_ref, a21, xh, xl, x32, wh, wl, sem):
    me = idx_ref[0]
    nrhs, order = b_ref.shape
    low = order - PIV
    copies = place_rows(me, near_ref, far_ref, a21, sem)
    inverses = [pair_inverse(i, lh, ll, t_ref) for i in range(2, 4)]
    for copy in copies:
        copy.wait()
    solve_half(1, inverses, a21, next_ref, lh, ll, dinv_ref, xh, xl, x32, wh, wl)
    eli_ref[:, :PIV] = y_ref[...]
    mine = pl.ds(pl.multiple_of(jnp.maximum(me - NP, 0) * B, B), B)
    for c, prod in products(mine, xh, xl, wh, wl, y_ref[:, HALF:]):
        rows = slice(c * W2, (c + 1) * W2)
        dst = slice(PIV + c * W2, PIV + (c + 1) * W2)
        prod = prod + prod_ref[:, rows]
        row = me * B + lax.broadcasted_iota(jnp.int32, (B, W2), 0)
        col = PIV + c * W2 + lax.broadcasted_iota(jnp.int32, (B, W2), 1)
        fac_ref[:, dst] = jnp.where(row >= col, tail_ref[:, rows] - prod[:B], 0.0)
        eli_ref[:, dst] = b_ref[:, dst] - prod[B:]
    lower = me >= NP

    @pl.when(lower)
    def _():
        fac_ref[:, :HALF] = lown_ref[...]
        fac_ref[:, HALF:PIV] = x32[mine, :] * dinv_ref[0:1, HALF:]

    @pl.when(jnp.logical_not(lower))
    def _():
        fac_ref[:, :PIV] = own_ref[...]


def fourth(index, near, far, solved, state, tail, rhs):
    nrhs, order = rhs.shape
    low = order - PIV
    return pl.pallas_call(
        fourth_kernel,
        out_shape=(
            jax.ShapeDtypeStruct((B, order), F32),
            jax.ShapeDtypeStruct((nrhs, order), F32),
        ),
        in_specs=[pl.BlockSpec(memory_space=pltpu.SMEM)] + [VMEM_SPEC] * (len(solved) + len(state) + 4),
        out_specs=(VMEM_SPEC, VMEM_SPEC),
        scratch_shapes=[
            pltpu.VMEM((low, HALF), F32),
            pltpu.VMEM((low, HALF), BF16),
            pltpu.VMEM((low, HALF), BF16),
            pltpu.VMEM((low, HALF), F32),
            pltpu.VMEM((low, HALF), BF16),
            pltpu.VMEM((low, HALF), BF16),
            pltpu.SemaphoreType.DMA((8,)),
        ],
        compiler_params=pltpu.CompilerParams(vmem_limit_bytes=24 * 1024 * 1024),
        name="fourth",
    )(index, near, far, *solved, *state, tail, rhs)


def shift_y(x, d, zs=(0, 1, 2, 3)):
    return lax.ppermute(x, "front", [(4 * z + y, 4 * z + (y + d) % 4) for z in zs for y in range(4)])


def planes(x, pairs):
    return lax.ppermute(x, "front", [(4 * a + y, 4 * b + y) for a, b in pairs for y in range(4)])


def pick(z, *values):
    return jnp.where(z == 0, values[0], jnp.where(z == 1, values[1], jnp.where(z == 2, values[2], values[3])))


def ring_y(x, zs=(0, 1, 2, 3)):
    return [x] + [shift_y(x, d, zs) for d in (1, 2, 3)]


def local(front_matrix, child_blocks, child_target, child_count, shot_rhs):
    leaves, slots = child_blocks.shape[1:3]
    slot_ids = lax.broadcasted_iota(jnp.int32, (leaves, slots), 1)
    live_code = jnp.where(slot_ids < child_count[0][:, None], child_target[0], -1)
    code_rows = jnp.zeros((leaves, 8, B), F32).at[:, 0, :slots].set(live_code.astype(F32))
    payload = jnp.concatenate([child_blocks[0].reshape(leaves, slots * B, B), code_rows], axis=1)
    arrived = lax.all_to_all(payload, "leaf", split_axis=0, concat_axis=0, tiled=True)
    codes = arrived[:, slots * B, :slots].astype(jnp.int32)
    index = lax.axis_index("front").astype(jnp.int32).reshape(1)
    tail, early, late = assemble(codes, index, arrived, front_matrix[0])
    z = lax.axis_index("front") // 4
    rhs = shot_rhs[0]
    swap = planes(early, ((0, 1), (1, 0)))
    side = planes(early, ((1, 2), (0, 3)))
    cross = planes(early, ((0, 2), (1, 3)))
    near_first = jnp.concatenate(ring_y(early, (2, 3)), 0)
    early_parts = ring_y(jnp.concatenate([pick(z, early, swap, cross, side), pick(z, swap, early, side, cross)], 0))
    late_x, _ = lax.optimization_barrier((late, (swap, side, cross)))
    to0, to2, to3 = (planes(late_x, ((1, d),)) for d in (0, 2, 3))
    far_first = planes(near_first, ((2, 3), (3, 2)))
    mixed = jnp.concatenate([pick(z, to0, late_x, to2, to3), late], 0)
    late_parts = ring_y(mixed)
    state = first(index, early_parts, rhs)
    near_last = jnp.concatenate([part[B:] for part in late_parts], 0)
    near_last, _ = lax.optimization_barrier((near_last, state[6]))
    far_last = planes(near_last, ((2, 3), (3, 2)))
    state = second(index, late_parts, state, rhs)
    solved = third(index, near_first, far_first, state)
    factored, eliminated = fourth(index, near_last, far_last, solved, state, tail, rhs)
    tail = eliminated[:, PIV:]
    tail = jnp.where(z < 2, planes(tail, ((2, 1), (3, 0))), tail)
    eliminated = jnp.concatenate([eliminated[:, :PIV], tail], 1)
    return factored[None], eliminated[None]


def solution(mesh):
    return jax.shard_map(
        local,
        mesh=mesh,
        in_specs=(
            P("leaf", "front", None),
            P(("leaf", "front"), None, None, None, None),
            P(("leaf", "front"), None, None),
            P(("leaf", "front"), None),
            P("leaf", None, None),
        ),
        out_specs=(P("leaf", "front", None), P("leaf", None, None)),
        check_vma=False,
    )
```
